32 devices in a mesh: seq: 4 (over z), fsdp: 8 (over y, x, core).
Axes of the slice: x: 2, y: 2, z: 4, core: 2. Of those that a mesh axis runs over, the one named last changes fastest.
Arguments:
- layer_input: bfloat16 [8192, 1024], P(('fsdp', 'seq')), may hold values from -6 to 6
- v_first: bfloat16 [8192, 1024], P(('fsdp', 'seq')), may hold values from -6 to 6
- offsets: int32 [8192], P('fsdp'), may hold values from 0 to 4095, as said below
- g_attn: bfloat16 [1024], P(('seq', 'fsdp')), may hold values from 0.099609375 to 1.8984375
- w_query: bfloat16 [1024, 1024], P(('seq', 'fsdp')), may hold values from -0.25 to 0.25
- w_key: bfloat16 [1024, 1024], P(('seq', 'fsdp')), may hold values from -0.25 to 0.25
- w_value: bfloat16 [1024, 1024], P(('seq', 'fsdp')), may hold values from -0.1875 to 0.1875
- w_out: bfloat16 [1024, 1024], P(('seq', 'fsdp')), may hold values from -1.5 to 1.5
- g_ffn: bfloat16 [1024], P(('seq', 'fsdp')), may hold values from 0.099609375 to 1.8984375
- w_gate: bfloat16 [1024, 2816], P(('seq', 'fsdp')), may hold values from -0.1875 to 0.1875
- w_up: bfloat16 [1024, 2816], P(('seq', 'fsdp')), may hold values from -0.1875 to 0.1875
- w_down: bfloat16 [2816, 1024], P(('seq', 'fsdp')), may hold values from -0.109375 to 0.109375
- out_cot: bfloat16 [8192, 1024], P(('fsdp', 'seq')), may hold values from -6 to 6
Outputs:
- layer_output: bfloat16 [8192, 1024], P(('fsdp', 'seq'))
- grad_input: float32 [8192, 1024], P(('fsdp', 'seq'))
- grad_v_first: float32 [8192, 1024], P(('fsdp', 'seq'))
- grad_g_attn: float32 [1024], P(('seq', 'fsdp'))
- grad_w_query: float32 [1024, 1024], P(('seq', 'fsdp'))
- grad_w_key: float32 [1024, 1024], P(('seq', 'fsdp'))
- grad_w_value: float32 [1024, 1024], P(('seq', 'fsdp'))
- grad_w_out: float32 [1024, 1024], P(('seq', 'fsdp'))
- grad_g_ffn: float32 [1024], P(('seq', 'fsdp'))
- grad_w_gate: float32 [1024, 2816], P(('seq', 'fsdp'))
- grad_w_up: float32 [1024, 2816], P(('seq', 'fsdp'))
- grad_w_down: float32 [2816, 1024], P(('seq', 'fsdp'))
The draws below stay inside these ranges and needn't reach their ends.
Inputs may be any that keep to these rules, and one draw needn't show every extreme that they name: offsets[0] = 0, and offsets[i] is either 0 (a document begins at i) or offsets[i-1] + 1; exactly one document has 4096 tokens.
All inputs are finite; a program needn't handle non-finite values.
Results may differ from the reference program's by a relative error of at most 0.015.
Values may be sent and summed in bfloat16 or wider, within the bound.
A program may use at most 192 MiB of HBM per device.

```python
import jax
import jax.numpy as jnp
from jax import lax

D = 1024
FF = 2816
HEADS = 16
HEAD_DIM = 64
TOKENS = 8192
LONGEST = 4096


def draw_offsets(key, part):
    key_start, key_break = jax.random.split(key)
    places = jnp.arange(TOKENS, dtype=jnp.int32)
    long_first = jax.random.randint(key_start, (), 0, TOKENS - LONGEST + 1, dtype=jnp.int32)
    break_rate = max(16, LONGEST // 32)
    break_every = min(4096, LONGEST)
    fresh_start = (jax.random.randint(key_break, (TOKENS,), 0, break_rate, dtype=jnp.int32) == 0) | (places % break_every == 0)
    inside = (places > long_first) & (places < long_first + LONGEST)
    starts = fresh_start & jnp.logical_not(inside) | (places == long_first) | (places == long_first + LONGEST)
    begins = lax.cummax(jnp.where(starts, places, 0), axis=0)
    return places - begins


def raised(values, own_key, source, target, parts, factor):
    owner, partner = [(jnp.arange(values.shape[position]) // (values.shape[position] // parts)).reshape([-1 if axis == position else 1 for axis in range(values.ndim)]) for position in (source, target)]
    chosen = jax.random.permutation(own_key, parts)[partner]
    strong = (owner == chosen) | (owner == (partner + parts // 2) % parts)
    return jnp.where(strong, factor * values, values)


def steps_of(key, dims, shards, smallest, high):
    level = 1.0
    for axis_at, shards_of in shards:
        steps = jax.random.uniform(jax.random.fold_in(jax.random.fold_in(key, 6), axis_at), (shards_of,), jnp.float32, smallest / len(shards), high / len(shards))
        level = level * jnp.repeat(jnp.exp(steps), dims[axis_at] // shards_of).reshape((-1,) + (1,) * (len(dims) - 1 - axis_at))
    return level


def centred(stream_key, dims, scale, most, cuts=(), kind=jnp.bfloat16):
    drawn = scale * jax.random.normal(stream_key, dims, jnp.float32)
    if cuts:
        drawn = drawn * steps_of(stream_key, dims, cuts, -0.22, 0.18)
    return jnp.clip(drawn, -most, most).astype(kind)


def noise_with(rng, shape, scale, reach, shards, heavy, held_as=jnp.bfloat16):
    entries = scale * jax.random.normal(rng, shape, jnp.float32)
    if shards:
        entries = entries * steps_of(rng, shape, shards, -0.22, 0.18)
    return jnp.clip(raised(entries, jax.random.fold_in(rng, 3), *heavy), -reach, reach).astype(held_as)


def setup_inputs(seed: int = 0) -> dict:
    key_list = jax.random.split(jax.random.key(seed), 14)
    return {
        "layer_input": noise_with(key_list[0], (TOKENS, D), 1.0, 6.0, ((0, 32),), (0, 1, 32, 2.75)),
        "v_first": centred(key_list[1], (TOKENS, D), 1.0, 6.0, ((0, 32),)),
        "offsets": draw_offsets(jax.random.fold_in(key_list[13], 71), 0),
        "g_attn": jnp.clip(1.0 + 0.18 * jax.random.normal(key_list[3], (D,), jnp.float32), 0.099609375, 1.8984375).astype(jnp.bfloat16),
        "w_query": centred(key_list[4], (D, D), (D // 2) ** -0.5, 0.25, ((0, 32),)),
        "w_key": centred(key_list[5], (D, D), (D // 2) ** -0.5, 0.25, ((0, 32),)),
        "w_value": centred(key_list[6], (D, D), D ** -0.5, 0.1875, ((0, 32),)),
        "w_out": centred(key_list[7], (D, D), (D // 64) ** -0.5, 1.5, ((0, 32),)),
        "g_ffn": jnp.clip(1.0 + 0.18 * jax.random.normal(key_list[8], (D,), jnp.float32), 0.099609375, 1.8984375).astype(jnp.bfloat16),
        "w_gate": centred(key_list[9], (D, FF), D ** -0.5, 0.1875, ((0, 32),)),
        "w_up": centred(key_list[10], (D, FF), D ** -0.5, 0.1875, ((0, 32),)),
        "w_down": centred(key_list[11], (FF, D), FF ** -0.5, 0.109375, ((0, 32),)),
        "out_cot": centred(key_list[12], (TOKENS, D), 1.0, 6.0, ((0, 32),)),
    }


@jax.custom_vjp
def low(v):
    return lax.optimization_barrier(v.astype(jnp.bfloat16)).astype(jnp.float32)

@jax.custom_vjp
def low_back(v):
    return v

def low_keep(v):
    return (low(v), None)

def low_pass(kept, grad):
    return (grad,)

def back_keep(v):
    return (v, None)

def back_low(kept, grad):
    return (low(grad),)
low.defvjp(low_keep, low_pass)
low_back.defvjp(back_keep, back_low)
EPSILON = 1e-06
NEGATIVE = -1e+30
PRECISE = lax.Precision.HIGHEST

def matmul(left, right):
    return jnp.dot(left, right, precision=PRECISE, preferred_element_type=jnp.float32)

def rms_scale(tensor):
    return lax.rsqrt(lax.optimization_barrier(jnp.mean(tensor * tensor, axis=-1, keepdims=True)) + EPSILON)

def angle_tables(offsets):
    half_dim = HEAD_DIM // 2
    frequency = jnp.power(10000.0, -jnp.arange(half_dim, dtype=jnp.float32) / half_dim)
    angles = offsets.astype(jnp.float32)[:, None] * frequency[None, :]
    return (jnp.cos(angles)[:, None, :], jnp.sin(angles)[:, None, :])

def rotate(tensor, cosine, sine_tab):
    half_dim = HEAD_DIM // 2
    front_half = tensor[..., :half_dim]
    back_half = tensor[..., half_dim:]
    return jnp.concatenate([front_half * cosine - back_half * sine_tab, back_half * cosine + front_half * sine_tab], axis=-1)

def attend(queries, key_rows, value_rows, offsets):
    block_rows = min(512, TOKENS)
    window = min(TOKENS, LONGEST + block_rows)
    score_scale = HEAD_DIM ** (-0.5)
    starts = jnp.arange(TOKENS // block_rows, dtype=jnp.int32) * block_rows

    def one_block(q_first):
        q_rows = lax.dynamic_slice_in_dim(queries, q_first, block_rows, 0)
        q_pos = q_first + jnp.arange(block_rows, dtype=jnp.int32)
        q_begin = q_pos - lax.dynamic_slice_in_dim(offsets, q_first, block_rows, 0)
        k_first = jnp.clip(q_first + block_rows - window, 0, TOKENS - window).astype(jnp.int32)
        k_rows = lax.dynamic_slice_in_dim(key_rows, k_first, window, 0)
        v_rows = lax.dynamic_slice_in_dim(value_rows, k_first, window, 0)
        k_pos = k_first + jnp.arange(window, dtype=jnp.int32)
        allowed = (k_pos[None, :] <= q_pos[:, None]) & (k_pos[None, :] >= q_begin[:, None])
        scores = low_back(score_scale * jnp.einsum('qhd,khd->hqk', q_rows, k_rows, precision=PRECISE))
        scores = jnp.where(allowed[None], scores, NEGATIVE)
        row_top = lax.optimization_barrier(jnp.max(scores, axis=-1, keepdims=True))
        weights = jnp.exp(scores - row_top)
        low_probs = low(weights / lax.optimization_barrier(jnp.sum(weights, axis=-1, keepdims=True)))
        return jnp.einsum('hqk,khd->qhd', low_probs, v_rows, precision=PRECISE)
    blocks = lax.map(jax.checkpoint(one_block), starts)
    return blocks.reshape(TOKENS, HEADS * HEAD_DIM)

def reference(layer_input, v_first, offsets, g_attn, w_query, w_key, w_value, w_out, g_ffn, w_gate, w_up, w_down, out_cot):
    cosine, sine_tab = angle_tables(offsets)

    def forward(input_f32, first_values, gain_attn, proj_query, proj_key, proj_value, proj_out, gain_ffn, proj_gate, proj_up, proj_down):
        normed_a = low(input_f32 * rms_scale(input_f32) * gain_attn)
        queries = low_back(matmul(normed_a, proj_query))
        key_proj = low_back(matmul(normed_a, proj_key))
        mixed_values = low_back(low(0.5 * matmul(normed_a, proj_value) + 0.5 * first_values))
        queries = low_back(low(rotate(queries.reshape(TOKENS, HEADS, HEAD_DIM), cosine, sine_tab)))
        key_proj = low_back(low(rotate(key_proj.reshape(TOKENS, HEADS, HEAD_DIM), cosine, sine_tab)))
        attended = attend(queries, key_proj, mixed_values.reshape(TOKENS, HEADS, HEAD_DIM), offsets)
        attended = low_back(low(attended))
        after_attn = input_f32 + low_back(matmul(attended, proj_out))
        normed_f = low(after_attn * rms_scale(after_attn) * gain_ffn)
        gate_proj = low_back(matmul(normed_f, proj_gate))
        up_proj = low_back(matmul(normed_f, proj_up))
        hidden = low(gate_proj * jax.nn.sigmoid(gate_proj) * up_proj)
        return after_attn + matmul(hidden, proj_down)
    inputs = (layer_input.astype(jnp.float32), v_first.astype(jnp.float32), g_attn.astype(jnp.float32), w_query.astype(jnp.float32), w_key.astype(jnp.float32), w_value.astype(jnp.float32), w_out.astype(jnp.float32), g_ffn.astype(jnp.float32), w_gate.astype(jnp.float32), w_up.astype(jnp.float32), w_down.astype(jnp.float32))
    result, pullback = jax.vjp(forward, *inputs)
    gradients = pullback(out_cot.astype(jnp.float32))
    return (result.astype(jnp.bfloat16), gradients[0], gradients[1], gradients[2], gradients[3], gradients[4], gradients[5], gradients[6], gradients[7], gradients[8], gradients[9], gradients[10])
```

```python
import functools, math
import jax
import jax.numpy as jnp
from jax import lax
from jax.experimental import pallas as pl
from jax.experimental.pallas import tpu as pltpu
from jax.sharding import PartitionSpec as P

HEADS = 16
HEAD_DIM = 64


EPSILON = 1e-06
NEGATIVE = -1e30


def rms_scale(tensor):
    return lax.rsqrt(jnp.mean(tensor * tensor, axis=-1, keepdims=True) + EPSILON)


def angle_tables(offsets):
    half_dim = HEAD_DIM // 2
    frequency = jnp.power(10000.0, -jnp.arange(half_dim, dtype=jnp.float32) / half_dim)
    angles = offsets.astype(jnp.float32)[:, None] * frequency[None, :]
    return (jnp.cos(angles)[:, None, :], jnp.sin(angles)[:, None, :])


def rotate(tensor, cosine, sine_tab):
    half_dim = HEAD_DIM // 2
    front_half = tensor[..., :half_dim]
    back_half = tensor[..., half_dim:]
    return jnp.concatenate(
        [front_half * cosine - back_half * sine_tab, back_half * cosine + front_half * sine_tab],
        axis=-1,
    )


def unrotate(tensor, cosine, sine_tab):
    half_dim = HEAD_DIM // 2
    front_half = tensor[..., :half_dim]
    back_half = tensor[..., half_dim:]
    return jnp.concatenate(
        [front_half * cosine + back_half * sine_tab, back_half * cosine - front_half * sine_tab],
        axis=-1,
    )


def matmul(left, right):
    return jnp.dot(left, right, preferred_element_type=jnp.float32)


def contract_rows(left, right):
    return lax.dot_general(
        left, right, (((0,), (0,)), ((), ())), preferred_element_type=jnp.float32
    )


def contract_cols(left, right):
    return lax.dot_general(
        left, right, (((1,), (1,)), ((), ())), preferred_element_type=jnp.float32
    )


def mask_for(q_pos, q_begin, k_first, count):
    k_pos = k_first + jnp.arange(count, dtype=jnp.int32)
    return (k_pos[None, :] <= q_pos[:, None]) & (k_pos[None, :] >= q_begin[:, None])


def is_live(q_pos, q_begin, k_first, count):
    return (k_first <= q_pos[-1]) & (k_first + count - 1 >= q_begin[0])


def fetch_rows(source, number, piece_rows, heads_here):
    return lax.dynamic_slice_in_dim(source, number * piece_rows, piece_rows, 0).reshape(
        piece_rows, heads_here, HEAD_DIM
    )


def masked_scores(q_rows, k_rows, allowed, score_scale):
    scores = (
        jnp.einsum("qhd,khd->hqk", q_rows, k_rows, preferred_element_type=jnp.float32) * score_scale
    )
    return jnp.where(allowed[None], scores, NEGATIVE)


def forward_block(q_rows, q_pos, q_begin, key_rows, value_rows, piece_rows, score_scale):
    heads_here = q_rows.shape[1]
    height = q_rows.shape[0]
    numbers = jnp.arange(key_rows.shape[0] // piece_rows, dtype=jnp.int32)

    def first_pass(running, number):
        k_first = number * piece_rows

        def first_update(current):
            row_top, row_total = current
            allowed = mask_for(q_pos, q_begin, k_first, piece_rows)
            scores = masked_scores(
                q_rows, fetch_rows(key_rows, number, piece_rows, heads_here), allowed, score_scale
            )
            new_top = jnp.maximum(row_top, jnp.max(scores, axis=-1))
            weights = jnp.where(allowed[None], jnp.exp(scores - new_top[..., None]), 0.0)
            return (new_top, row_total * jnp.exp(row_top - new_top) + jnp.sum(weights, axis=-1))

        live = is_live(q_pos, q_begin, k_first, piece_rows)
        return (lax.cond(live, first_update, lambda current: current, running), None)

    start_state = (
        jnp.full((heads_here, height), NEGATIVE, jnp.float32),
        jnp.zeros((heads_here, height), jnp.float32),
    )
    final_state = lax.scan(first_pass, start_state, numbers)[0]
    log_total = final_state[0] + jnp.log(final_state[1])

    def second_pass(running, number):
        k_first = number * piece_rows

        def second_update(out_sum):
            allowed = mask_for(q_pos, q_begin, k_first, piece_rows)
            scores = masked_scores(
                q_rows, fetch_rows(key_rows, number, piece_rows, heads_here), allowed, score_scale
            )
            low_probs = jnp.where(
                allowed[None], jnp.exp(scores - log_total[..., None]), 0.0
            ).astype(jnp.bfloat16)
            return out_sum + jnp.einsum(
                "hqk,khd->qhd",
                low_probs,
                fetch_rows(value_rows, number, piece_rows, heads_here),
                preferred_element_type=jnp.float32,
            )

        live = is_live(q_pos, q_begin, k_first, piece_rows)
        return (lax.cond(live, second_update, lambda out_sum: out_sum, running), None)

    attended = lax.scan(
        second_pass, jnp.zeros((height, heads_here, HEAD_DIM), jnp.float32), numbers
    )[0]
    return (log_total, attended)


def backward_block(
    q_rows,
    grad_rows,
    log_total,
    spread,
    q_pos,
    q_begin,
    key_rows,
    value_rows,
    piece_rows,
    score_scale,
    key_grads,
    value_grads,
):
    heads_here = q_rows.shape[1]
    numbers = jnp.arange(key_rows.shape[0] // piece_rows, dtype=jnp.int32)

    def step_back(running, number):
        local_first = number * piece_rows

        def step_update(current):
            grad_query, grad_keys, grad_values = current
            k_rows = fetch_rows(key_rows, number, piece_rows, heads_here)
            v_rows = fetch_rows(value_rows, number, piece_rows, heads_here)
            allowed = mask_for(q_pos, q_begin, local_first, piece_rows)
            scores = masked_scores(q_rows, k_rows, allowed, score_scale)
            probs = jnp.where(allowed[None], jnp.exp(scores - log_total[..., None]), 0.0)
            low_probs = probs.astype(jnp.bfloat16)
            value_part = jnp.einsum(
                "hqk,qhd->khd", low_probs, grad_rows, preferred_element_type=jnp.float32
            )
            grad_probs = jnp.einsum(
                "qhd,khd->hqk", grad_rows, v_rows, preferred_element_type=jnp.float32
            )
            grad_scores = (probs * (grad_probs - spread[..., None])).astype(jnp.bfloat16)
            grad_query = grad_query + score_scale * jnp.einsum(
                "hqk,khd->qhd", grad_scores, k_rows, preferred_element_type=jnp.float32
            )
            key_part = score_scale * jnp.einsum(
                "hqk,qhd->khd", grad_scores, q_rows, preferred_element_type=jnp.float32
            )
            old_keys = lax.dynamic_slice_in_dim(grad_keys, local_first, piece_rows, 0)
            grad_keys = lax.dynamic_update_slice_in_dim(
                grad_keys, old_keys + key_part.reshape(piece_rows, -1), local_first, 0
            )
            old_values = lax.dynamic_slice_in_dim(grad_values, local_first, piece_rows, 0)
            grad_values = lax.dynamic_update_slice_in_dim(
                grad_values, old_values + value_part.reshape(piece_rows, -1), local_first, 0
            )
            return (grad_query, grad_keys, grad_values)

        live = is_live(q_pos, q_begin, local_first, piece_rows)
        return (lax.cond(live, step_update, lambda current: current, running), None)

    start_state = (jnp.zeros(q_rows.shape, jnp.float32), key_grads, value_grads)
    return lax.scan(step_back, start_state, numbers)[0]


MESH = pl.DeviceIdType.MESH


class Grid:
    def __init__(self):
        self.seq = lax.axis_size("seq")
        self.fsdp = lax.axis_size("fsdp")
        self.size = {"z": self.seq, "y": 2, "x": self.fsdp // 4}
        self.stride = {"x": 2, "y": 2 * (self.fsdp // 4)}
        self.total = self.seq * self.fsdp
        self.plane = self.total // 2

    def locate(self):
        z, f = lax.axis_index("seq"), lax.axis_index("fsdp")
        nx = self.size["x"]
        self.f, self.zi = f, z
        self.core = lax.rem(f, 2)
        self.me = {"z": z, "y": lax.div(f, 2 * nx), "x": lax.rem(lax.div(f, 2), nx)}

    def step(self, dim, delta):
        if dim == "z":
            return {"seq": self.zi + delta}
        if dim == "core":
            return {"fsdp": self.f + 1 - 2 * self.core}
        return {"fsdp": self.f + delta * self.stride[dim]}

    def partner(self, dim):
        return self.step(dim, 1 - 2 * self.me[dim])

    def dirs(self, dim):
        return (0,) if self.size[dim] == 2 else (1, -1)

    def linear(self, at, core):
        nx = self.size["x"]
        return at["z"] * self.fsdp + (at["y"] * nx + at["x"]) * 2 + core

    def neighbours(self):
        found = [(None, self.step("core", 1))]
        for dim in ("z", "y", "x"):
            n = self.size[dim]
            if n == 1:
                continue
            if n == 2:
                found.append((None, self.partner(dim)))
            else:
                found.append((self.me[dim] < n - 1, self.step(dim, 1)))
                found.append((self.me[dim] > 0, self.step(dim, -1)))
        return found

    def barrier(self):
        sem = pltpu.get_barrier_semaphore()
        count = 0
        for exists, device in self.neighbours():
            if exists is None:
                pl.semaphore_signal(sem, inc=1, device_id=device, device_id_type=MESH)
                count = count + 1
            else:

                @pl.when(exists)
                def _(device=device):
                    pl.semaphore_signal(sem, inc=1, device_id=device, device_id_type=MESH)

                count = count + exists.astype(jnp.int32)
        pl.semaphore_wait(sem, count)

    def digits(self, order, number):
        at, ok = {}, None
        rest = number
        for dim in order:
            n = self.size[dim]
            base = 2 if n == 2 else 2 * n - 1
            digit = lax.rem(rest, base)
            rest = lax.div(rest, base)
            if n == 2:
                at[dim] = lax.rem(self.me[dim] + digit, 2)
            elif n == 1:
                at[dim] = self.me[dim]
            else:
                away = lax.div(digit + 1, 2)
                at[dim] = jnp.where(lax.rem(digit, 2) == 1, self.me[dim] - away, self.me[dim] + away)
                inside = (at[dim] >= 0) & (at[dim] < n)
                ok = inside if ok is None else ok & inside
        return at, ok

    def places(self, order):
        return math.prod(2 if self.size[d] == 2 else 2 * self.size[d] - 1 for d in order)

    def rank(self, order, at, upto):
        value, width = 0, 1
        for dim in order[:upto]:
            value = value + at[dim] * width
            width *= self.size[dim]
        return value

    def slots(self, order):
        first, count, width = [], 0, 1
        for dim in order:
            width *= self.size[dim]
            first.append(count)
            if self.size[dim] > 1:
                count += width * len(self.dirs(dim))
        return first, count

    def branch(self, order, j, way, at):
        dim = order[j]
        n = self.size[dim]
        ok = None
        for later in order[j + 1 :]:
            same = at[later] == self.me[later]
            ok = same if ok is None else ok & same
        if n == 2:
            here = at[dim] == self.me[dim]
        elif way == 1:
            here = (at[dim] <= self.me[dim]) & (self.me[dim] < n - 1)
        else:
            here = (at[dim] >= self.me[dim]) & (self.me[dim] > 0)
        return here if ok is None else ok & here


ORDERS = {"A": ("z", "x", "y"), "B": ("x", "y", "z"), "C": ("y", "z", "x")}


def gather_kernel(pieces, n_arrays, *refs):
    sources, outs = refs[:n_arrays], refs[n_arrays : 2 * n_arrays]
    recv, send, core_send, own_sem = refs[2 * n_arrays :]
    grid = Grid()
    grid.locate()
    mine = grid.linear(grid.me, grid.core)
    own = [
        pltpu.make_async_copy(sources[i], outs[i].at[mine], own_sem.at[i]) for i in range(n_arrays)
    ]
    for copy in own:
        copy.start()
    grid.barrier()

    def view(ref, piece):
        return ref.at[:, pl.ds(piece[1], piece[2])]

    def sends(p, at, source, act):
        array, _, _, scheme = pieces[p]
        order = ORDERS[scheme]
        first, _ = grid.slots(order)
        number = grid.linear(at, grid.core)
        target = view(outs[array].at[number], pieces[p])
        for j, dim in enumerate(order):
            if grid.size[dim] == 1:
                continue
            ways = grid.dirs(dim)
            for w, way in enumerate(ways):
                slot = first[j] + grid.rank(order, at, j + 1) * len(ways) + w
                device = grid.partner(dim) if way == 0 else grid.step(dim, way)

                @pl.when(grid.branch(order, j, way, at))
                def _(device=device, slot=slot):
                    act(
                        pltpu.make_async_remote_copy(
                            src_ref=source,
                            dst_ref=target,
                            send_sem=send.at[p, slot],
                            recv_sem=recv.at[p, number],
                            device_id=device,
                            device_id_type=MESH,
                        )
                    )

        act(
            pltpu.make_async_remote_copy(
                src_ref=source,
                dst_ref=target,
                send_sem=core_send.at[p, grid.rank(order, at, 3)],
                recv_sem=recv.at[p, number],
                device_id=grid.step("core", 1),
                device_id_type=MESH,
            )
        )

    def arrival(p, number):
        array = pieces[p][0]
        there = view(outs[array].at[number], pieces[p])
        return pltpu.make_async_remote_copy(
            src_ref=there,
            dst_ref=there,
            send_sem=core_send.at[p, 0],
            recv_sem=recv.at[p, number],
            device_id=grid.step("core", 1),
            device_id_type=MESH,
        )

    for p in range(len(pieces)):
        sends(p, grid.me, view(sources[pieces[p][0]], pieces[p]), lambda copy: copy.start())

    def forward(number, carry):
        for p in range(len(pieces)):
            at, ok = grid.digits(ORDERS[pieces[p][3]], number)

            def relay(p=p, at=at):
                where = grid.linear(at, grid.core)
                arrival(p, where).wait_recv()
                sends(p, at, view(outs[pieces[p][0]].at[where], pieces[p]), lambda copy: copy.start())

            if ok is None:
                relay()
            else:
                pl.when(ok)(relay)
        return carry

    lax.fori_loop(1, grid.places(ORDERS["A"]), forward, 0)

    def finish(number, carry):
        for p in range(len(pieces)):
            at, ok = grid.digits(ORDERS[pieces[p][3]], number)

            def drain(p=p, at=at):
                arrival(p, grid.linear(at, 1 - grid.core)).wait_recv()
                where = grid.linear(at, grid.core)
                sends(
                    p, at, view(outs[pieces[p][0]].at[where], pieces[p]), lambda copy: copy.wait_send()
                )

            if ok is None:
                drain()
            else:
                pl.when(ok)(drain)
        return carry

    lax.fori_loop(0, grid.places(ORDERS["A"]), finish, 0)
    for copy in own:
        copy.wait()


def gather_all(arrays, pieces, ident):
    grid = Grid()
    n = len(arrays)
    slots = max(grid.slots(order)[1] for order in ORDERS.values())
    moved = sum(a.size * a.dtype.itemsize for a in arrays) * grid.total
    return pl.pallas_call(
        functools.partial(gather_kernel, pieces, n),
        out_shape=[jax.ShapeDtypeStruct((grid.total, *a.shape), a.dtype) for a in arrays],
        in_specs=[pl.BlockSpec(memory_space=pl.ANY)] * n,
        out_specs=[pl.BlockSpec(memory_space=pl.ANY)] * n,
        scratch_shapes=[
            pltpu.SemaphoreType.DMA((len(pieces), grid.total)),
            pltpu.SemaphoreType.DMA((len(pieces), slots)),
            pltpu.SemaphoreType.DMA((len(pieces), grid.plane)),
            pltpu.SemaphoreType.DMA((n,)),
        ],
        compiler_params=pltpu.CompilerParams(collective_id=ident, has_side_effects=True),
        cost_estimate=pl.CostEstimate(flops=0, bytes_accessed=moved, transcendentals=0),
    )(*arrays)


def reduce_kernel(pieces, n_arrays, *refs):
    parts, outs = refs[:n_arrays], refs[n_arrays : 2 * n_arrays]
    rest = list(refs[2 * n_arrays :])
    n = len(pieces)
    pair, slot_of, own, total = rest[:n], rest[n : 2 * n], rest[2 * n : 3 * n], rest[3 * n : 4 * n]
    core_send, core_recv, tree_send, tree_recv, own_sem = rest[4 * n :]
    grid = Grid()
    grid.locate()
    grid.barrier()
    places = grid.places(ORDERS["A"])

    def each(number, act):
        for p in range(n):
            at, ok = grid.digits(ORDERS[pieces[p][3]], number)

            def run(p=p, at=at):
                act(p, at)

            if ok is None:
                run()
            else:
                pl.when(ok)(run)

    def block(p, at, core):
        array, lower, count, _ = pieces[p]
        return parts[array].at[grid.linear(at, core), :, pl.ds(lower, count)]

    def to_sibling(p, at):
        rank = grid.rank(ORDERS[pieces[p][3]], at, 3)
        return pltpu.make_async_remote_copy(
            src_ref=block(p, at, 1 - grid.core),
            dst_ref=pair[p].at[rank],
            send_sem=core_send.at[p, rank],
            recv_sem=core_recv.at[p, rank],
            device_id=grid.step("core", 1),
            device_id_type=MESH,
        )

    def fetch(p, at, number):
        slot = lax.rem(number, 2)
        return pltpu.make_async_copy(
            block(p, at, grid.core), own[p].at[slot], own_sem.at[p, slot]
        )

    def to_parent(p, at, act):
        order = ORDERS[pieces[p][3]]
        first, _ = grid.slots(order)
        rank = grid.rank(order, at, 3)
        for j, dim in enumerate(order):
            if grid.size[dim] == 1:
                continue
            ways = grid.dirs(dim)
            ok = None
            for later in order[j + 1 :]:
                same = at[later] == grid.me[later]
                ok = same if ok is None else ok & same
            for w, way in enumerate(ways):
                slot = first[j] + grid.rank(order, at, j + 1) * len(ways) + w
                if way == 0:
                    here, device = at[dim] != grid.me[dim], grid.partner(dim)
                elif way == 1:
                    here, device = at[dim] < grid.me[dim], grid.step(dim, -1)
                else:
                    here, device = at[dim] > grid.me[dim], grid.step(dim, 1)
                here = here if ok is None else ok & here

                @pl.when(here)
                def _(slot=slot, device=device):
                    act(
                        pltpu.make_async_remote_copy(
                            src_ref=pair[p].at[rank],
                            dst_ref=slot_of[p].at[slot],
                            send_sem=tree_send.at[p, rank],
                            recv_sem=tree_recv.at[p, slot],
                            device_id=device,
                            device_id_type=MESH,
                        )
                    )

    def combine(p, at, number):
        order = ORDERS[pieces[p][3]]
        first, _ = grid.slots(order)
        rank = grid.rank(order, at, 3)
        to_sibling(p, at).wait_recv()
        fetch(p, at, number).wait()
        total[p][...] = own[p][lax.rem(number, 2)].astype(jnp.float32) + pair[p][rank].astype(
            jnp.float32
        )
        for j in reversed(range(3)):
            dim = order[j]
            if grid.size[dim] == 1:
                continue
            ways = grid.dirs(dim)
            for w, way in enumerate(ways):
                slot = first[j] + grid.rank(order, at, j + 1) * len(ways) + w

                @pl.when(grid.branch(order, j, way, at))
                def _(slot=slot):
                    pltpu.make_async_remote_copy(
                        src_ref=slot_of[p].at[slot],
                        dst_ref=slot_of[p].at[slot],
                        send_sem=tree_send.at[p, rank],
                        recv_sem=tree_recv.at[p, slot],
                        device_id=grid.step("core", 1),
                        device_id_type=MESH,
                    ).wait_recv()
                    total[p][...] += slot_of[p][slot].astype(jnp.float32)

    def start_all(step, carry):
        each(places - 1 - step, lambda p, at: to_sibling(p, at).start())
        return carry

    each(places - 1, lambda p, at: fetch(p, at, places - 1).start())
    lax.fori_loop(0, places, start_all, 0)

    def climb(step, carry):
        number = places - 1 - step
        each(number - 1, lambda p, at: fetch(p, at, number - 1).start())

        def work(p, at):
            combine(p, at, number)
            rank = grid.rank(ORDERS[pieces[p][3]], at, 3)
            pair[p][rank] = total[p][...].astype(pair[p].dtype)
            to_parent(p, at, lambda copy: copy.start())

        each(number, work)
        return carry

    lax.fori_loop(0, places - 1, climb, 0)

    def root(p, at):
        combine(p, at, 0)
        array, lower, count, _ = pieces[p]
        outs[array][:, lower : lower + count] = total[p][...]

    each(0, root)

    def finish(step, carry):
        number = places - 1 - step

        def drain(p, at):
            to_sibling(p, at).wait_send()

            @pl.when(number > 0)
            def _():
                to_parent(p, at, lambda copy: copy.wait_send())

        each(number, drain)
        return carry

    lax.fori_loop(0, places, finish, 0)


def reduce_all(arrays, pieces, ident):
    grid = Grid()
    n = len(arrays)
    most = max(grid.slots(order)[1] for order in ORDERS.values())
    moved = sum(a.size * a.dtype.itemsize for a in arrays)
    shape = [(arrays[p[0]].shape[1], p[2]) for p in pieces]
    kind = [arrays[p[0]].dtype for p in pieces]
    count = [grid.slots(ORDERS[p[3]])[1] for p in pieces]
    return pl.pallas_call(
        functools.partial(reduce_kernel, pieces, n),
        out_shape=[jax.ShapeDtypeStruct(a.shape[1:], jnp.float32) for a in arrays],
        in_specs=[pl.BlockSpec(memory_space=pl.ANY)] * n,
        out_specs=[pl.BlockSpec(memory_space=pltpu.VMEM)] * n,
        scratch_shapes=[pltpu.VMEM((grid.plane, *s), k) for s, k in zip(shape, kind)]
        + [pltpu.VMEM((c, *s), k) for c, s, k in zip(count, shape, kind)]
        + [pltpu.VMEM((2, *s), k) for s, k in zip(shape, kind)]
        + [pltpu.VMEM(s, jnp.float32) for s in shape]
        + [
            pltpu.SemaphoreType.DMA((len(pieces), grid.plane)),
            pltpu.SemaphoreType.DMA((len(pieces), grid.plane)),
            pltpu.SemaphoreType.DMA((len(pieces), grid.plane)),
            pltpu.SemaphoreType.DMA((len(pieces), most)),
            pltpu.SemaphoreType.DMA((len(pieces), 2)),
        ],
        compiler_params=pltpu.CompilerParams(
            collective_id=ident, has_side_effects=True, vmem_limit_bytes=60 << 20
        ),
        cost_estimate=pl.CostEstimate(flops=0, bytes_accessed=2 * moved, transcendentals=0),
    )(*arrays)


SCHEMES = ("A", "A", "A", "B", "C", "C", "C", "C")


def per_device(
    layer_input,
    v_first,
    offsets,
    g_attn,
    w_query,
    w_key,
    w_value,
    w_out,
    g_ffn,
    w_gate,
    w_up,
    w_down,
    out_cot,
):
    gains = jnp.zeros((16, 128), jnp.bfloat16)
    gains = lax.dynamic_update_slice(gains, g_attn[None], (0, 0))
    gains = lax.dynamic_update_slice(gains, g_ffn[None], (1, 0))
    shards = (w_gate, w_up, w_query, w_key, w_down, w_value, w_out, gains)
    pieces = [(i, 0, shard.shape[1], scheme) for i, (shard, scheme) in enumerate(zip(shards, SCHEMES))]
    *wholes, whole_gains = gather_all(shards, pieces, 0)
    proj_gate, proj_up, proj_query, proj_key, proj_down, proj_value, proj_out = (
        whole.reshape(-1, whole.shape[2]) for whole in wholes
    )
    gain_attn = whole_gains[:, 0, : g_attn.shape[0]].reshape(-1)
    gain_ffn = whole_gains[:, 1, : g_ffn.shape[0]].reshape(-1)
    tokens = layer_input.shape[0]
    group_size = lax.axis_size("seq")
    group_rows = tokens * group_size
    heads_here = HEADS // group_size
    score_scale = HEAD_DIM ** (-0.5)
    seq_index = lax.axis_index("seq")
    part_index = lax.axis_index("fsdp")
    own_offsets = lax.dynamic_slice_in_dim(offsets, seq_index * tokens, tokens, 0)
    cos_tokens, sin_tokens = angle_tables(own_offsets)
    input_f32 = layer_input.astype(jnp.float32)
    norm_attn = rms_scale(input_f32)
    normed_a = (input_f32 * norm_attn * gain_attn.astype(jnp.float32)).astype(jnp.bfloat16)
    q_tokens = (
        rotate(
            matmul(normed_a, proj_query).reshape(tokens, HEADS, HEAD_DIM), cos_tokens, sin_tokens
        )
        .reshape(tokens, -1)
        .astype(jnp.bfloat16)
    )
    k_tokens = (
        rotate(matmul(normed_a, proj_key).reshape(tokens, HEADS, HEAD_DIM), cos_tokens, sin_tokens)
        .reshape(tokens, -1)
        .astype(jnp.bfloat16)
    )
    mixed_values = (0.5 * matmul(normed_a, proj_value) + 0.5 * v_first.astype(jnp.float32)).astype(
        jnp.bfloat16
    )
    q_heads, k_heads, v_heads = (
        lax.all_to_all(q_tokens, "seq", split_axis=1, concat_axis=0, tiled=True),
        lax.all_to_all(k_tokens, "seq", split_axis=1, concat_axis=0, tiled=True),
        lax.all_to_all(mixed_values, "seq", split_axis=1, concat_axis=0, tiled=True),
    )
    k_whole, v_whole = (
        lax.all_gather(k_heads, "fsdp", axis=0, tiled=True),
        lax.all_gather(v_heads, "fsdp", axis=0, tiled=True),
    )
    positions = part_index * group_rows + jnp.arange(group_rows, dtype=jnp.int32)
    doc_begins = positions - offsets
    block_rows = min(1024, group_rows)
    q_three = q_heads.reshape(group_rows, heads_here, HEAD_DIM)
    lse_parts = []
    out_parts = []
    for number in range(group_rows // block_rows):
        lower = number * block_rows
        upper = lower + block_rows
        log_total, attended = forward_block(
            q_three[lower:upper],
            positions[lower:upper],
            doc_begins[lower:upper],
            k_whole,
            v_whole,
            group_rows,
            score_scale,
        )
        lse_parts.append(log_total)
        out_parts.append(attended)
    attended_all = jnp.concatenate(out_parts, axis=0)
    attended_low = attended_all.reshape(group_rows, -1).astype(jnp.bfloat16)
    attn_tokens = lax.all_to_all(attended_low, "seq", split_axis=0, concat_axis=1, tiled=True)
    after_attn = input_f32 + matmul(attn_tokens, proj_out)
    norm_ffn = rms_scale(after_attn)
    normed_f = (after_attn * norm_ffn * gain_ffn.astype(jnp.float32)).astype(jnp.bfloat16)
    gate_act = matmul(normed_f, proj_gate)
    up_act = matmul(normed_f, proj_up)
    sigmoid_gate = jax.nn.sigmoid(gate_act)
    silu_gate = gate_act * sigmoid_gate
    hidden = (silu_gate * up_act).astype(jnp.bfloat16)
    result = (after_attn + matmul(hidden, proj_down)).astype(jnp.bfloat16)
    grad_down = contract_rows(hidden, out_cot)
    grad_hidden = contract_cols(out_cot, proj_down)
    grad_gate_low = (
        grad_hidden * up_act * sigmoid_gate * (1.0 + gate_act * (1.0 - sigmoid_gate))
    ).astype(jnp.bfloat16)
    grad_up_low = (grad_hidden * silu_gate).astype(jnp.bfloat16)
    grad_gate_w = contract_rows(normed_f, grad_gate_low)
    grad_up_w = contract_rows(normed_f, grad_up_low)
    grad_normed_f = contract_cols(grad_gate_low, proj_gate) + contract_cols(grad_up_low, proj_up)
    grad_gain_ffn = jnp.sum(grad_normed_f * after_attn * norm_ffn, axis=0)
    scaled_ffn = grad_normed_f * gain_ffn.astype(jnp.float32)
    grad_after = (
        out_cot.astype(jnp.float32)
        + norm_ffn * scaled_ffn
        - after_attn * norm_ffn**3 * jnp.mean(scaled_ffn * after_attn, axis=-1, keepdims=True)
    )
    grad_attn_low = grad_after.astype(jnp.bfloat16)
    grad_out_w = contract_rows(attn_tokens, grad_attn_low)
    grad_attended = contract_cols(grad_attn_low, proj_out).astype(jnp.bfloat16)
    grad_heads = lax.all_to_all(grad_attended, "seq", split_axis=1, concat_axis=0, tiled=True)
    grad_three = grad_heads.reshape(group_rows, heads_here, HEAD_DIM)
    spread_all = jnp.einsum("qhd,qhd->hq", grad_three.astype(jnp.float32), attended_all)
    key_grads = jnp.zeros((k_whole.shape[0], k_whole.shape[1]), jnp.float32)
    value_grads = jnp.zeros((v_whole.shape[0], v_whole.shape[1]), jnp.float32)
    query_parts = []
    for number in range(group_rows // block_rows):
        lower = number * block_rows
        upper = lower + block_rows
        grad_query, key_grads, value_grads = backward_block(
            q_three[lower:upper],
            grad_three[lower:upper],
            lse_parts[number],
            spread_all[:, lower:upper],
            positions[lower:upper],
            doc_begins[lower:upper],
            k_whole,
            v_whole,
            group_rows,
            score_scale,
            key_grads,
            value_grads,
        )
        query_parts.append(grad_query)
    own_keys, own_values = (
        lax.psum_scatter(
            key_grads.astype(jnp.bfloat16), "fsdp", scatter_dimension=0, tiled=True
        ).astype(jnp.float32),
        lax.psum_scatter(
            value_grads.astype(jnp.bfloat16), "fsdp", scatter_dimension=0, tiled=True
        ).astype(jnp.float32),
    )
    cos_group, sin_group = angle_tables(offsets)
    grad_q_rot = lax.optimization_barrier(
        jnp.concatenate(query_parts, axis=0).astype(jnp.bfloat16)
    ).astype(jnp.float32)
    grad_k_rot = lax.optimization_barrier(own_keys.astype(jnp.bfloat16)).astype(jnp.float32)
    grad_q_pre = (
        unrotate(grad_q_rot, cos_group, sin_group).reshape(group_rows, -1).astype(jnp.bfloat16)
    )
    grad_k_pre = (
        unrotate(grad_k_rot.reshape(group_rows, heads_here, HEAD_DIM), cos_group, sin_group)
        .reshape(group_rows, -1)
        .astype(jnp.bfloat16)
    )
    grad_mixed = own_values.astype(jnp.bfloat16)
    grad_q_tok, grad_k_tok, grad_mix_tok = (
        lax.all_to_all(grad_q_pre, "seq", split_axis=0, concat_axis=1, tiled=True),
        lax.all_to_all(grad_k_pre, "seq", split_axis=0, concat_axis=1, tiled=True),
        lax.all_to_all(grad_mixed, "seq", split_axis=0, concat_axis=1, tiled=True),
    )
    grad_first = 0.5 * grad_mix_tok.astype(jnp.float32)
    grad_value_low = grad_first.astype(jnp.bfloat16)
    grad_query_w = contract_rows(normed_a, grad_q_tok)
    grad_key_w = contract_rows(normed_a, grad_k_tok)
    grad_value_w = contract_rows(normed_a, grad_value_low)
    grad_normed_a = (
        contract_cols(grad_q_tok, proj_query)
        + contract_cols(grad_k_tok, proj_key)
        + contract_cols(grad_value_low, proj_value)
    )
    grad_gain_attn = jnp.sum(grad_normed_a * input_f32 * norm_attn, axis=0)
    scaled_attn = grad_normed_a * gain_attn.astype(jnp.float32)
    grad_layer = (
        grad_after
        + norm_attn * scaled_attn
        - input_f32 * norm_attn**3 * jnp.mean(scaled_attn * input_f32, axis=-1, keepdims=True)
    )
    devices = lax.axis_size("seq") * lax.axis_size("fsdp")
    terms = [
        grad.astype(jnp.bfloat16).reshape(devices, -1, grad.shape[1])
        for grad in (grad_gate_w, grad_up_w, grad_query_w, grad_key_w, grad_down, grad_value_w, grad_out_w)
    ]
    gain_terms = jnp.zeros((devices, 8, 128), jnp.float32)
    for row, grad in enumerate((grad_gain_attn, grad_gain_ffn)):
        gain_terms = lax.dynamic_update_slice(
            gain_terms, grad.reshape(devices, 1, -1), (0, row, 0)
        )
    sums = reduce_all([*terms, gain_terms], pieces, 1)
    sum_gate, sum_up, sum_query, sum_key, sum_down, sum_value, sum_out, sum_gains = sums
    return (
        result,
        grad_layer,
        grad_first,
        sum_gains[0, : g_attn.shape[0]],
        sum_query,
        sum_key,
        sum_value,
        sum_out,
        sum_gains[1, : g_ffn.shape[0]],
        sum_gate,
        sum_up,
        sum_down,
    )


def solution(mesh):
    return jax.shard_map(
        per_device,
        mesh=mesh,
        in_specs=(
            P(("fsdp", "seq"), None),
            P(("fsdp", "seq"), None),
            P("fsdp"),
            P(("seq", "fsdp")),
            P(("seq", "fsdp"), None),
            P(("seq", "fsdp"), None),
            P(("seq", "fsdp"), None),
            P(("seq", "fsdp"), None),
            P(("seq", "fsdp")),
            P(("seq", "fsdp"), None),
            P(("seq", "fsdp"), None),
            P(("seq", "fsdp"), None),
            P(("fsdp", "seq"), None),
        ),
        out_specs=(
            P(("fsdp", "seq"), None),
            P(("fsdp", "seq"), None),
            P(("fsdp", "seq"), None),
            P(("seq", "fsdp")),
            P(("seq", "fsdp"), None),
            P(("seq", "fsdp"), None),
            P(("seq", "fsdp"), None),
            P(("seq", "fsdp"), None),
            P(("seq", "fsdp")),
            P(("seq", "fsdp"), None),
            P(("seq", "fsdp"), None),
            P(("seq", "fsdp"), None),
        ),
        check_vma=False,
    )
```

```python
import functools, math
import jax
import jax.numpy as jnp
from jax import lax
from jax.experimental import pallas as pl
from jax.experimental.pallas import tpu as pltpu
from jax.sharding import PartitionSpec as P

EPSILON = 1e-06
MESH = pl.DeviceIdType.MESH


class Grid:
    def __init__(self):
        self.seq = lax.axis_size("seq")
        self.fsdp = lax.axis_size("fsdp")
        self.size = {"z": self.seq, "y": 2, "x": self.fsdp // 4}
        self.stride = {"x": 2, "y": 2 * (self.fsdp // 4)}
        self.total = self.seq * self.fsdp
        self.plane = self.total // 2

    def locate(self):
        z, f = lax.axis_index("seq"), lax.axis_index("fsdp")
        nx = self.size["x"]
        self.f, self.zi = f, z
        self.core = lax.rem(f, 2)
        self.me = {"z": z, "y": lax.div(f, 2 * nx), "x": lax.rem(lax.div(f, 2), nx)}

    def step(self, dim, delta):
        if dim == "z":
            return {"seq": self.zi + delta}
        if dim == "core":
            return {"fsdp": self.f + 1 - 2 * self.core}
        return {"fsdp": self.f + delta * self.stride[dim]}

    def partner(self, dim):
        return self.step(dim, 1 - 2 * self.me[dim])

    def dirs(self, dim):
        return (0,) if self.size[dim] == 2 else (1, -1)

    def linear(self, at, core):
        nx = self.size["x"]
        return at["z"] * self.fsdp + (at["y"] * nx + at["x"]) * 2 + core

    def neighbours(self):
        found = [(None, self.step("core", 1))]
        for dim in ("z", "y", "x"):
            n = self.size[dim]
            if n == 1:
                continue
            if n == 2:
                found.append((None, self.partner(dim)))
            else:
                found.append((self.me[dim] < n - 1, self.step(dim, 1)))
                found.append((self.me[dim] > 0, self.step(dim, -1)))
        return found

    def barrier(self):
        sem = pltpu.get_barrier_semaphore()
        count = 0
        for exists, device in self.neighbours():
            if exists is None:
                pl.semaphore_signal(sem, inc=1, device_id=device, device_id_type=MESH)
                count = count + 1
            else:

                @pl.when(exists)
                def _(device=device):
                    pl.semaphore_signal(sem, inc=1, device_id=device, device_id_type=MESH)

                count = count + exists.astype(jnp.int32)
        pl.semaphore_wait(sem, count)

    def digits(self, order, number):
        at, ok = {}, None
        rest = number
        for dim in order:
            n = self.size[dim]
            base = 2 if n == 2 else 2 * n - 1
            digit = lax.rem(rest, base)
            rest = lax.div(rest, base)
            if n == 2:
                at[dim] = lax.rem(self.me[dim] + digit, 2)
            elif n == 1:
                at[dim] = self.me[dim]
            else:
                away = lax.div(digit + 1, 2)
                at[dim] = jnp.where(lax.rem(digit, 2) == 1, self.me[dim] - away, self.me[dim] + away)
                inside = (at[dim] >= 0) & (at[dim] < n)
                ok = inside if ok is None else ok & inside
        return at, ok

    def places(self, order):
        return math.prod(2 if self.size[d] == 2 else 2 * self.size[d] - 1 for d in order)

    def rank(self, order, at, upto):
        value, width = 0, 1
        for dim in order[:upto]:
            value = value + at[dim] * width
            width *= self.size[dim]
        return value

    def slots(self, order):
        first, count, width = [], 0, 1
        for dim in order:
            width *= self.size[dim]
            first.append(count)
            if self.size[dim] > 1:
                count += width * len(self.dirs(dim))
        return first, count

    def branch(self, order, j, way, at):
        dim = order[j]
        n = self.size[dim]
        ok = None
        for later in order[j + 1 :]:
            same = at[later] == self.me[later]
            ok = same if ok is None else ok & same
        if n == 2:
            here = at[dim] == self.me[dim]
        elif way == 1:
            here = (at[dim] <= self.me[dim]) & (self.me[dim] < n - 1)
        else:
            here = (at[dim] >= self.me[dim]) & (self.me[dim] > 0)
        return here if ok is None else ok & here


ORDERS = {"A": ("z", "x", "y"), "B": ("x", "y", "z"), "C": ("y", "z", "x")}


def gather_kernel(pieces, n_arrays, *refs):
    sources, outs = refs[:n_arrays], refs[n_arrays : 2 * n_arrays]
    recv, send, core_send, own_sem = refs[2 * n_arrays :]
    grid = Grid()
    grid.locate()
    mine = grid.linear(grid.me, grid.core)
    own = [
        pltpu.make_async_copy(sources[i], outs[i].at[mine], own_sem.at[i]) for i in range(n_arrays)
    ]
    for copy in own:
        copy.start()
    grid.barrier()

    def view(ref, piece):
        return ref.at[:, pl.ds(piece[1], piece[2])]

    def sends(p, at, source, act):
        array, _, _, scheme = pieces[p]
        order = ORDERS[scheme]
        first, _ = grid.slots(order)
        number = grid.linear(at, grid.core)
        target = view(outs[array].at[number], pieces[p])
        for j, dim in enumerate(order):
            if grid.size[dim] == 1:
                continue
            ways = grid.dirs(dim)
            for w, way in enumerate(ways):
                slot = first[j] + grid.rank(order, at, j + 1) * len(ways) + w
                device = grid.partner(dim) if way == 0 else grid.step(dim, way)

                @pl.when(grid.branch(order, j, way, at))
                def _(device=device, slot=slot):
                    act(
                        pltpu.make_async_remote_copy(
                            src_ref=source,
                            dst_ref=target,
                            send_sem=send.at[p, slot],
                            recv_sem=recv.at[p, number],
                            device_id=device,
                            device_id_type=MESH,
                        )
                    )

        act(
            pltpu.make_async_remote_copy(
                src_ref=source,
                dst_ref=target,
                send_sem=core_send.at[p, grid.rank(order, at, 3)],
                recv_sem=recv.at[p, number],
                device_id=grid.step("core", 1),
                device_id_type=MESH,
            )
        )

    def arrival(p, number):
        array = pieces[p][0]
        there = view(outs[array].at[number], pieces[p])
        return pltpu.make_async_remote_copy(
            src_ref=there,
            dst_ref=there,
            send_sem=core_send.at[p, 0],
            recv_sem=recv.at[p, number],
            device_id=grid.step("core", 1),
            device_id_type=MESH,
        )

    for p in range(len(pieces)):
        sends(p, grid.me, view(sources[pieces[p][0]], pieces[p]), lambda copy: copy.start())

    def forward(number, carry):
        for p in range(len(pieces)):
            at, ok = grid.digits(ORDERS[pieces[p][3]], number)

            def relay(p=p, at=at):
                where = grid.linear(at, grid.core)
                arrival(p, where).wait_recv()
                sends(p, at, view(outs[pieces[p][0]].at[where], pieces[p]), lambda copy: copy.start())

            if ok is None:
                relay()
            else:
                pl.when(ok)(relay)
        return carry

    lax.fori_loop(1, grid.places(ORDERS["A"]), forward, 0)

    def finish(number, carry):
        for p in range(len(pieces)):
            at, ok = grid.digits(ORDERS[pieces[p][3]], number)

            def drain(p=p, at=at):
                arrival(p, grid.linear(at, 1 - grid.core)).wait_recv()
                where = grid.linear(at, grid.core)
                sends(
                    p, at, view(outs[pieces[p][0]].at[where], pieces[p]), lambda copy: copy.wait_send()
                )

            if ok is None:
                drain()
            else:
                pl.when(ok)(drain)
        return carry

    lax.fori_loop(0, grid.places(ORDERS["A"]), finish, 0)
    for copy in own:
        copy.wait()


def gather_all(arrays, pieces, ident):
    grid = Grid()
    n = len(arrays)
    slots = max(grid.slots(order)[1] for order in ORDERS.values())
    moved = sum(a.size * a.dtype.itemsize for a in arrays) * grid.total
    return pl.pallas_call(
        functools.partial(gather_kernel, pieces, n),
        out_shape=[jax.ShapeDtypeStruct((grid.total, *a.shape), a.dtype) for a in arrays],
        in_specs=[pl.BlockSpec(memory_space=pl.ANY)] * n,
        out_specs=[pl.BlockSpec(memory_space=pl.ANY)] * n,
        scratch_shapes=[
            pltpu.SemaphoreType.DMA((len(pieces), grid.total)),
            pltpu.SemaphoreType.DMA((len(pieces), slots)),
            pltpu.SemaphoreType.DMA((len(pieces), grid.plane)),
            pltpu.SemaphoreType.DMA((n,)),
        ],
        compiler_params=pltpu.CompilerParams(collective_id=ident, has_side_effects=True),
        cost_estimate=pl.CostEstimate(flops=0, bytes_accessed=moved, transcendentals=0),
    )(*arrays)


def reduce_kernel(pieces, n_arrays, *refs):
    parts, outs = refs[:n_arrays], refs[n_arrays : 2 * n_arrays]
    rest = list(refs[2 * n_arrays :])
    n = len(pieces)
    pair, slot_of, own, total = rest[:n], rest[n : 2 * n], rest[2 * n : 3 * n], rest[3 * n : 4 * n]
    core_send, core_recv, tree_send, tree_recv, own_sem = rest[4 * n :]
    grid = Grid()
    grid.locate()
    grid.barrier()
    places = grid.places(ORDERS["A"])

    def each(number, act):
        for p in range(n):
            at, ok = grid.digits(ORDERS[pieces[p][3]], number)

            def run(p=p, at=at):
                act(p, at)

            if ok is None:
                run()
            else:
                pl.when(ok)(run)

    def block(p, at, core):
        array, lower, count, _ = pieces[p]
        return parts[array].at[grid.linear(at, core), :, pl.ds(lower, count)]

    def to_sibling(p, at):
        rank = grid.rank(ORDERS[pieces[p][3]], at, 3)
        return pltpu.make_async_remote_copy(
            src_ref=block(p, at, 1 - grid.core),
            dst_ref=pair[p].at[rank],
            send_sem=core_send.at[p, rank],
            recv_sem=core_recv.at[p, rank],
            device_id=grid.step("core", 1),
            device_id_type=MESH,
        )

    def fetch(p, at, number):
        slot = lax.rem(number, 2)
        return pltpu.make_async_copy(
            block(p, at, grid.core), own[p].at[slot], own_sem.at[p, slot]
        )

    def to_parent(p, at, act):
        order = ORDERS[pieces[p][3]]
        first, _ = grid.slots(order)
        rank = grid.rank(order, at, 3)
        for j, dim in enumerate(order):
            if grid.size[dim] == 1:
                continue
            ways = grid.dirs(dim)
            ok = None
            for later in order[j + 1 :]:
                same = at[later] == grid.me[later]
                ok = same if ok is None else ok & same
            for w, way in enumerate(ways):
                slot = first[j] + grid.rank(order, at, j + 1) * len(ways) + w
                if way == 0:
                    here, device = at[dim] != grid.me[dim], grid.partner(dim)
                elif way == 1:
                    here, device = at[dim] < grid.me[dim], grid.step(dim, -1)
                else:
                    here, device = at[dim] > grid.me[dim], grid.step(dim, 1)
                here = here if ok is None else ok & here

                @pl.when(here)
                def _(slot=slot, device=device):
                    act(
                        pltpu.make_async_remote_copy(
                            src_ref=pair[p].at[rank],
                            dst_ref=slot_of[p].at[slot],
                            send_sem=tree_send.at[p, rank],
                            recv_sem=tree_recv.at[p, slot],
                            device_id=device,
                            device_id_type=MESH,
                        )
                    )

    def combine(p, at, number):
        order = ORDERS[pieces[p][3]]
        first, _ = grid.slots(order)
        rank = grid.rank(order, at, 3)
        to_sibling(p, at).wait_recv()
        fetch(p, at, number).wait()
        total[p][...] = own[p][lax.rem(number, 2)].astype(jnp.float32) + pair[p][rank].astype(
            jnp.float32
        )
        for j in reversed(range(3)):
            dim = order[j]
            if grid.size[dim] == 1:
                continue
            ways = grid.dirs(dim)
            for w, way in enumerate(ways):
                slot = first[j] + grid.rank(order, at, j + 1) * len(ways) + w

                @pl.when(grid.branch(order, j, way, at))
                def _(slot=slot):
                    pltpu.make_async_remote_copy(
                        src_ref=slot_of[p].at[slot],
                        dst_ref=slot_of[p].at[slot],
                        send_sem=tree_send.at[p, rank],
                        recv_sem=tree_recv.at[p, slot],
                        device_id=grid.step("core", 1),
                        device_id_type=MESH,
                    ).wait_recv()
                    total[p][...] += slot_of[p][slot].astype(jnp.float32)

    def start_all(step, carry):
        each(places - 1 - step, lambda p, at: to_sibling(p, at).start())
        return carry

    each(places - 1, lambda p, at: fetch(p, at, places - 1).start())
    lax.fori_loop(0, places, start_all, 0)

    def climb(step, carry):
        number = places - 1 - step
        each(number - 1, lambda p, at: fetch(p, at, number - 1).start())

        def work(p, at):
            combine(p, at, number)
            rank = grid.rank(ORDERS[pieces[p][3]], at, 3)
            pair[p][rank] = total[p][...].astype(pair[p].dtype)
            to_parent(p, at, lambda copy: copy.start())

        each(number, work)
        return carry

    lax.fori_loop(0, places - 1, climb, 0)

    def root(p, at):
        combine(p, at, 0)
        array, lower, count, _ = pieces[p]
        outs[array][:, lower : lower + count] = total[p][...]

    each(0, root)

    def finish(step, carry):
        number = places - 1 - step

        def drain(p, at):
            to_sibling(p, at).wait_send()

            @pl.when(number > 0)
            def _():
                to_parent(p, at, lambda copy: copy.wait_send())

        each(number, drain)
        return carry

    lax.fori_loop(0, places, finish, 0)


def reduce_all(arrays, pieces, ident):
    grid = Grid()
    n = len(arrays)
    most = max(grid.slots(order)[1] for order in ORDERS.values())
    moved = sum(a.size * a.dtype.itemsize for a in arrays)
    shape = [(arrays[p[0]].shape[1], p[2]) for p in pieces]
    kind = [arrays[p[0]].dtype for p in pieces]
    count = [grid.slots(ORDERS[p[3]])[1] for p in pieces]
    return pl.pallas_call(
        functools.partial(reduce_kernel, pieces, n),
        out_shape=[jax.ShapeDtypeStruct(a.shape[1:], jnp.float32) for a in arrays],
        in_specs=[pl.BlockSpec(memory_space=pl.ANY)] * n,
        out_specs=[pl.BlockSpec(memory_space=pltpu.VMEM)] * n,
        scratch_shapes=[pltpu.VMEM((grid.plane, *s), k) for s, k in zip(shape, kind)]
        + [pltpu.VMEM((c, *s), k) for c, s, k in zip(count, shape, kind)]
        + [pltpu.VMEM((2, *s), k) for s, k in zip(shape, kind)]
        + [pltpu.VMEM(s, jnp.float32) for s in shape]
        + [
            pltpu.SemaphoreType.DMA((len(pieces), grid.plane)),
            pltpu.SemaphoreType.DMA((len(pieces), grid.plane)),
            pltpu.SemaphoreType.DMA((len(pieces), grid.plane)),
            pltpu.SemaphoreType.DMA((len(pieces), most)),
            pltpu.SemaphoreType.DMA((len(pieces), 2)),
        ],
        compiler_params=pltpu.CompilerParams(
            collective_id=ident, has_side_effects=True, vmem_limit_bytes=60 << 20
        ),
        cost_estimate=pl.CostEstimate(flops=0, bytes_accessed=2 * moved, transcendentals=0),
    )(*arrays)


HEADS = 16
HEAD_DIM = 64
UNIT = 128
NEGATIVE = -1e30


class Owners:
    def __init__(self, tokens):
        self.seq, self.fsdp = lax.axis_size("seq"), lax.axis_size("fsdp")
        self.total = self.seq * self.fsdp
        self.members = self.total // HEADS
        self.heads_here = HEADS // self.seq
        self.tokens = tokens
        self.halves = tokens // UNIT
        self.units = self.halves * self.total // self.members

    def locate(self):
        s, f = lax.axis_index("seq"), lax.axis_index("fsdp")
        self.s, self.f = s, f
        self.linear = s * self.fsdp + f
        self.block = f * self.seq + s
        self.head = s * self.heads_here + lax.div(f, self.members)
        self.member = lax.rem(f, self.members)

    def of_head(self, head, member):
        return {
            "seq": lax.div(head, self.heads_here),
            "fsdp": lax.rem(head, self.heads_here) * self.members + member,
        }

    def of_block(self, block):
        return {"seq": lax.rem(block, self.seq), "fsdp": lax.div(block, self.seq)}

    def barrier(self):
        sem = pltpu.get_barrier_semaphore()

        def greet(delta, carry):
            other = lax.rem(self.linear + delta, self.total)
            device = {"seq": lax.div(other, self.fsdp), "fsdp": lax.rem(other, self.fsdp)}
            pl.semaphore_signal(sem, inc=1, device_id=device, device_id_type=MESH)
            return carry

        lax.fori_loop(1, self.total, greet, 0)
        pl.semaphore_wait(sem, self.total - 1)


def remote(source, target, send_sem, recv_sem, device):
    return pltpu.make_async_remote_copy(
        src_ref=source,
        dst_ref=target,
        send_sem=send_sem,
        recv_sem=recv_sem,
        device_id=device,
        device_id_type=MESH,
    )


def head_rows(head):
    return pl.ds(pl.multiple_of(head * HEAD_DIM, HEAD_DIM), HEAD_DIM)


def lanes(number, width):
    return pl.ds(pl.multiple_of(number * width, width), width)


def spread_units(own, source, target, send, recv, local, act):
    def to_head(delta, carry):
        head = lax.rem(own.head + delta, HEADS)
        for half in range(own.halves):
            unit = own.halves * own.block + half
            member = lax.rem(unit, own.members)
            place = lax.div(unit, own.members)
            piece = source.at[head_rows(head), pl.ds(half * UNIT, UNIT)]
            there = target.at[:, lanes(place, UNIT)]
            here = (head == own.head) & (member == own.member)

            @pl.when(here)
            def _(piece=piece, there=there, half=half):
                copy = pltpu.make_async_copy(piece, there, local.at[half])
                copy.start() if act == "start" else copy.wait()

            @pl.when(jnp.logical_not(here))
            def _(piece=piece, there=there, half=half, member=member, place=place, head=head):
                copy = remote(
                    piece, there, send.at[head, half], recv.at[place], own.of_head(head, member)
                )
                copy.start() if act == "start" else copy.wait_send()

        return carry

    lax.fori_loop(0, HEADS, to_head, 0)


def await_units(own, target, send, recv):
    def one(place, carry):
        unit = place * own.members + own.member
        there = target.at[:, lanes(place, UNIT)]

        @pl.when(lax.div(unit, own.halves) != own.block)
        def _():
            remote(
                there, there, send.at[0, 0], recv.at[place], own.of_block(0)
            ).wait_recv()

        return carry

    lax.fori_loop(0, own.units, one, 0)


def collect_units(own, source, target, send, recv, local, act):
    def one(step, carry):
        place = lax.rem(step + lax.div(own.block * own.halves, own.members), own.units)
        unit = place * own.members + own.member
        block, half = lax.div(unit, own.halves), lax.rem(unit, own.halves)
        piece = source.at[:, lanes(place, UNIT)]
        there = target.at[head_rows(own.head), lanes(half, UNIT)]

        @pl.when(block == own.block)
        def _():
            copy = pltpu.make_async_copy(piece, there, local.at[half])
            copy.start() if act == "start" else copy.wait()

        @pl.when(block != own.block)
        def _():
            copy = remote(
                piece, there, send.at[place], recv.at[own.head, half], own.of_block(block)
            )
            copy.start() if act == "start" else copy.wait_send()

        return carry

    lax.fori_loop(0, own.units, one, 0)


def await_heads(own, target, send, recv):
    def one(head, carry):
        for half in range(own.halves):
            unit = own.halves * own.block + half
            there = target.at[head_rows(head), pl.ds(half * UNIT, UNIT)]

            @pl.when((head != own.head) | (lax.rem(unit, own.members) != own.member))
            def _(there=there, half=half):
                remote(
                    there, there, send.at[0], recv.at[head, half], own.of_block(0)
                ).wait_recv()

        return carry

    lax.fori_loop(0, HEADS, one, 0)


def to_heads_kernel(tokens, q_ref, k_ref, v_ref, q_out, k_out, v_out, *sems):
    q_send, q_recv, q_local, kv_send, kv_recv, kv_local, hand_send = sems
    own = Owners(tokens)
    own.locate()
    own.barrier()
    pairs = ((k_ref, k_out), (v_ref, v_out))

    def keys(act):
        def to_head(delta, carry):
            head = lax.rem(own.head + delta, HEADS)
            for i, (source, target) in enumerate(pairs):
                piece = source.at[head_rows(head), :]
                there = target.at[:, lanes(own.block, tokens)]

                @pl.when(head == own.head)
                def _(piece=piece, there=there, i=i):
                    copy = pltpu.make_async_copy(piece, there, kv_local.at[i])
                    copy.start() if act == "start" else copy.wait()

                @pl.when(head != own.head)
                def _(piece=piece, there=there, i=i):
                    copy = remote(
                        piece,
                        there,
                        kv_send.at[i, head],
                        kv_recv.at[i, own.block],
                        own.of_head(head, own.member),
                    )
                    copy.start() if act == "start" else copy.wait_send()

            return carry

        return to_head

    lax.fori_loop(0, HEADS, keys("start"), 0)
    spread_units(own, q_ref, q_out, q_send, q_recv, q_local, "start")

    def hand(i, order, block, source, act):
        for away in range(1, own.members):
            member = lax.rem(own.member + away, own.members)
            copy = remote(
                source,
                pairs[i][1].at[:, lanes(block, tokens)],
                hand_send.at[i, order * (own.members - 1) + away - 1],
                kv_recv.at[i, block],
                own.of_head(own.head, member),
            )
            copy.start() if act == "start" else copy.wait_send()

    shares = own.total // own.members

    def block_of(order):
        f = own.member + own.members * lax.div(order, own.seq)
        return f * own.seq + lax.rem(order, own.seq)

    for i, (source, _) in enumerate(pairs):
        hand(i, shares - 1, own.block, source.at[head_rows(own.head), :], "start")

    mine = lax.div(own.f, own.members) * own.seq + own.s

    def relay(step, carry):
        order = lax.rem(mine + step, shares)
        block = block_of(order)
        for i, (_, target) in enumerate(pairs):
            there = target.at[:, lanes(block, tokens)]
            remote(
                there, there, kv_send.at[i, 0], kv_recv.at[i, block], own.of_block(0)
            ).wait_recv()
            hand(i, step - 1, block, there, "start")
        return carry

    lax.fori_loop(1, shares, relay, 0)

    def rest(block, carry):
        @pl.when(lax.rem(lax.div(block, own.seq), own.members) != own.member)
        def _():
            for i, (_, target) in enumerate(pairs):
                there = target.at[:, lanes(block, tokens)]
                remote(
                    there, there, kv_send.at[i, 0], kv_recv.at[i, block], own.of_block(0)
                ).wait_recv()

        return carry

    lax.fori_loop(0, own.total, rest, 0)
    await_units(own, q_out, q_send, q_recv)
    lax.fori_loop(0, HEADS, keys("wait"), 0)
    spread_units(own, q_ref, q_out, q_send, q_recv, q_local, "wait")
    for i, (source, _) in enumerate(pairs):
        hand(i, shares - 1, own.block, source.at[head_rows(own.head), :], "wait")

    def settle(step, carry):
        block = block_of(lax.rem(mine + step, shares))
        for i, (_, target) in enumerate(pairs):
            hand(i, step - 1, block, target.at[:, lanes(block, tokens)], "wait")
        return carry

    lax.fori_loop(1, shares, settle, 0)


ANY = pl.BlockSpec(memory_space=pl.ANY)


def comm_params(ident):
    return pltpu.CompilerParams(collective_id=ident, has_side_effects=True)


def to_heads(q, k, v, ident):
    tokens = q.shape[1]
    own = Owners(tokens)
    whole = jax.ShapeDtypeStruct((HEAD_DIM, tokens * own.total), q.dtype)
    few = jax.ShapeDtypeStruct((HEAD_DIM, own.units * UNIT), q.dtype)
    dma = pltpu.SemaphoreType.DMA
    return pl.pallas_call(
        functools.partial(to_heads_kernel, tokens),
        out_shape=[few, whole, whole],
        in_specs=[ANY] * 3,
        out_specs=[ANY] * 3,
        scratch_shapes=[
            dma((HEADS, own.halves)),
            dma((own.units,)),
            dma((own.halves,)),
            dma((2, HEADS)),
            dma((2, own.total)),
            dma((2,)),
            dma((2, own.total // own.members * (own.members - 1))),
        ],
        compiler_params=comm_params(ident),
        cost_estimate=pl.CostEstimate(flops=0, bytes_accessed=whole.size * 8, transcendentals=0),
    )(q, k, v)


def units_to_heads_kernel(tokens, source, target, send, recv, local):
    own = Owners(tokens)
    own.locate()
    own.barrier()
    spread_units(own, source, target, send, recv, local, "start")
    await_units(own, target, send, recv)
    spread_units(own, source, target, send, recv, local, "wait")


def units_to_heads(value, ident):
    tokens = value.shape[1]
    own = Owners(tokens)
    dma = pltpu.SemaphoreType.DMA
    few = jax.ShapeDtypeStruct((HEAD_DIM, own.units * UNIT), value.dtype)
    return pl.pallas_call(
        functools.partial(units_to_heads_kernel, tokens),
        out_shape=few,
        in_specs=[ANY],
        out_specs=ANY,
        scratch_shapes=[dma((HEADS, own.halves)), dma((own.units,)), dma((own.halves,))],
        compiler_params=comm_params(ident),
        cost_estimate=pl.CostEstimate(flops=0, bytes_accessed=few.size * 4, transcendentals=0),
    )(value)


def units_to_tokens_kernel(tokens, source, target, send, recv, local):
    own = Owners(tokens)
    own.locate()
    own.barrier()
    collect_units(own, source, target, send, recv, local, "start")
    await_heads(own, target, send, recv)
    collect_units(own, source, target, send, recv, local, "wait")


def units_to_tokens(value, tokens, ident):
    own = Owners(tokens)
    dma = pltpu.SemaphoreType.DMA
    back = jax.ShapeDtypeStruct((HEADS * HEAD_DIM, tokens), value.dtype)
    return pl.pallas_call(
        functools.partial(units_to_tokens_kernel, tokens),
        out_shape=back,
        in_specs=[ANY],
        out_specs=ANY,
        scratch_shapes=[dma((own.units,)), dma((HEADS, own.halves)), dma((own.halves,))],
        compiler_params=comm_params(ident),
        cost_estimate=pl.CostEstimate(flops=0, bytes_accessed=back.size * 4, transcendentals=0),
    )(value)


def grads_to_tokens_kernel(
    tokens, dq_ref, dk_ref, dv_ref, dq_out, dk_out, dv_out, given, held, total, *sems
):
    q_send, q_recv, q_local, give_send, give_recv, back_send, back_recv, own_sem, local = sems
    own = Owners(tokens)
    own.locate()
    own.barrier()
    pairs = ((dk_ref, dk_out), (dv_ref, dv_out))
    shares = own.total // own.members
    others = own.members - 1
    mine = lax.div(own.f, own.members) * own.seq + own.s

    def block_of(order, member):
        f = member + own.members * lax.div(order, own.seq)
        return f * own.seq + lax.rem(order, own.seq)

    def give(act):
        def one(step, carry):
            order = lax.rem(mine + step, shares)
            for away in range(1, own.members):
                member = lax.rem(own.member + away, own.members)
                block = block_of(order, member)
                for i, (source, _) in enumerate(pairs):
                    copy = remote(
                        source.at[:, lanes(block, tokens)],
                        given.at[i, order * others + others - away],
                        give_send.at[i, order * others + away - 1],
                        give_recv.at[i, order * others + others - away],
                        own.of_head(own.head, member),
                    )
                    copy.start() if act == "start" else copy.wait_send()
            return carry

        return one

    def take(order, i):
        return pltpu.make_async_copy(
            pairs[i][0].at[:, lanes(block_of(order, own.member), tokens)],
            held.at[i, order],
            own_sem.at[i, order],
        )

    def load(order, carry):
        for i in range(2):
            take(order, i).start()
        return carry

    lax.fori_loop(1, shares + 1, lambda s, c: give("start")(lax.rem(s, shares), c), 0)
    lax.fori_loop(0, shares, load, 0)
    collect_units(own, dq_ref, dq_out, q_send, q_recv, q_local, "start")

    def back(order, i, act):
        block = block_of(order, own.member)
        there = pairs[i][1].at[head_rows(own.head), :]

        @pl.when(block == own.block)
        def _():
            copy = pltpu.make_async_copy(held.at[i, order], there, local.at[i])
            copy.start() if act == "start" else copy.wait()

        @pl.when(block != own.block)
        def _():
            copy = remote(
                held.at[i, order],
                there,
                back_send.at[i, order],
                back_recv.at[i, own.head],
                own.of_block(block),
            )
            copy.start() if act == "start" else copy.wait_send()

    def add(step, carry):
        order = lax.rem(mine + step, shares)
        for i in range(2):
            take(order, i).wait()
            total[...] = held[i, order].astype(jnp.float32)
            for j in range(others):
                slot = order * others + j
                remote(
                    given.at[i, slot],
                    given.at[i, slot],
                    give_send.at[i, 0],
                    give_recv.at[i, slot],
                    own.of_block(0),
                ).wait_recv()
                total[...] += given[i, slot].astype(jnp.float32)
            held[i, order] = total[...].astype(held.dtype)
            back(order, i, "start")
        return carry

    lax.fori_loop(1, shares + 1, add, 0)
    await_heads(own, dq_out, q_send, q_recv)

    def arrive(head, carry):
        @pl.when(head != own.head)
        def _():
            for i, (_, target) in enumerate(pairs):
                there = target.at[head_rows(head), :]
                remote(
                    there, there, back_send.at[i, 0], back_recv.at[i, head], own.of_block(0)
                ).wait_recv()

        return carry

    lax.fori_loop(0, HEADS, arrive, 0)
    lax.fori_loop(0, shares, give("wait"), 0)
    collect_units(own, dq_ref, dq_out, q_send, q_recv, q_local, "wait")

    def settle(order, carry):
        for i in range(2):
            back(order, i, "wait")
        return carry

    lax.fori_loop(0, shares, settle, 0)


def grads_to_tokens(dq, dk, dv, tokens, ident):
    own = Owners(tokens)
    dma = pltpu.SemaphoreType.DMA
    back = jax.ShapeDtypeStruct((HEADS * HEAD_DIM, tokens), dq.dtype)
    shares = own.total // own.members
    others = own.members - 1
    return pl.pallas_call(
        functools.partial(grads_to_tokens_kernel, tokens),
        out_shape=[back] * 3,
        in_specs=[ANY] * 3,
        out_specs=[ANY] * 3,
        scratch_shapes=[
            pltpu.VMEM((2, shares * others, HEAD_DIM, tokens), dq.dtype),
            pltpu.VMEM((2, shares, HEAD_DIM, tokens), dq.dtype),
            pltpu.VMEM((HEAD_DIM, tokens), jnp.float32),
            dma((own.units,)),
            dma((HEADS, own.halves)),
            dma((own.halves,)),
            dma((2, shares * others)),
            dma((2, shares * others)),
            dma((2, shares)),
            dma((2, HEADS)),
            dma((2, shares)),
            dma((2,)),
        ],
        compiler_params=comm_params(ident),
        cost_estimate=pl.CostEstimate(flops=0, bytes_accessed=back.size * 12, transcendentals=0),
    )(dq, dk, dv)


QUERIES = 512
KEYS = 512
VMEM_LIMIT = 60 << 20


def first_dims(left, right):
    return lax.dot_general(left, right, (((0,), (0,)), ((), ())), preferred_element_type=jnp.float32)


def plain(left, right):
    return lax.dot_general(left, right, (((1,), (0,)), ((), ())), preferred_element_type=jnp.float32)


def last_dims(left, right):
    return lax.dot_general(left, right, (((1,), (1,)), ((), ())), preferred_element_type=jnp.float32)


def tile_bounds(places, begins, group, width):
    pos, begin = places.reshape(-1, group), begins.reshape(-1, group)
    low, high = begin[:, 0] // width, pos[:, -1] // width + 1
    inner, outer = (begin[:, -1] + width - 1) // width, (pos[:, 0] + 1) // width
    some = inner < outer
    return jnp.stack([low, jnp.where(some, inner, high), jnp.where(some, outer, high), high])


def over_tiles(bounds, group, body, state):
    low, inner, outer, high = (bounds[i, group] for i in range(4))
    before = inner - low

    def edge(step, current):
        return body(jnp.where(step < before, low + step, outer + step - before), True, current)

    state = lax.fori_loop(0, before + high - outer, edge, state)
    return lax.fori_loop(inner, outer, lambda tile, current: body(tile, False, current), state)


def key_lanes(tile):
    return pl.ds(pl.multiple_of(tile * KEYS, KEYS), KEYS)


def visible(tile, pos, begin):
    number = tile * KEYS + lax.broadcasted_iota(jnp.int32, (KEYS, 1), 0)
    return (number <= pos) & (number >= begin)


def attend_kernel(bounds, q_ref, k_ref, v_ref, pos_ref, begin_ref, low_ref, out_ref, lse_ref):
    def one_group(group, carry):
        here = pl.ds(pl.multiple_of(group * QUERIES, QUERIES), QUERIES)
        queries = q_ref[:, here]
        pos, begin = pos_ref[:, here], begin_ref[:, here]

        def tile_step(tile, masked, current):
            top, total, summed = current
            scores = first_dims(k_ref[:, key_lanes(tile)], queries)
            if masked:
                scores = jnp.where(visible(tile, pos, begin), scores, NEGATIVE)
            new_top = jnp.maximum(top, jnp.max(scores, axis=0, keepdims=True))
            weights = jnp.exp(scores - new_top)
            shrink = jnp.exp(top - new_top)
            total = total * shrink + jnp.sum(weights, axis=0, keepdims=True)
            summed = summed * shrink + plain(v_ref[:, key_lanes(tile)], weights.astype(jnp.bfloat16))
            return new_top, total, summed

        top, total, summed = over_tiles(
            bounds,
            group,
            tile_step,
            (
                jnp.full((1, QUERIES), NEGATIVE, jnp.float32),
                jnp.zeros((1, QUERIES), jnp.float32),
                jnp.zeros((HEAD_DIM, QUERIES), jnp.float32),
            ),
        )
        attended = summed / total
        out_ref[:, here] = attended
        low_ref[:, here] = attended.astype(jnp.bfloat16)
        lse_ref[:, here] = top + jnp.log(total)
        return carry

    lax.fori_loop(0, q_ref.shape[1] // QUERIES, one_group, 0)


WHOLE = pl.BlockSpec(memory_space=pltpu.VMEM)


def attend(bounds, q, k, v, pos, begin):
    count = q.shape[1]
    pairs = count * k.shape[1] // 4
    return pl.pallas_call(
        attend_kernel,
        out_shape=[
            jax.ShapeDtypeStruct((HEAD_DIM, count), jnp.bfloat16),
            jax.ShapeDtypeStruct((HEAD_DIM, count), jnp.float32),
            jax.ShapeDtypeStruct((1, count), jnp.float32),
        ],
        in_specs=[pl.BlockSpec(memory_space=pltpu.SMEM)] + [WHOLE] * 5,
        out_specs=[WHOLE] * 3,
        compiler_params=pltpu.CompilerParams(vmem_limit_bytes=VMEM_LIMIT),
        cost_estimate=pl.CostEstimate(
            flops=pairs * 4 * HEAD_DIM, bytes_accessed=4 * k.size, transcendentals=pairs
        ),
    )(bounds, q, k, v, pos, begin)


def attend_back_kernel(
    bounds, q_ref, k_ref, v_ref, g_ref, out_ref, lse_ref, pos_ref, begin_ref, dq_ref, dk_ref, dv_ref,
    dk_sum, dv_sum,
):
    dk_sum[...] = jnp.zeros_like(dk_sum)
    dv_sum[...] = jnp.zeros_like(dv_sum)

    def one_group(group, carry):
        here = pl.ds(pl.multiple_of(group * QUERIES, QUERIES), QUERIES)
        queries, grads = q_ref[:, here], g_ref[:, here]
        pos, begin, lse = pos_ref[:, here], begin_ref[:, here], lse_ref[:, here]
        delta = jnp.sum(grads.astype(jnp.float32) * out_ref[:, here], axis=0, keepdims=True)

        def tile_step(tile, masked, dq):
            there = key_lanes(tile)
            keys, values = k_ref[:, there], v_ref[:, there]
            scores = first_dims(keys, queries)
            if masked:
                scores = jnp.where(visible(tile, pos, begin), scores, NEGATIVE)
            probs = jnp.exp(scores - lse)
            dv_sum[:, there] += last_dims(grads, probs.astype(jnp.bfloat16))
            dscores = (probs * (first_dims(values, grads) - delta)).astype(jnp.bfloat16)
            dk_sum[:, there] += last_dims(queries, dscores)
            return dq + plain(keys, dscores)

        dq = over_tiles(bounds, group, tile_step, jnp.zeros((HEAD_DIM, QUERIES), jnp.float32))
        dq_ref[:, here] = (dq * HEAD_DIM**-0.5).astype(dq_ref.dtype)
        return carry

    lax.fori_loop(0, q_ref.shape[1] // QUERIES, one_group, 0)
    dk_ref[...] = dk_sum[...].astype(dk_ref.dtype)
    dv_ref[...] = dv_sum[...].astype(dv_ref.dtype)


def attend_back(bounds, q, k, v, grads, out, lse, pos, begin):
    pairs = q.shape[1] * k.shape[1] // 4
    return pl.pallas_call(
        attend_back_kernel,
        out_shape=[jax.ShapeDtypeStruct(a.shape, jnp.bfloat16) for a in (q, k, v)],
        in_specs=[pl.BlockSpec(memory_space=pltpu.SMEM)] + [WHOLE] * 8,
        out_specs=[WHOLE] * 3,
        scratch_shapes=[pltpu.VMEM(k.shape, jnp.float32)] * 2,
        compiler_params=pltpu.CompilerParams(vmem_limit_bytes=VMEM_LIMIT),
        cost_estimate=pl.CostEstimate(
            flops=pairs * 10 * HEAD_DIM, bytes_accessed=6 * k.size, transcendentals=pairs
        ),
    )(bounds, q, k, v, grads, out, lse, pos, begin)


SCHEMES = ("A", "A", "A", "B", "C", "C", "C", "C")


def rms_scale(tensor):
    return lax.rsqrt(jnp.mean(tensor * tensor, axis=-1, keepdims=True) + EPSILON)


def angle_tables(offsets):
    half_dim = HEAD_DIM // 2
    frequency = jnp.power(10000.0, -jnp.arange(half_dim, dtype=jnp.float32) / half_dim)
    angles = frequency[:, None] * offsets.astype(jnp.float32)[None, :]
    return jnp.cos(angles)[None], jnp.sin(angles)[None]


def rotate(tensor, cosine, sine_tab):
    pairs = tensor.reshape(HEADS, 2, HEAD_DIM // 2, -1)
    front, back = pairs[:, 0], pairs[:, 1]
    turned = jnp.stack([front * cosine - back * sine_tab, back * cosine + front * sine_tab], axis=1)
    return turned.reshape(tensor.shape)


def matmul(left, right):
    return jnp.dot(left, right, preferred_element_type=jnp.float32)


def contract(left, right, left_dim, right_dim):
    return lax.dot_general(
        left, right, (((left_dim,), (right_dim,)), ((), ())), preferred_element_type=jnp.float32
    )


def per_device(
    layer_input,
    v_first,
    offsets,
    g_attn,
    w_query,
    w_key,
    w_value,
    w_out,
    g_ffn,
    w_gate,
    w_up,
    w_down,
    out_cot,
):
    low = jnp.bfloat16
    tokens = layer_input.shape[0]
    seq, fsdp = lax.axis_size("seq"), lax.axis_size("fsdp")
    devices = seq * fsdp
    seq_index = lax.axis_index("seq")
    own_offsets = lax.dynamic_slice_in_dim(offsets, seq_index * tokens, tokens, 0)

    gains = jnp.zeros((16, 128), low)
    gains = lax.dynamic_update_slice(gains, g_attn[None], (0, 0))
    gains = lax.dynamic_update_slice(gains, g_ffn[None], (1, 0))
    places = jnp.zeros((8, 128), jnp.int32)
    places = lax.dynamic_update_slice(places, own_offsets.reshape(-1, 128), (0, 0))
    shards = (w_gate, w_up, w_query, w_key, w_down, w_value, w_out, gains, places)
    pieces = [(i, 0, shard.shape[1], scheme) for i, (shard, scheme) in enumerate(zip(shards, SCHEMES + ("C",)))]
    *wholes, whole_gains, whole_places = gather_all(shards, pieces, 0)
    proj_gate, proj_up, proj_query, proj_key, proj_down, proj_value, proj_out = (
        whole.reshape(-1, whole.shape[2]) for whole in wholes
    )
    gain_attn = whole_gains[:, 0, : g_attn.shape[0]].reshape(-1).astype(jnp.float32)
    gain_ffn = whole_gains[:, 1, : g_ffn.shape[0]].reshape(-1).astype(jnp.float32)
    all_offsets = (
        whole_places[:, : tokens // 128].reshape(seq, fsdp, tokens).transpose(1, 0, 2).reshape(-1)
    )

    own = Owners(tokens)
    member = lax.rem(lax.axis_index("fsdp"), own.members)
    unit_begins = (jnp.arange(devices * tokens, dtype=jnp.int32) - all_offsets).reshape(
        own.units, own.members, UNIT
    )
    begin = lax.dynamic_index_in_dim(unit_begins, member, 1, keepdims=False).reshape(1, -1)
    pos = (
        (jnp.arange(own.units, dtype=jnp.int32)[:, None] * own.members + member) * UNIT
        + jnp.arange(UNIT, dtype=jnp.int32)[None]
    ).reshape(1, -1)
    bounds = tile_bounds(pos, begin, QUERIES, KEYS)

    cosine, sine_tab = angle_tables(own_offsets)
    input_f32 = layer_input.astype(jnp.float32)
    norm_attn = rms_scale(input_f32)
    normed_a = (input_f32 * norm_attn * gain_attn).astype(low)
    scale = jnp.asarray(HEAD_DIM**-0.5, low)
    q_tokens = rotate(contract(proj_query, normed_a, 0, 1), cosine, sine_tab).astype(low) * scale
    k_tokens = rotate(contract(proj_key, normed_a, 0, 1), cosine, sine_tab).astype(low)
    mixed = (
        0.5 * contract(proj_value, normed_a, 0, 1) + 0.5 * v_first.astype(jnp.float32).T
    ).astype(low)
    q_head, k_head, v_head = to_heads(q_tokens, k_tokens, mixed, 1)
    attended_low, attended, lse = attend(bounds, q_head, k_head, v_head, pos, begin)
    attn_tokens = units_to_tokens(attended_low, tokens, 2)

    after_attn = input_f32 + contract(attn_tokens, proj_out, 0, 0)
    norm_ffn = rms_scale(after_attn)
    normed_f = (after_attn * norm_ffn * gain_ffn).astype(low)
    gate_act = matmul(normed_f, proj_gate)
    up_act = matmul(normed_f, proj_up)
    sigmoid_gate = jax.nn.sigmoid(gate_act)
    silu_gate = gate_act * sigmoid_gate
    hidden = (silu_gate * up_act).astype(low)
    result = (after_attn + matmul(hidden, proj_down)).astype(low)

    grad_down = contract(hidden, out_cot, 0, 0)
    grad_hidden = contract(out_cot, proj_down, 1, 1)
    grad_gate_low = (
        grad_hidden * up_act * sigmoid_gate * (1.0 + gate_act * (1.0 - sigmoid_gate))
    ).astype(low)
    grad_up_low = (grad_hidden * silu_gate).astype(low)
    grad_gate_w = contract(normed_f, grad_gate_low, 0, 0)
    grad_up_w = contract(normed_f, grad_up_low, 0, 0)
    grad_normed_f = contract(grad_gate_low, proj_gate, 1, 1) + contract(grad_up_low, proj_up, 1, 1)
    grad_gain_ffn = jnp.sum(grad_normed_f * after_attn * norm_ffn, axis=0)
    scaled_ffn = grad_normed_f * gain_ffn
    grad_after = (
        out_cot.astype(jnp.float32)
        + norm_ffn * scaled_ffn
        - after_attn * norm_ffn**3 * jnp.mean(scaled_ffn * after_attn, axis=-1, keepdims=True)
    )
    grad_attn_low = grad_after.astype(low)
    grad_out_w = contract(attn_tokens, grad_attn_low, 1, 0)
    grad_attended = contract(proj_out, grad_attn_low, 1, 1).astype(low)

    grad_head = units_to_heads(grad_attended, 3)
    dq_head, dk_head, dv_head = attend_back(
        bounds, q_head, k_head, v_head, grad_head, attended, lse, pos, begin
    )
    dq_rot, dk_rot, grad_mixed = grads_to_tokens(dq_head, dk_head, dv_head, tokens, 4)
    grad_q = rotate(dq_rot.astype(jnp.float32), cosine, -sine_tab).astype(low)
    grad_k = rotate(dk_rot.astype(jnp.float32), cosine, -sine_tab).astype(low)
    grad_v = grad_mixed * jnp.asarray(0.5, low)
    grad_first = grad_v.T.astype(jnp.float32)
    grad_query_w = contract(normed_a, grad_q, 0, 1)
    grad_key_w = contract(normed_a, grad_k, 0, 1)
    grad_value_w = contract(normed_a, grad_v, 0, 1)
    grad_normed_a = (
        contract(grad_q, proj_query, 0, 1)
        + contract(grad_k, proj_key, 0, 1)
        + contract(grad_v, proj_value, 0, 1)
    )
    grad_gain_attn = jnp.sum(grad_normed_a * input_f32 * norm_attn, axis=0)
    scaled_attn = grad_normed_a * gain_attn
    grad_layer = (
        grad_after
        + norm_attn * scaled_attn
        - input_f32 * norm_attn**3 * jnp.mean(scaled_attn * input_f32, axis=-1, keepdims=True)
    )

    terms = [
        grad.astype(low).reshape(devices, -1, grad.shape[1])
        for grad in (grad_gate_w, grad_up_w, grad_query_w, grad_key_w, grad_down, grad_value_w, grad_out_w)
    ]
    gain_terms = jnp.zeros((devices, 8, 128), jnp.float32)
    for row, grad in enumerate((grad_gain_attn, grad_gain_ffn)):
        gain_terms = lax.dynamic_update_slice(gain_terms, grad.reshape(devices, 1, -1), (0, row, 0))
    sums = reduce_all([*terms, gain_terms], pieces[:-1], 5)
    sum_gate, sum_up, sum_query, sum_key, sum_down, sum_value, sum_out, sum_gains = sums
    return (
        result,
        grad_layer,
        grad_first,
        sum_gains[0, : g_attn.shape[0]],
        sum_query,
        sum_key,
        sum_value,
        sum_out,
        sum_gains[1, : g_ffn.shape[0]],
        sum_gate,
        sum_up,
        sum_down,
    )


def solution(mesh):
    return jax.shard_map(
        per_device,
        mesh=mesh,
        in_specs=(
            P(("fsdp", "seq"), None),
            P(("fsdp", "seq"), None),
            P("fsdp"),
            P(("seq", "fsdp")),
            P(("seq", "fsdp"), None),
            P(("seq", "fsdp"), None),
            P(("seq", "fsdp"), None),
            P(("seq", "fsdp"), None),
            P(("seq", "fsdp")),
            P(("seq", "fsdp"), None),
            P(("seq", "fsdp"), None),
            P(("seq", "fsdp"), None),
            P(("fsdp", "seq"), None),
        ),
        out_specs=(
            P(("fsdp", "seq"), None),
            P(("fsdp", "seq"), None),
            P(("fsdp", "seq"), None),
            P(("seq", "fsdp")),
            P(("seq", "fsdp"), None),
            P(("seq", "fsdp"), None),
            P(("seq", "fsdp"), None),
            P(("seq", "fsdp"), None),
            P(("seq", "fsdp")),
            P(("seq", "fsdp"), None),
            P(("seq", "fsdp"), None),
            P(("seq", "fsdp"), None),
        ),
        check_vma=False,
    )
```

```python
import functools, math
import jax
import jax.numpy as jnp
from jax import lax
from jax.experimental import pallas as pl
from jax.experimental.pallas import tpu as pltpu
from jax.sharding import PartitionSpec as P

EPSILON = 1e-06
MESH = pl.DeviceIdType.MESH


class Grid:
    def __init__(self):
        self.seq = lax.axis_size("seq")
        self.fsdp = lax.axis_size("fsdp")
        self.size = {"z": self.seq, "y": 2, "x": self.fsdp // 4}
        self.stride = {"x": 2, "y": 2 * (self.fsdp // 4)}
        self.total = self.seq * self.fsdp
        self.plane = self.total // 2

    def locate(self):
        z, f = lax.axis_index("seq"), lax.axis_index("fsdp")
        nx = self.size["x"]
        self.f, self.zi = f, z
        self.core = lax.rem(f, 2)
        self.me = {"z": z, "y": lax.div(f, 2 * nx), "x": lax.rem(lax.div(f, 2), nx)}

    def step(self, dim, delta):
        if dim == "z":
            return {"seq": self.zi + delta}
        if dim == "core":
            return {"fsdp": self.f + 1 - 2 * self.core}
        return {"fsdp": self.f + delta * self.stride[dim]}

    def partner(self, dim):
        return self.step(dim, 1 - 2 * self.me[dim])

    def dirs(self, dim):
        return (0,) if self.size[dim] == 2 else (1, -1)

    def linear(self, at, core):
        nx = self.size["x"]
        return at["z"] * self.fsdp + (at["y"] * nx + at["x"]) * 2 + core

    def neighbours(self):
        found = [(None, self.step("core", 1))]
        for dim in ("z", "y", "x"):
            n = self.size[dim]
            if n == 1:
                continue
            if n == 2:
                found.append((None, self.partner(dim)))
            else:
                found.append((self.me[dim] < n - 1, self.step(dim, 1)))
                found.append((self.me[dim] > 0, self.step(dim, -1)))
        return found

    def barrier(self):
        sem = pltpu.get_barrier_semaphore()
        count = 0
        for exists, device in self.neighbours():
            if exists is None:
                pl.semaphore_signal(sem, inc=1, device_id=device, device_id_type=MESH)
                count = count + 1
            else:

                @pl.when(exists)
                def _(device=device):
                    pl.semaphore_signal(sem, inc=1, device_id=device, device_id_type=MESH)

                count = count + exists.astype(jnp.int32)
        pl.semaphore_wait(sem, count)

    def digits(self, order, number):
        at, ok = {}, None
        rest = number
        for dim in order:
            n = self.size[dim]
            base = 2 if n == 2 else 2 * n - 1
            digit = lax.rem(rest, base)
            rest = lax.div(rest, base)
            if n == 2:
                at[dim] = lax.rem(self.me[dim] + digit, 2)
            elif n == 1:
                at[dim] = self.me[dim]
            else:
                away = lax.div(digit + 1, 2)
                at[dim] = jnp.where(lax.rem(digit, 2) == 1, self.me[dim] - away, self.me[dim] + away)
                inside = (at[dim] >= 0) & (at[dim] < n)
                ok = inside if ok is None else ok & inside
        return at, ok

    def places(self, order):
        return math.prod(2 if self.size[d] == 2 else 2 * self.size[d] - 1 for d in order)

    def rank(self, order, at, upto):
        value, width = 0, 1
        for dim in order[:upto]:
            value = value + at[dim] * width
            width *= self.size[dim]
        return value

    def slots(self, order):
        first, count, width = [], 0, 1
        for dim in order:
            width *= self.size[dim]
            first.append(count)
            if self.size[dim] > 1:
                count += width * len(self.dirs(dim))
        return first, count

    def branch(self, order, j, way, at):
        dim = order[j]
        n = self.size[dim]
        ok = None
        for later in order[j + 1 :]:
            same = at[later] == self.me[later]
            ok = same if ok is None else ok & same
        if n == 2:
            here = at[dim] == self.me[dim]
        elif way == 1:
            here = (at[dim] <= self.me[dim]) & (self.me[dim] < n - 1)
        else:
            here = (at[dim] >= self.me[dim]) & (self.me[dim] > 0)
        return here if ok is None else ok & here


ORDERS = {"A": ("z", "x", "y"), "B": ("x", "y", "z"), "C": ("y", "z", "x")}


class Gather:
    def __init__(self, grid, pieces, sources, outs, sems):
        self.grid, self.pieces, self.sources, self.outs = grid, pieces, sources, outs
        self.recv, self.send, self.core_send, self.own_sem = sems
        self.places = grid.places(ORDERS["A"])

    @staticmethod
    def semaphores(grid, pieces, arrays):
        slots = max(grid.slots(order)[1] for order in ORDERS.values())
        dma = pltpu.SemaphoreType.DMA
        return [
            dma((len(pieces), grid.total)),
            dma((len(pieces), slots)),
            dma((len(pieces), grid.plane)),
            dma((arrays,)),
        ]

    def own(self, i):
        mine = self.grid.linear(self.grid.me, self.grid.core)
        return pltpu.make_async_copy(self.sources[i], self.outs[i].at[mine], self.own_sem.at[i])

    def view(self, ref, p):
        return ref.at[:, pl.ds(self.pieces[p][1], self.pieces[p][2])]

    def sends(self, p, at, source, act):
        grid = self.grid
        order = ORDERS[self.pieces[p][3]]
        first, _ = grid.slots(order)
        number = grid.linear(at, grid.core)
        target = self.view(self.outs[self.pieces[p][0]].at[number], p)

        def copy(sem, device):
            return pltpu.make_async_remote_copy(
                src_ref=source,
                dst_ref=target,
                send_sem=sem,
                recv_sem=self.recv.at[p, number],
                device_id=device,
                device_id_type=MESH,
            )

        for j, dim in enumerate(order):
            if grid.size[dim] == 1:
                continue
            ways = grid.dirs(dim)
            for w, way in enumerate(ways):
                slot = first[j] + grid.rank(order, at, j + 1) * len(ways) + w
                device = grid.partner(dim) if way == 0 else grid.step(dim, way)

                @pl.when(grid.branch(order, j, way, at))
                def _(device=device, slot=slot):
                    act(copy(self.send.at[p, slot], device))

        act(copy(self.core_send.at[p, grid.rank(order, at, 3)], grid.step("core", 1)))

    def arrive(self, p, number):
        there = self.view(self.outs[self.pieces[p][0]].at[number], p)
        pltpu.make_async_remote_copy(
            src_ref=there,
            dst_ref=there,
            send_sem=self.core_send.at[p, 0],
            recv_sem=self.recv.at[p, number],
            device_id=self.grid.step("core", 1),
            device_id_type=MESH,
        ).wait_recv()

    def each(self, number, act):
        for p in range(len(self.pieces)):
            at, ok = self.grid.digits(ORDERS[self.pieces[p][3]], number)

            def run(p=p, at=at):
                act(p, at)

            if ok is None:
                run()
            else:
                pl.when(ok)(run)

    def start(self):
        for i in range(len(self.sources)):
            self.own(i).start()
        for p in range(len(self.pieces)):
            self.sends(
                p, self.grid.me, self.view(self.sources[self.pieces[p][0]], p), lambda c: c.start()
            )

    def relay(self, number):
        def act(p, at):
            where = self.grid.linear(at, self.grid.core)
            self.arrive(p, where)
            self.sends(p, at, self.view(self.outs[self.pieces[p][0]].at[where], p), lambda c: c.start())

        self.each(number, act)

    def finish(self):
        def act(p, at):
            self.arrive(p, self.grid.linear(at, 1 - self.grid.core))
            where = self.grid.linear(at, self.grid.core)
            self.sends(
                p, at, self.view(self.outs[self.pieces[p][0]].at[where], p), lambda c: c.wait_send()
            )

        def one(number, carry):
            self.each(number, act)
            return carry

        lax.fori_loop(0, self.places, one, 0)
        for i in range(len(self.sources)):
            self.own(i).wait()


def gather_kernel(pieces, n_arrays, *refs):
    grid = Grid()
    grid.locate()
    tree = Gather(grid, pieces, refs[:n_arrays], refs[n_arrays : 2 * n_arrays], refs[2 * n_arrays :])
    grid.barrier()
    tree.start()

    def forward(number, carry):
        tree.relay(number)
        return carry

    lax.fori_loop(1, tree.places, forward, 0)
    tree.finish()


def gathered_shapes(grid, arrays):
    return [jax.ShapeDtypeStruct((grid.total, *a.shape), a.dtype) for a in arrays]


def gather_all(arrays, pieces, ident):
    grid = Grid()
    n = len(arrays)
    moved = sum(a.size * a.dtype.itemsize for a in arrays) * grid.total
    return pl.pallas_call(
        functools.partial(gather_kernel, pieces, n),
        out_shape=gathered_shapes(grid, arrays),
        in_specs=[pl.BlockSpec(memory_space=pl.ANY)] * n,
        out_specs=[pl.BlockSpec(memory_space=pl.ANY)] * n,
        scratch_shapes=Gather.semaphores(grid, pieces, n),
        compiler_params=pltpu.CompilerParams(collective_id=ident, has_side_effects=True),
        cost_estimate=pl.CostEstimate(flops=0, bytes_accessed=moved, transcendentals=0),
    )(*arrays)


class Reduce:
    def __init__(self, grid, pieces, parts, outs, scratch):
        n = len(pieces)
        self.grid, self.pieces, self.parts, self.outs = grid, pieces, parts, outs
        self.pair, self.slot, self.held, self.total = (
            scratch[i * n : (i + 1) * n] for i in range(4)
        )
        sems = scratch[4 * n :]
        self.core_send, self.core_recv, self.tree_send, self.tree_recv, self.own_sem = sems
        self.places = grid.places(ORDERS["A"])

    @staticmethod
    def scratch(grid, pieces, arrays):
        most = max(grid.slots(order)[1] for order in ORDERS.values())
        shape = [(arrays[p[0]].shape[1], p[2]) for p in pieces]
        kind = [arrays[p[0]].dtype for p in pieces]
        count = [grid.slots(ORDERS[p[3]])[1] for p in pieces]
        dma = pltpu.SemaphoreType.DMA
        n = len(pieces)
        return (
            [pltpu.VMEM((grid.plane, *s), k) for s, k in zip(shape, kind)]
            + [pltpu.VMEM((c, *s), k) for c, s, k in zip(count, shape, kind)]
            + [pltpu.VMEM((2, *s), k) for s, k in zip(shape, kind)]
            + [pltpu.VMEM(s, jnp.float32) for s in shape]
            + [dma((n, grid.plane)), dma((n, grid.plane)), dma((n, grid.plane)), dma((n, most)), dma((n, 2))]
        )

    def each(self, number, act):
        for p in range(len(self.pieces)):
            at, ok = self.grid.digits(ORDERS[self.pieces[p][3]], number)

            def run(p=p, at=at):
                act(p, at)

            if ok is None:
                run()
            else:
                pl.when(ok)(run)

    def block(self, p, at, core):
        array, lower, count, _ = self.pieces[p]
        return self.parts[array].at[self.grid.linear(at, core), :, pl.ds(lower, count)]

    def rank(self, p, at):
        return self.grid.rank(ORDERS[self.pieces[p][3]], at, 3)

    def to_sibling(self, p, at):
        rank = self.rank(p, at)
        return pltpu.make_async_remote_copy(
            src_ref=self.block(p, at, 1 - self.grid.core),
            dst_ref=self.pair[p].at[rank],
            send_sem=self.core_send.at[p, rank],
            recv_sem=self.core_recv.at[p, rank],
            device_id=self.grid.step("core", 1),
            device_id_type=MESH,
        )

    def fetch(self, p, at, number):
        slot = lax.rem(number, 2)
        return pltpu.make_async_copy(
            self.block(p, at, self.grid.core), self.held[p].at[slot], self.own_sem.at[p, slot]
        )

    def to_parent(self, p, at, act):
        grid = self.grid
        order = ORDERS[self.pieces[p][3]]
        first, _ = grid.slots(order)
        rank = self.rank(p, at)
        for j, dim in enumerate(order):
            if grid.size[dim] == 1:
                continue
            ways = grid.dirs(dim)
            ok = None
            for later in order[j + 1 :]:
                same = at[later] == grid.me[later]
                ok = same if ok is None else ok & same
            for w, way in enumerate(ways):
                slot = first[j] + grid.rank(order, at, j + 1) * len(ways) + w
                if way == 0:
                    here, device = at[dim] != grid.me[dim], grid.partner(dim)
                elif way == 1:
                    here, device = at[dim] < grid.me[dim], grid.step(dim, -1)
                else:
                    here, device = at[dim] > grid.me[dim], grid.step(dim, 1)
                here = here if ok is None else ok & here

                @pl.when(here)
                def _(slot=slot, device=device):
                    act(
                        pltpu.make_async_remote_copy(
                            src_ref=self.pair[p].at[rank],
                            dst_ref=self.slot[p].at[slot],
                            send_sem=self.tree_send.at[p, rank],
                            recv_sem=self.tree_recv.at[p, slot],
                            device_id=device,
                            device_id_type=MESH,
                        )
                    )

    def combine(self, p, at, number):
        grid = self.grid
        order = ORDERS[self.pieces[p][3]]
        first, _ = grid.slots(order)
        rank = self.rank(p, at)
        total, slots = self.total[p], self.slot[p]
        self.to_sibling(p, at).wait_recv()
        self.fetch(p, at, number).wait()
        total[...] = self.held[p][lax.rem(number, 2)].astype(jnp.float32) + self.pair[p][
            rank
        ].astype(jnp.float32)
        for j in reversed(range(3)):
            dim = order[j]
            if grid.size[dim] == 1:
                continue
            ways = grid.dirs(dim)
            for w, way in enumerate(ways):
                slot = first[j] + grid.rank(order, at, j + 1) * len(ways) + w

                @pl.when(grid.branch(order, j, way, at))
                def _(slot=slot):
                    pltpu.make_async_remote_copy(
                        src_ref=slots.at[slot],
                        dst_ref=slots.at[slot],
                        send_sem=self.tree_send.at[p, rank],
                        recv_sem=self.tree_recv.at[p, slot],
                        device_id=grid.step("core", 1),
                        device_id_type=MESH,
                    ).wait_recv()
                    total[...] += slots[slot].astype(jnp.float32)

    def start(self):
        places = self.places

        def one(step, carry):
            self.each(places - 1 - step, lambda p, at: self.to_sibling(p, at).start())
            return carry

        self.each(places - 1, lambda p, at: self.fetch(p, at, places - 1).start())
        lax.fori_loop(0, places, one, 0)

    def climb(self, step):
        number = self.places - 1 - step
        self.each(number - 1, lambda p, at: self.fetch(p, at, number - 1).start())

        def work(p, at):
            self.combine(p, at, number)
            self.pair[p][self.rank(p, at)] = self.total[p][...].astype(self.pair[p].dtype)
            self.to_parent(p, at, lambda copy: copy.start())

        self.each(number, work)

    def finish(self):
        def root(p, at):
            self.combine(p, at, 0)
            array, lower, count, _ = self.pieces[p]
            self.outs[array][:, lower : lower + count] = self.total[p][...]

        self.each(0, root)

        def one(number, carry):
            def drain(p, at):
                self.to_sibling(p, at).wait_send()

                @pl.when(number > 0)
                def _():
                    self.to_parent(p, at, lambda copy: copy.wait_send())

            self.each(number, drain)
            return carry

        lax.fori_loop(0, self.places, one, 0)


def reduce_kernel(pieces, n_arrays, *refs):
    grid = Grid()
    grid.locate()
    tree = Reduce(grid, pieces, refs[:n_arrays], refs[n_arrays : 2 * n_arrays], refs[2 * n_arrays :])
    grid.barrier()
    tree.start()

    def climb(step, carry):
        tree.climb(step)
        return carry

    lax.fori_loop(0, tree.places - 1, climb, 0)
    tree.finish()


VMEM_LIMIT = 60 << 20


def summed_shapes(arrays):
    return [jax.ShapeDtypeStruct(a.shape[1:], jnp.float32) for a in arrays]


def reduce_all(arrays, pieces, ident):
    grid = Grid()
    n = len(arrays)
    moved = sum(a.size * a.dtype.itemsize for a in arrays)
    return pl.pallas_call(
        functools.partial(reduce_kernel, pieces, n),
        out_shape=summed_shapes(arrays),
        in_specs=[pl.BlockSpec(memory_space=pl.ANY)] * n,
        out_specs=[pl.BlockSpec(memory_space=pltpu.VMEM)] * n,
        scratch_shapes=Reduce.scratch(grid, pieces, arrays),
        compiler_params=pltpu.CompilerParams(
            collective_id=ident, has_side_effects=True, vmem_limit_bytes=VMEM_LIMIT
        ),
        cost_estimate=pl.CostEstimate(flops=0, bytes_accessed=2 * moved, transcendentals=0),
    )(*arrays)


HEADS = 16
HEAD_DIM = 64
UNIT = 128
NEGATIVE = -1e30


class Owners:
    def __init__(self, tokens):
        self.seq, self.fsdp = lax.axis_size("seq"), lax.axis_size("fsdp")
        self.total = self.seq * self.fsdp
        self.members = self.total // HEADS
        self.heads_here = HEADS // self.seq
        self.tokens = tokens
        self.halves = tokens // UNIT
        self.units = self.halves * self.total // self.members

    def locate(self):
        s, f = lax.axis_index("seq"), lax.axis_index("fsdp")
        self.s, self.f = s, f
        self.linear = s * self.fsdp + f
        self.block = f * self.seq + s
        self.head = s * self.heads_here + lax.div(f, self.members)
        self.member = lax.rem(f, self.members)

    def of_head(self, head, member):
        return {
            "seq": lax.div(head, self.heads_here),
            "fsdp": lax.rem(head, self.heads_here) * self.members + member,
        }

    def of_block(self, block):
        return {"seq": lax.rem(block, self.seq), "fsdp": lax.div(block, self.seq)}

    def barrier(self):
        sem = pltpu.get_barrier_semaphore()

        def greet(delta, carry):
            other = lax.rem(self.linear + delta, self.total)
            device = {"seq": lax.div(other, self.fsdp), "fsdp": lax.rem(other, self.fsdp)}
            pl.semaphore_signal(sem, inc=1, device_id=device, device_id_type=MESH)
            return carry

        lax.fori_loop(1, self.total, greet, 0)
        pl.semaphore_wait(sem, self.total - 1)


def remote(source, target, send_sem, recv_sem, device):
    return pltpu.make_async_remote_copy(
        src_ref=source,
        dst_ref=target,
        send_sem=send_sem,
        recv_sem=recv_sem,
        device_id=device,
        device_id_type=MESH,
    )


def head_rows(head):
    return pl.ds(pl.multiple_of(head * HEAD_DIM, HEAD_DIM), HEAD_DIM)


def lanes(number, width):
    return pl.ds(pl.multiple_of(number * width, width), width)


def spread_units(own, source, target, send, recv, local, act):
    def to_head(delta, carry):
        head = lax.rem(own.head + delta, HEADS)
        for half in range(own.halves):
            unit = own.halves * own.block + half
            member = lax.rem(unit, own.members)
            place = lax.div(unit, own.members)
            piece = source.at[head_rows(head), pl.ds(half * UNIT, UNIT)]
            there = target.at[:, lanes(place, UNIT)]
            here = (head == own.head) & (member == own.member)

            @pl.when(here)
            def _(piece=piece, there=there, half=half):
                copy = pltpu.make_async_copy(piece, there, local.at[half])
                copy.start() if act == "start" else copy.wait()

            @pl.when(jnp.logical_not(here))
            def _(piece=piece, there=there, half=half, member=member, place=place, head=head):
                copy = remote(
                    piece, there, send.at[head, half], recv.at[place], own.of_head(head, member)
                )
                copy.start() if act == "start" else copy.wait_send()

        return carry

    lax.fori_loop(0, HEADS, to_head, 0)


def await_units(own, target, send, recv):
    def one(place, carry):
        unit = place * own.members + own.member
        there = target.at[:, lanes(place, UNIT)]

        @pl.when(lax.div(unit, own.halves) != own.block)
        def _():
            remote(
                there, there, send.at[0, 0], recv.at[place], own.of_block(0)
            ).wait_recv()

        return carry

    lax.fori_loop(0, own.units, one, 0)


def collect_units(own, source, target, send, recv, local, act, first, count):
    def one(step, carry):
        place = first + step
        unit = place * own.members + own.member
        block, half = lax.div(unit, own.halves), lax.rem(unit, own.halves)
        piece = source.at[:, lanes(place, UNIT)]
        there = target.at[head_rows(own.head), lanes(half, UNIT)]

        @pl.when(block == own.block)
        def _():
            copy = pltpu.make_async_copy(piece, there, local.at[half])
            copy.start() if act == "start" else copy.wait()

        @pl.when(block != own.block)
        def _():
            copy = remote(
                piece, there, send.at[place], recv.at[own.head, half], own.of_block(block)
            )
            copy.start() if act == "start" else copy.wait_send()

        return carry

    lax.fori_loop(0, count, one, 0)


def await_heads(own, target, send, recv):
    def one(head, carry):
        for half in range(own.halves):
            unit = own.halves * own.block + half
            there = target.at[head_rows(head), pl.ds(half * UNIT, UNIT)]

            @pl.when((head != own.head) | (lax.rem(unit, own.members) != own.member))
            def _(there=there, half=half):
                remote(
                    there, there, send.at[0], recv.at[head, half], own.of_block(0)
                ).wait_recv()

        return carry

    lax.fori_loop(0, HEADS, one, 0)


QUERIES = 512
KEYS = 1024
BESIDE_EXCHANGE = 2
BESIDE_TILES = 2
ANY = pl.BlockSpec(memory_space=pl.ANY)
WHOLE = pl.BlockSpec(memory_space=pltpu.VMEM)


def plain(left, right):
    return lax.dot_general(left, right, (((1,), (0,)), ((), ())), preferred_element_type=jnp.float32)


def first_dims(left, right):
    return lax.dot_general(left, right, (((0,), (0,)), ((), ())), preferred_element_type=jnp.float32)


def last_dims(left, right):
    return lax.dot_general(left, right, (((1,), (1,)), ((), ())), preferred_element_type=jnp.float32)


class Tiles:
    def __init__(self, own):
        self.span = QUERIES * own.members
        self.groups = own.units * UNIT // QUERIES
        self.longest = own.total * own.tokens // 2

    def fold(self, group, body, state):
        start = group * self.span
        low = lax.div(jnp.maximum(start - self.longest + 1, 0), KEYS)
        edge, high = lax.div(start, KEYS), lax.div(start + self.span + KEYS - 1, KEYS)
        state = lax.fori_loop(low, edge, lambda tile, s: body(tile, False, s), state)
        return lax.fori_loop(edge, high, lambda tile, s: body(tile, True, s), state)


def key_lanes(tile):
    return pl.ds(pl.multiple_of(tile * KEYS, KEYS), KEYS)


def group_lanes(group):
    return pl.ds(pl.multiple_of(group * QUERIES, QUERIES), QUERIES)


def shown(scores, tile, causal, pos, begin):
    number = tile * KEYS + lax.broadcasted_iota(jnp.int32, (KEYS, 1), 0)
    allowed = number >= begin
    if causal:
        allowed = allowed & (number <= pos)
    return jnp.where(allowed, scores, NEGATIVE)


def attend_group(tiles, group, q_ref, k_ref, v_ref, pos_ref, begin_ref, step, number):
    here = group_lanes(group)
    queries, pos, begin = q_ref[:, here], pos_ref[:, here], begin_ref[:, here]

    def body(tile, causal, current):
        number, top, total, summed = current
        number = step(number)
        scores = shown(first_dims(k_ref[:, key_lanes(tile)], queries), tile, causal, pos, begin)
        new_top = jnp.maximum(top, jnp.max(scores, axis=0, keepdims=True))
        weights = jnp.exp(scores - new_top)
        shrink = jnp.exp(top - new_top)
        total = total * shrink + jnp.sum(weights, axis=0, keepdims=True)
        summed = summed * shrink + plain(v_ref[:, key_lanes(tile)], weights.astype(jnp.bfloat16))
        return number, new_top, total, summed

    number, top, total, summed = tiles.fold(
        group,
        body,
        (
            number,
            jnp.full((1, QUERIES), NEGATIVE, jnp.float32),
            jnp.zeros((1, QUERIES), jnp.float32),
            jnp.zeros((HEAD_DIM, QUERIES), jnp.float32),
        ),
    )
    return summed / total, top + jnp.log(total), number


class ToHeads:
    def __init__(self, own, sources, targets, sems):
        self.own = own
        self.q_ref, *pairs = sources
        self.q_out, *outs = targets
        self.pairs = tuple(zip(pairs, outs))
        self.q_send, self.q_recv, self.q_local, self.send, self.recv, self.local, self.hand_send = sems
        self.shares = own.total // own.members
        self.mine = lax.div(own.f, own.members) * own.seq + own.s

    @staticmethod
    def semaphores(own):
        dma = pltpu.SemaphoreType.DMA
        return [
            dma((HEADS, own.halves)),
            dma((own.units,)),
            dma((own.halves,)),
            dma((2, HEADS)),
            dma((2, own.total)),
            dma((2,)),
            dma((2, own.total // own.members * (own.members - 1))),
        ]

    def keys(self, act):
        own = self.own

        def to_head(delta, carry):
            head = lax.rem(own.head + delta, HEADS)
            for i, (source, target) in enumerate(self.pairs):
                piece = source.at[head_rows(head), :]
                there = target.at[:, lanes(own.block, own.tokens)]

                @pl.when(head == own.head)
                def _(piece=piece, there=there, i=i):
                    copy = pltpu.make_async_copy(piece, there, self.local.at[i])
                    copy.start() if act == "start" else copy.wait()

                @pl.when(head != own.head)
                def _(piece=piece, there=there, i=i):
                    copy = remote(
                        piece,
                        there,
                        self.send.at[i, head],
                        self.recv.at[i, own.block],
                        own.of_head(head, own.member),
                    )
                    copy.start() if act == "start" else copy.wait_send()

            return carry

        lax.fori_loop(0, HEADS, to_head, 0)

    def hand(self, i, order, block, source, act):
        own = self.own
        for away in range(1, own.members):
            member = lax.rem(own.member + away, own.members)
            copy = remote(
                source,
                self.pairs[i][1].at[:, lanes(block, own.tokens)],
                self.hand_send.at[i, order * (own.members - 1) + away - 1],
                self.recv.at[i, block],
                own.of_head(own.head, member),
            )
            copy.start() if act == "start" else copy.wait_send()

    def hand_own(self, act):
        for i, (source, _) in enumerate(self.pairs):
            self.hand(i, self.shares - 1, self.own.block, source.at[head_rows(self.own.head), :], act)

    def block_of(self, step):
        order = lax.rem(self.mine + step, self.shares)
        f = self.own.member + self.own.members * lax.div(order, self.own.seq)
        return f * self.own.seq + lax.rem(order, self.own.seq)

    def arrive(self, i, block):
        there = self.pairs[i][1].at[:, lanes(block, self.own.tokens)]
        remote(
            there, there, self.send.at[i, 0], self.recv.at[i, block], self.own.of_block(0)
        ).wait_recv()
        return there

    def start(self):
        self.keys("start")
        spread_units(self.own, self.q_ref, self.q_out, self.q_send, self.q_recv, self.q_local, "start")
        self.hand_own("start")

    def relay(self, step):
        block = self.block_of(step)
        for i in range(2):
            self.hand(i, step - 1, block, self.arrive(i, block), "start")

    def finish(self):
        own = self.own

        def rest(block, carry):
            @pl.when(lax.rem(lax.div(block, own.seq), own.members) != own.member)
            def _():
                for i in range(2):
                    self.arrive(i, block)

            return carry

        lax.fori_loop(0, own.total, rest, 0)
        await_units(own, self.q_out, self.q_send, self.q_recv)
        self.keys("wait")
        spread_units(own, self.q_ref, self.q_out, self.q_send, self.q_recv, self.q_local, "wait")
        self.hand_own("wait")

        def settle(step, carry):
            block = self.block_of(step)
            for i, (_, target) in enumerate(self.pairs):
                self.hand(i, step - 1, block, target.at[:, lanes(block, own.tokens)], "wait")
            return carry

        lax.fori_loop(1, self.shares, settle, 0)


def forward_kernel(tokens, pieces, n, *refs):
    tokens_of = refs[:3]
    pos_ref, begin_ref = refs[3:5]
    sources = refs[5 : 5 + n]
    wholes = refs[5 + n : 5 + 2 * n]
    keep = refs[5 + 2 * n : 8 + 2 * n]
    out_ref, lse_ref, back_ref = refs[8 + 2 * n : 11 + 2 * n]
    *heads, low_ref = refs[11 + 2 * n : 15 + 2 * n]
    sems = refs[15 + 2 * n :]
    grid, own = Grid(), Owners(tokens)
    grid.locate()
    own.locate()
    tree = Gather(grid, pieces, sources, wholes, sems[:4])
    exchange = ToHeads(own, tokens_of, heads, sems[4:11])
    out_send, out_recv, out_local, keep_sem = sems[11:]
    tiles = Tiles(own)

    own.barrier()
    exchange.start()
    tree.start()

    def paced(every, first):
        def advance(count):
            number = lax.div(count, every)

            @pl.when((lax.rem(count, every) == 0) & (number < tree.places))
            def _():
                tree.relay(number)

            return count + 1

        return advance, first * every

    beside, count = paced(BESIDE_EXCHANGE, 1)

    def relay(step, count):
        exchange.relay(step)
        return beside(count)

    count = lax.fori_loop(1, exchange.shares, relay, jnp.int32(count))
    number = lax.div(count + BESIDE_EXCHANGE - 1, BESIDE_EXCHANGE)
    advance, number = paced(BESIDE_TILES, number)
    exchange.finish()
    keeping = [pltpu.make_async_copy(heads[i], keep[i], keep_sem.at[i]) for i in range(3)]
    for copy in keeping:
        copy.start()
    units = QUERIES // UNIT

    def one_group(group, number):
        here = group_lanes(group)
        attended, lse, number = attend_group(
            tiles, group, *heads, pos_ref, begin_ref, advance, number
        )
        out_ref[:, here] = attended
        lse_ref[:, here] = lse
        low_ref[:, here] = attended.astype(low_ref.dtype)
        collect_units(
            own, low_ref, back_ref, out_send, out_recv, out_local, "start", group * units, units
        )
        return number

    number = lax.fori_loop(0, tiles.groups, one_group, number)
    number = lax.div(number + BESIDE_TILES - 1, BESIDE_TILES)

    def last(number, carry):
        tree.relay(number)
        return carry

    lax.fori_loop(number, tree.places, last, 0)
    await_heads(own, back_ref, out_send, out_recv)
    collect_units(own, low_ref, back_ref, out_send, out_recv, out_local, "wait", 0, own.units)
    tree.finish()
    for copy in keeping:
        copy.wait()


def forward(q, k, v, pos, begin, arrays, pieces, ident):
    tokens, kind = q.shape[1], q.dtype
    grid, own = Grid(), Owners(tokens)
    n = len(arrays)
    count = own.units * UNIT
    dma = pltpu.SemaphoreType.DMA
    heads = [(HEAD_DIM, count)] + [(HEAD_DIM, own.total * tokens)] * 2
    pairs = count * own.total * tokens // 3
    moved = sum(a.size * a.dtype.itemsize for a in arrays) * grid.total
    outs = pl.pallas_call(
        functools.partial(forward_kernel, tokens, pieces, n),
        out_shape=gathered_shapes(grid, arrays)
        + [jax.ShapeDtypeStruct(s, kind) for s in heads]
        + [
            jax.ShapeDtypeStruct((HEAD_DIM, count), jnp.float32),
            jax.ShapeDtypeStruct((1, count), jnp.float32),
            jax.ShapeDtypeStruct(q.shape, kind),
        ],
        in_specs=[ANY] * 3 + [WHOLE] * 2 + [ANY] * n,
        out_specs=[ANY] * (n + 3) + [WHOLE] * 2 + [ANY],
        scratch_shapes=[pltpu.VMEM(s, kind) for s in heads]
        + [pltpu.VMEM((HEAD_DIM, count), kind)]
        + Gather.semaphores(grid, pieces, n)
        + ToHeads.semaphores(own)
        + [dma((own.units,)), dma((HEADS, own.halves)), dma((own.halves,)), dma((3,))],
        compiler_params=pltpu.CompilerParams(
            collective_id=ident, has_side_effects=True, vmem_limit_bytes=VMEM_LIMIT
        ),
        cost_estimate=pl.CostEstimate(
            flops=pairs * 4 * HEAD_DIM, bytes_accessed=moved, transcendentals=pairs
        ),
    )(q, k, v, pos, begin, *arrays)
    return outs[:n], outs[n : n + 3], outs[n + 3 :]


class GradsBack:
    def __init__(self, own, sums, outs, give_from, given, held, sems):
        self.own, self.sums, self.outs = own, sums, outs
        self.give_from, self.given, self.held = give_from, given, held
        self.give_send, self.give_recv, self.send, self.recv, self.local = sems
        self.shares = own.total // own.members
        self.others = own.members - 1
        self.mine = lax.div(own.f, own.members) * own.seq + own.s

    @staticmethod
    def scratch(own, kind):
        shares, others = own.total // own.members, own.members - 1
        dma = pltpu.SemaphoreType.DMA
        blocks = (2, shares * others, HEAD_DIM, own.tokens)
        return [
            pltpu.VMEM(blocks, kind),
            pltpu.VMEM(blocks, kind),
            pltpu.VMEM((2, shares, HEAD_DIM, own.tokens), kind),
            dma((2, shares * others)),
            dma((2, shares * others)),
            dma((2, shares)),
            dma((2, HEADS)),
            dma((2,)),
        ]

    def block_of(self, order, member):
        f = member + self.own.members * lax.div(order, self.own.seq)
        return f * self.own.seq + lax.rem(order, self.own.seq)

    def given_at(self, i, slot):
        there = self.given.at[i, slot]
        remote(
            there, there, self.give_send.at[i, 0], self.give_recv.at[i, slot], self.own.of_block(0)
        ).wait_recv()
        return self.given[i, slot].astype(jnp.float32)

    def give(self, act):
        own = self.own

        def one(step, carry):
            order = lax.rem(self.mine + step, self.shares)
            for away in range(1, own.members):
                member = lax.rem(own.member + away, own.members)
                columns = lanes(self.block_of(order, member), own.tokens)
                out, back = order * self.others + away - 1, order * self.others + self.others - away
                for i in range(2):
                    if act == "start":
                        self.give_from[i, out] = self.sums[i][:, columns].astype(self.held.dtype)
                    copy = remote(
                        self.give_from.at[i, out],
                        self.given.at[i, back],
                        self.give_send.at[i, out],
                        self.give_recv.at[i, back],
                        own.of_head(own.head, member),
                    )
                    copy.start() if act == "start" else copy.wait_send()
            return carry

        lax.fori_loop(1, self.shares + 1, one, 0)

    def back(self, order, i, act):
        own = self.own
        block = self.block_of(order, own.member)
        there = self.outs[i].at[head_rows(own.head), :]

        @pl.when(block == own.block)
        def _():
            copy = pltpu.make_async_copy(self.held.at[i, order], there, self.local.at[i])
            copy.start() if act == "start" else copy.wait()

        @pl.when(block != own.block)
        def _():
            copy = remote(
                self.held.at[i, order],
                there,
                self.send.at[i, order],
                self.recv.at[i, own.head],
                own.of_block(block),
            )
            copy.start() if act == "start" else copy.wait_send()

    def add(self, step):
        order = lax.rem(self.mine + step, self.shares)
        columns = lanes(self.block_of(order, self.own.member), self.own.tokens)
        for i in range(2):
            total = self.sums[i][:, columns]
            for j in range(self.others):
                total = total + self.given_at(i, order * self.others + j)
            self.held[i, order] = total.astype(self.held.dtype)
            self.back(order, i, "start")

    def finish(self):
        def arrive(head, carry):
            @pl.when(head != self.own.head)
            def _():
                for i in range(2):
                    there = self.outs[i].at[head_rows(head), :]
                    remote(
                        there, there, self.send.at[i, 0], self.recv.at[i, head], self.own.of_block(0)
                    ).wait_recv()

            return carry

        lax.fori_loop(0, HEADS, arrive, 0)
        self.give("wait")

        def settle(order, carry):
            for i in range(2):
                self.back(order, i, "wait")
            return carry

        lax.fori_loop(0, self.shares, settle, 0)


def backward_kernel(tokens, pieces, n, n_tree, *refs):
    g_ref, q_ref, k_ref, v_ref, out_ref, lse_ref, pos_ref, begin_ref = refs[:8]
    parts = refs[8 : 8 + n]
    dq_out, dk_out, dv_out = refs[8 + n : 11 + n]
    sums = refs[11 + n : 11 + 2 * n]
    rest = refs[11 + 2 * n :]
    tree_scratch, rest = rest[:n_tree], rest[n_tree:]
    grads_ref, dq_ref, dk_sum, dv_sum = rest[:4]
    back_scratch, sems = rest[4:12], rest[12:]
    own = Owners(tokens)
    own.locate()
    tree = None
    if n:
        grid = Grid()
        grid.locate()
        tree = Reduce(grid, pieces, parts, sums, tree_scratch)
    grads_back = GradsBack(own, (dk_sum, dv_sum), (dk_out, dv_out), *back_scratch[:3], back_scratch[3:])
    g_send, g_recv, g_local, dq_send, dq_recv, dq_local = sems
    tiles = Tiles(own)

    own.barrier()
    spread_units(own, g_ref, grads_ref, g_send, g_recv, g_local, "start")
    if tree:
        tree.start()
    dk_sum[...] = jnp.zeros_like(dk_sum)
    dv_sum[...] = jnp.zeros_like(dv_sum)

    def advance(number):
        if tree:

            @pl.when(number < tree.places - 1)
            def _():
                tree.climb(number)

        return number + 1

    number = advance(jnp.int32(0))
    await_units(own, grads_ref, g_send, g_recv)
    spread_units(own, g_ref, grads_ref, g_send, g_recv, g_local, "wait")
    units = QUERIES // UNIT

    def one_group(group, number):
        here = group_lanes(group)
        queries, grads = q_ref[:, here], grads_ref[:, here]
        pos, begin, lse = pos_ref[:, here], begin_ref[:, here], lse_ref[:, here]
        delta = jnp.sum(grads.astype(jnp.float32) * out_ref[:, here], axis=0, keepdims=True)

        def body(tile, causal, current):
            number, dq = current
            number = advance(number)
            there = key_lanes(tile)
            keys = k_ref[:, there]
            scores = shown(first_dims(keys, queries), tile, causal, pos, begin)
            probs = jnp.exp(scores - lse)
            dv_sum[:, there] += last_dims(grads, probs.astype(jnp.bfloat16))
            dscores = (probs * (first_dims(v_ref[:, there], grads) - delta)).astype(jnp.bfloat16)
            dk_sum[:, there] += last_dims(queries, dscores)
            return number, dq + plain(keys, dscores)

        number, dq = tiles.fold(
            group, body, (number, jnp.zeros((HEAD_DIM, QUERIES), jnp.float32))
        )
        dq_ref[:, here] = (dq * HEAD_DIM**-0.5).astype(dq_ref.dtype)
        collect_units(
            own, dq_ref, dq_out, dq_send, dq_recv, dq_local, "start", group * units, units
        )
        return number

    number = lax.fori_loop(0, tiles.groups, one_group, number)
    grads_back.give("start")

    def add(step, number):
        grads_back.add(step)
        return number

    number = lax.fori_loop(1, grads_back.shares + 1, add, number)
    if tree:

        def last(number, carry):
            tree.climb(number)
            return carry

        lax.fori_loop(number, tree.places - 1, last, 0)
    await_heads(own, dq_out, dq_send, dq_recv)
    collect_units(own, dq_ref, dq_out, dq_send, dq_recv, dq_local, "wait", 0, own.units)
    grads_back.finish()
    if tree:
        tree.finish()


def backward(grads, q, k, v, out, lse, pos, begin, arrays, pieces, ident):
    tokens, kind = grads.shape[1], grads.dtype
    grid, own = Grid(), Owners(tokens)
    n = len(arrays)
    count = own.units * UNIT
    dma = pltpu.SemaphoreType.DMA
    tree_scratch = Reduce.scratch(grid, pieces, arrays) if n else []
    pairs = count * own.total * tokens // 3
    moved = sum(a.size * a.dtype.itemsize for a in arrays) + 6 * k.size
    unit_sems = [
        [dma((HEADS, own.halves)), dma((own.units,)), dma((own.halves,))],
        [dma((own.units,)), dma((HEADS, own.halves)), dma((own.halves,))],
    ]
    outs = pl.pallas_call(
        functools.partial(backward_kernel, tokens, pieces, n, len(tree_scratch)),
        out_shape=[jax.ShapeDtypeStruct(grads.shape, kind)] * 3 + summed_shapes(arrays),
        in_specs=[ANY] + [WHOLE] * 7 + [ANY] * n,
        out_specs=[ANY] * 3 + [WHOLE] * n,
        scratch_shapes=tree_scratch
        + [pltpu.VMEM((HEAD_DIM, count), kind)] * 2
        + [pltpu.VMEM(k.shape, jnp.float32)] * 2
        + GradsBack.scratch(own, kind)
        + unit_sems[0]
        + unit_sems[1],
        compiler_params=pltpu.CompilerParams(
            collective_id=ident, has_side_effects=True, vmem_limit_bytes=VMEM_LIMIT
        ),
        cost_estimate=pl.CostEstimate(
            flops=pairs * 10 * HEAD_DIM, bytes_accessed=moved, transcendentals=pairs
        ),
    )(grads, q, k, v, out, lse, pos, begin, *arrays)
    return outs[:3], outs[3:]


def publish_kernel(*refs):
    half = len(refs) // 2
    for source, target in zip(refs[:half], refs[half:]):
        target[...] = source[...]


def publish(arrays):
    return pl.pallas_call(
        publish_kernel,
        out_shape=[jax.ShapeDtypeStruct(a.shape, a.dtype) for a in arrays],
        in_specs=[WHOLE] * len(arrays),
        out_specs=[WHOLE] * len(arrays),
        compiler_params=pltpu.CompilerParams(vmem_limit_bytes=VMEM_LIMIT),
    )(*arrays)


def plan(columns, *pieces):
    found, used = [], [0] * len(columns)
    for array, part, order in pieces:
        count = columns[array] if part is None else part
        count = min(count, columns[array] - used[array])
        found.append((array, used[array], count, order))
        used[array] += count
    return found


def rms_scale(tensor):
    return lax.rsqrt(jnp.mean(tensor * tensor, axis=-1, keepdims=True) + EPSILON)


def angle_tables(offsets):
    half_dim = HEAD_DIM // 2
    frequency = jnp.power(10000.0, -jnp.arange(half_dim, dtype=jnp.float32) / half_dim)
    angles = frequency[:, None] * offsets.astype(jnp.float32)[None, :]
    return jnp.cos(angles)[None], jnp.sin(angles)[None]


def rotate(tensor, cosine, sine_tab):
    pairs = tensor.reshape(HEADS, 2, HEAD_DIM // 2, -1)
    front, back = pairs[:, 0], pairs[:, 1]
    turned = jnp.stack([front * cosine - back * sine_tab, back * cosine + front * sine_tab], axis=1)
    return turned.reshape(tensor.shape)


def matmul(left, right):
    return jnp.dot(left, right, preferred_element_type=jnp.float32)


def contract(left, right, left_dim, right_dim):
    return lax.dot_general(
        left, right, (((left_dim,), (right_dim,)), ((), ())), preferred_element_type=jnp.float32
    )


def per_device(
    layer_input,
    v_first,
    offsets,
    g_attn,
    w_query,
    w_key,
    w_value,
    w_out,
    g_ffn,
    w_gate,
    w_up,
    w_down,
    out_cot,
):
    low = jnp.bfloat16
    tokens = layer_input.shape[0]
    seq, fsdp = lax.axis_size("seq"), lax.axis_size("fsdp")
    devices = seq * fsdp
    seq_index = lax.axis_index("seq")
    own_offsets = lax.dynamic_slice_in_dim(offsets, seq_index * tokens, tokens, 0)

    share = g_attn.shape[0]
    neighbours = 128 // share
    turn = lax.rem(seq_index * fsdp + lax.axis_index("fsdp"), neighbours) * share
    gains = jnp.zeros((16, 128), low)
    gains = lax.dynamic_update_slice(gains, jnp.stack([g_attn, g_ffn]), (0, turn))
    places = jnp.zeros((8, 128), jnp.int32)
    places = lax.dynamic_update_slice(places, own_offsets.reshape(-1, 128), (0, 0))
    first = (w_query, w_key, w_value, gains, places)
    half = w_key.shape[1] // 2
    first_plan = plan(
        [shard.shape[1] for shard in first],
        (0, None, "A"), (1, half, "A"), (1, half, "B"), (2, None, "C"), (3, None, "C"), (4, None, "C"),
    )
    later = (w_gate, w_up, w_down, w_out)
    later_plan = plan(
        [shard.shape[1] for shard in later],
        (0, None, "A"), (1, None, "A"), (2, None, "C"), (3, half, "A"), (3, half, "B"),
    )
    *wholes, whole_gains, whole_places = gather_all(first, first_plan, 0)
    proj_query, proj_key, proj_value = (whole.reshape(-1, whole.shape[2]) for whole in wholes)
    whole_gains = whole_gains.reshape(-1, neighbours, 16, 128).astype(jnp.float32).sum(1)
    gain_attn, gain_ffn = whole_gains[:, 0].reshape(-1), whole_gains[:, 1].reshape(-1)
    all_offsets = (
        whole_places[:, : tokens // 128].reshape(seq, fsdp, tokens).transpose(1, 0, 2).reshape(-1)
    )

    own = Owners(tokens)
    member = lax.rem(lax.axis_index("fsdp"), own.members)
    unit_begins = (jnp.arange(devices * tokens, dtype=jnp.int32) - all_offsets).reshape(
        own.units, own.members, UNIT
    )
    begin = lax.dynamic_index_in_dim(unit_begins, member, 1, keepdims=False).reshape(1, -1)
    pos = (
        (jnp.arange(own.units, dtype=jnp.int32)[:, None] * own.members + member) * UNIT
        + jnp.arange(UNIT, dtype=jnp.int32)[None]
    ).reshape(1, -1)

    cosine, sine_tab = angle_tables(own_offsets)
    input_f32 = layer_input.astype(jnp.float32)
    norm_attn = rms_scale(input_f32)
    normed_a = (input_f32 * norm_attn * gain_attn).astype(low)
    scale = jnp.asarray(HEAD_DIM**-0.5, low)
    q_tokens = rotate(lax.optimization_barrier(contract(proj_query, normed_a, 0, 1)), cosine, sine_tab).astype(low) * scale
    k_tokens = rotate(lax.optimization_barrier(contract(proj_key, normed_a, 0, 1)), cosine, sine_tab).astype(low)
    mixed = (
        0.5 * contract(proj_value, normed_a, 0, 1) + 0.5 * v_first.astype(jnp.float32).T
    ).astype(low)
    wholes, heads, (attended, lse, attn_tokens) = forward(
        q_tokens, k_tokens, mixed, pos, begin, later, later_plan, 1
    )
    proj_gate, proj_up, proj_down, proj_out = (whole.reshape(-1, whole.shape[2]) for whole in wholes)

    after_attn = input_f32 + contract(attn_tokens, proj_out, 0, 0)
    norm_ffn = rms_scale(after_attn)
    normed_f = (after_attn * norm_ffn * gain_ffn).astype(low)
    gate_act = matmul(normed_f, proj_gate)
    up_act = matmul(normed_f, proj_up)
    sigmoid_gate = jax.nn.sigmoid(gate_act)
    silu_gate = gate_act * sigmoid_gate
    hidden = (silu_gate * up_act).astype(low)
    result = (after_attn + matmul(hidden, proj_down)).astype(low)

    grad_down = contract(hidden, out_cot, 0, 0)
    grad_hidden = contract(out_cot, proj_down, 1, 1)
    grad_gate_low = (
        grad_hidden * up_act * sigmoid_gate * (1.0 + gate_act * (1.0 - sigmoid_gate))
    ).astype(low)
    grad_up_low = (grad_hidden * silu_gate).astype(low)
    grad_gate_w = contract(normed_f, grad_gate_low, 0, 0)
    grad_up_w = contract(normed_f, grad_up_low, 0, 0)
    grad_normed_f = contract(grad_gate_low, proj_gate, 1, 1) + contract(grad_up_low, proj_up, 1, 1)
    grad_gain_ffn = jnp.sum(grad_normed_f * after_attn * norm_ffn, axis=0)
    scaled_ffn = grad_normed_f * gain_ffn
    grad_after = (
        out_cot.astype(jnp.float32)
        + norm_ffn * scaled_ffn
        - after_attn * norm_ffn**3 * jnp.mean(scaled_ffn * after_attn, axis=-1, keepdims=True)
    )
    grad_attn_low = grad_after.astype(low)
    grad_out_w = contract(attn_tokens, grad_attn_low, 1, 0)
    grad_attended = contract(proj_out, grad_attn_low, 1, 1).astype(low)

    def terms(*grads):
        return [grad.astype(low).reshape(devices, -1, grad.shape[1]) for grad in grads]

    later_terms = terms(grad_gate_w, grad_up_w, grad_down, grad_out_w)
    early = devices <= 32
    (dq_rot, dk_rot, grad_mixed), later_sums = backward(
        grad_attended, *heads, attended, lse, pos, begin,
        later_terms if early else [], later_plan if early else [], 2,
    )
    grad_q = rotate(dq_rot.astype(jnp.float32), cosine, -sine_tab).astype(low)
    grad_k = rotate(dk_rot.astype(jnp.float32), cosine, -sine_tab).astype(low)
    grad_v = grad_mixed * jnp.asarray(0.5, low)
    grad_first = grad_v.T.astype(jnp.float32)
    grad_query_w = contract(normed_a, grad_q, 0, 1)
    grad_key_w = contract(normed_a, grad_k, 0, 1)
    grad_value_w = contract(normed_a, grad_v, 0, 1)
    grad_normed_a = (
        contract(grad_q, proj_query, 0, 1)
        + contract(grad_k, proj_key, 0, 1)
        + contract(grad_v, proj_value, 0, 1)
    )
    grad_gain_attn = jnp.sum(grad_normed_a * input_f32 * norm_attn, axis=0)
    scaled_attn = grad_normed_a * gain_attn
    grad_layer = (
        grad_after
        + norm_attn * scaled_attn
        - input_f32 * norm_attn**3 * jnp.mean(scaled_attn * input_f32, axis=-1, keepdims=True)
    )

    gain_terms = jnp.pad(jnp.stack([grad_gain_attn, grad_gain_ffn]), ((0, 6), (0, 0)))
    gain_terms = jnp.repeat(gain_terms.reshape(8, -1, 128).transpose(1, 0, 2), neighbours, axis=0)
    first_terms = [*terms(grad_query_w, grad_key_w, grad_value_w), gain_terms]
    if early:
        first_sums = reduce_all(first_terms, first_plan[:-1], 3)
    else:
        every = plan(
            [term.shape[2] for term in first_terms + later_terms],
            (0, None, "A"), (1, None, "B"), (2, None, "C"), (3, None, "C"),
            (4, None, "A"), (5, None, "A"), (6, None, "C"), (7, None, "C"),
        )
        all_sums = reduce_all(first_terms + later_terms, every, 3)
        first_sums, later_sums = all_sums[:4], all_sums[4:]
    *sums, sum_gains = publish([*first_sums[:3], *later_sums, first_sums[3]])
    sum_query, sum_key, sum_value, sum_gate, sum_up, sum_down, sum_out = sums
    sum_gains = lax.dynamic_slice_in_dim(sum_gains, turn, share, 1)
    return (
        result,
        grad_layer,
        grad_first,
        sum_gains[0],
        sum_query,
        sum_key,
        sum_value,
        sum_out,
        sum_gains[1],
        sum_gate,
        sum_up,
        sum_down,
    )


def solution(mesh):
    return jax.shard_map(
        per_device,
        mesh=mesh,
        in_specs=(
            P(("fsdp", "seq"), None),
            P(("fsdp", "seq"), None),
            P("fsdp"),
            P(("seq", "fsdp")),
            P(("seq", "fsdp"), None),
            P(("seq", "fsdp"), None),
            P(("seq", "fsdp"), None),
            P(("seq", "fsdp"), None),
            P(("seq", "fsdp")),
            P(("seq", "fsdp"), None),
            P(("seq", "fsdp"), None),
            P(("seq", "fsdp"), None),
            P(("fsdp", "seq"), None),
        ),
        out_specs=(
            P(("fsdp", "seq"), None),
            P(("fsdp", "seq"), None),
            P(("fsdp", "seq"), None),
            P(("seq", "fsdp")),
            P(("seq", "fsdp"), None),
            P(("seq", "fsdp"), None),
            P(("seq", "fsdp"), None),
            P(("seq", "fsdp"), None),
            P(("seq", "fsdp")),
            P(("seq", "fsdp"), None),
            P(("seq", "fsdp"), None),
            P(("seq", "fsdp"), None),
        ),
        check_vma=False,
    )
```

```python
import functools, math
import jax
import jax.numpy as jnp
from jax import lax
from jax.experimental import pallas as pl
from jax.experimental.pallas import tpu as pltpu
from jax.sharding import PartitionSpec as P

EPSILON = 1e-06
MESH = pl.DeviceIdType.MESH


class Grid:
    def __init__(self):
        self.seq = lax.axis_size("seq")
        self.fsdp = lax.axis_size("fsdp")
        self.size = {"z": self.seq, "y": 2, "x": self.fsdp // 4}
        self.stride = {"x": 2, "y": 2 * (self.fsdp // 4)}
        self.total = self.seq * self.fsdp
        self.plane = self.total // 2

    def locate(self):
        z, f = lax.axis_index("seq"), lax.axis_index("fsdp")
        nx = self.size["x"]
        self.f, self.zi = f, z
        self.core = lax.rem(f, 2)
        self.me = {"z": z, "y": lax.div(f, 2 * nx), "x": lax.rem(lax.div(f, 2), nx)}

    def step(self, dim, delta):
        if dim == "z":
            return {"seq": self.zi + delta}
        if dim == "core":
            return {"fsdp": self.f + 1 - 2 * self.core}
        return {"fsdp": self.f + delta * self.stride[dim]}

    def partner(self, dim):
        return self.step(dim, 1 - 2 * self.me[dim])

    def dirs(self, dim):
        return (0,) if self.size[dim] == 2 else (1, -1)

    def linear(self, at, core):
        nx = self.size["x"]
        return at["z"] * self.fsdp + (at["y"] * nx + at["x"]) * 2 + core

    def neighbours(self):
        found = [(None, self.step("core", 1))]
        for dim in ("z", "y", "x"):
            n = self.size[dim]
            if n == 1:
                continue
            if n == 2:
                found.append((None, self.partner(dim)))
            else:
                found.append((self.me[dim] < n - 1, self.step(dim, 1)))
                found.append((self.me[dim] > 0, self.step(dim, -1)))
        return found

    def barrier(self):
        sem = pltpu.get_barrier_semaphore()
        count = 0
        for exists, device in self.neighbours():
            if exists is None:
                pl.semaphore_signal(sem, inc=1, device_id=device, device_id_type=MESH)
                count = count + 1
            else:

                @pl.when(exists)
                def _(device=device):
                    pl.semaphore_signal(sem, inc=1, device_id=device, device_id_type=MESH)

                count = count + exists.astype(jnp.int32)
        pl.semaphore_wait(sem, count)

    def digits(self, order, number):
        at, ok = {}, None
        rest = number
        for dim in order:
            n = self.size[dim]
            base = 2 if n == 2 else 2 * n - 1
            digit = lax.rem(rest, base)
            rest = lax.div(rest, base)
            if n == 2:
                at[dim] = lax.rem(self.me[dim] + digit, 2)
            elif n == 1:
                at[dim] = self.me[dim]
            else:
                away = lax.div(digit + 1, 2)
                at[dim] = jnp.where(lax.rem(digit, 2) == 1, self.me[dim] - away, self.me[dim] + away)
                inside = (at[dim] >= 0) & (at[dim] < n)
                ok = inside if ok is None else ok & inside
        return at, ok

    def places(self, order):
        return math.prod(2 if self.size[d] == 2 else 2 * self.size[d] - 1 for d in order)

    def rank(self, order, at, upto):
        value, width = 0, 1
        for dim in order[:upto]:
            value = value + at[dim] * width
            width *= self.size[dim]
        return value

    def slots(self, order):
        first, count, width = [], 0, 1
        for dim in order:
            n = self.size[dim]
            first.append(count)
            count += width * {1: 0, 2: 1}.get(n, n + 1)
            width *= n
        return first, count

    def slot(self, order, j, w, at):
        first, _ = self.slots(order)
        dim = order[j]
        place = self.rank(order, at, j)
        if self.size[dim] == 2:
            return first[j] + place
        width = math.prod(self.size[d] for d in order[:j])
        return first[j] + place + width * (at[dim] + w)

    def branch(self, order, j, way, at):
        dim = order[j]
        n = self.size[dim]
        ok = None
        for later in order[j + 1 :]:
            same = at[later] == self.me[later]
            ok = same if ok is None else ok & same
        if n == 2:
            here = at[dim] == self.me[dim]
        elif way == 1:
            here = (at[dim] <= self.me[dim]) & (self.me[dim] < n - 1)
        else:
            here = (at[dim] >= self.me[dim]) & (self.me[dim] > 0)
        return here if ok is None else ok & here


ORDERS = {"A": ("z", "x", "y"), "B": ("x", "y", "z"), "C": ("y", "z", "x")}


class Gather:
    def __init__(self, grid, pieces, sources, outs, sems):
        self.grid, self.pieces, self.sources, self.outs = grid, pieces, sources, outs
        self.recv, self.send, self.core_send, self.own_sem = sems
        self.base, slots = [], 0
        for piece in pieces:
            self.base.append(slots)
            slots += grid.slots(ORDERS[piece[3]])[1]
        self.places = grid.places(ORDERS["A"])

    @staticmethod
    def semaphores(grid, pieces, arrays):
        slots = sum(grid.slots(ORDERS[piece[3]])[1] for piece in pieces)
        dma = pltpu.SemaphoreType.DMA
        return [
            dma((len(pieces), grid.total)),
            dma((slots,)),
            dma((len(pieces), grid.plane)),
            dma((arrays,)),
        ]

    def own(self, i):
        mine = self.grid.linear(self.grid.me, self.grid.core)
        return pltpu.make_async_copy(self.sources[i], self.outs[i].at[mine], self.own_sem.at[i])

    def view(self, ref, p):
        return ref.at[:, pl.ds(self.pieces[p][1], self.pieces[p][2])]

    def sends(self, p, at, source, act):
        grid = self.grid
        order = ORDERS[self.pieces[p][3]]
        number = grid.linear(at, grid.core)
        target = self.view(self.outs[self.pieces[p][0]].at[number], p)

        def copy(sem, device):
            return pltpu.make_async_remote_copy(
                src_ref=source,
                dst_ref=target,
                send_sem=sem,
                recv_sem=self.recv.at[p, number],
                device_id=device,
                device_id_type=MESH,
            )

        for j, dim in enumerate(order):
            if grid.size[dim] == 1:
                continue
            ways = grid.dirs(dim)
            for w, way in enumerate(ways):
                slot = grid.slot(order, j, w, at)
                device = grid.partner(dim) if way == 0 else grid.step(dim, way)

                @pl.when(grid.branch(order, j, way, at))
                def _(device=device, slot=slot):
                    act(copy(self.send.at[self.base[p] + slot], device))

        act(copy(self.core_send.at[p, grid.rank(order, at, 3)], grid.step("core", 1)))

    def arrive(self, p, number):
        there = self.view(self.outs[self.pieces[p][0]].at[number], p)
        pltpu.make_async_remote_copy(
            src_ref=there,
            dst_ref=there,
            send_sem=self.core_send.at[p, 0],
            recv_sem=self.recv.at[p, number],
            device_id=self.grid.step("core", 1),
            device_id_type=MESH,
        ).wait_recv()

    def each(self, number, act):
        for p in range(len(self.pieces)):
            at, ok = self.grid.digits(ORDERS[self.pieces[p][3]], number)

            def run(p=p, at=at):
                act(p, at)

            if ok is None:
                run()
            else:
                pl.when(ok)(run)

    def start(self):
        for i in range(len(self.sources)):
            self.own(i).start()
        for p in range(len(self.pieces)):
            self.sends(
                p, self.grid.me, self.view(self.sources[self.pieces[p][0]], p), lambda c: c.start()
            )

    def relay(self, number):
        def act(p, at):
            where = self.grid.linear(at, self.grid.core)
            self.arrive(p, where)
            self.sends(p, at, self.view(self.outs[self.pieces[p][0]].at[where], p), lambda c: c.start())

        self.each(number, act)

    def finish(self):
        def act(p, at):
            self.arrive(p, self.grid.linear(at, 1 - self.grid.core))
            where = self.grid.linear(at, self.grid.core)
            self.sends(
                p, at, self.view(self.outs[self.pieces[p][0]].at[where], p), lambda c: c.wait_send()
            )

        def one(number, carry):
            self.each(number, act)
            return carry

        lax.fori_loop(0, self.places, one, 0)
        for i in range(len(self.sources)):
            self.own(i).wait()


def gather_kernel(pieces, n_arrays, *refs):
    grid = Grid()
    grid.locate()
    tree = Gather(grid, pieces, refs[:n_arrays], refs[n_arrays : 2 * n_arrays], refs[2 * n_arrays :])
    grid.barrier()
    tree.start()

    def forward(number, carry):
        tree.relay(number)
        return carry

    lax.fori_loop(1, tree.places, forward, 0)
    tree.finish()


def gathered_shapes(grid, arrays):
    return [jax.ShapeDtypeStruct((grid.total, *a.shape), a.dtype) for a in arrays]


def gather_all(arrays, pieces, ident):
    grid = Grid()
    n = len(arrays)
    moved = sum(a.size * a.dtype.itemsize for a in arrays) * grid.total
    return pl.pallas_call(
        functools.partial(gather_kernel, pieces, n),
        out_shape=gathered_shapes(grid, arrays),
        in_specs=[pl.BlockSpec(memory_space=pl.ANY)] * n,
        out_specs=[pl.BlockSpec(memory_space=pl.ANY)] * n,
        scratch_shapes=Gather.semaphores(grid, pieces, n),
        compiler_params=pltpu.CompilerParams(collective_id=ident, has_side_effects=True),
        cost_estimate=pl.CostEstimate(flops=0, bytes_accessed=moved, transcendentals=0),
    )(*arrays)


class Reduce:
    def __init__(self, grid, pieces, parts, outs, scratch):
        n = len(pieces)
        self.grid, self.pieces, self.parts, self.outs = grid, pieces, parts, outs
        self.pair, self.slot, self.held = (scratch[i * n : (i + 1) * n] for i in range(3))
        sems = scratch[3 * n :]
        self.core_send, self.core_recv, self.tree_send, self.tree_recv, self.own_sem = sems
        self.places = grid.places(ORDERS["A"])

    @staticmethod
    def scratch(grid, pieces, arrays):
        most = max(grid.slots(order)[1] for order in ORDERS.values())
        shape = [(arrays[p[0]].shape[1], p[2]) for p in pieces]
        kind = [arrays[p[0]].dtype for p in pieces]
        count = [grid.slots(ORDERS[p[3]])[1] for p in pieces]
        dma = pltpu.SemaphoreType.DMA
        n = len(pieces)
        return (
            [pltpu.VMEM((grid.plane, *s), k) for s, k in zip(shape, kind)]
            + [pltpu.VMEM((c, *s), k) for c, s, k in zip(count, shape, kind)]
            + [pltpu.VMEM((2, *s), k) for s, k in zip(shape, kind)]
            + [dma((n, grid.plane)), dma((n, grid.plane)), dma((n, grid.plane)), dma((n, most)), dma((n, 2))]
        )

    def each(self, number, act):
        for p in range(len(self.pieces)):
            at, ok = self.grid.digits(ORDERS[self.pieces[p][3]], number)

            def run(p=p, at=at):
                act(p, at)

            if ok is None:
                run()
            else:
                pl.when(ok)(run)

    def block(self, p, at, core):
        array, lower, count, _ = self.pieces[p]
        return self.parts[array].at[self.grid.linear(at, core), :, pl.ds(lower, count)]

    def rank(self, p, at):
        return self.grid.rank(ORDERS[self.pieces[p][3]], at, 3)

    def to_sibling(self, p, at):
        rank = self.rank(p, at)
        return pltpu.make_async_remote_copy(
            src_ref=self.block(p, at, 1 - self.grid.core),
            dst_ref=self.pair[p].at[rank],
            send_sem=self.core_send.at[p, rank],
            recv_sem=self.core_recv.at[p, rank],
            device_id=self.grid.step("core", 1),
            device_id_type=MESH,
        )

    def fetch(self, p, at, number):
        slot = lax.rem(number, 2)
        return pltpu.make_async_copy(
            self.block(p, at, self.grid.core), self.held[p].at[slot], self.own_sem.at[p, slot]
        )

    def to_parent(self, p, at, act):
        grid = self.grid
        order = ORDERS[self.pieces[p][3]]
        rank = self.rank(p, at)
        for j, dim in enumerate(order):
            if grid.size[dim] == 1:
                continue
            ways = grid.dirs(dim)
            ok = None
            for later in order[j + 1 :]:
                same = at[later] == grid.me[later]
                ok = same if ok is None else ok & same
            for w, way in enumerate(ways):
                slot = grid.slot(order, j, w, at)
                if way == 0:
                    here, device = at[dim] != grid.me[dim], grid.partner(dim)
                elif way == 1:
                    here, device = at[dim] < grid.me[dim], grid.step(dim, -1)
                else:
                    here, device = at[dim] > grid.me[dim], grid.step(dim, 1)
                here = here if ok is None else ok & here

                @pl.when(here)
                def _(slot=slot, device=device):
                    act(
                        pltpu.make_async_remote_copy(
                            src_ref=self.pair[p].at[rank],
                            dst_ref=self.slot[p].at[slot],
                            send_sem=self.tree_send.at[p, rank],
                            recv_sem=self.tree_recv.at[p, slot],
                            device_id=device,
                            device_id_type=MESH,
                        )
                    )

    def add(self, p, at, number, children, out):
        held, pair, slots = self.held[p], self.pair[p], self.slot[p]
        slot, rank = lax.rem(number, 2), self.rank(p, at)
        rows, columns = held.shape[1:]
        width = max(
            w for w in range(128, columns + 1, 128) if columns % w == 0 and (w == 128 or rows * w <= 49152)
        )
        array, lower, _, _ = self.pieces[p]

        def one(step, carry):
            first = pl.multiple_of(step * width, 128)
            here = pl.ds(first, width)
            total = held[slot, :, here].astype(jnp.float32) + pair[rank, :, here].astype(jnp.float32)
            for child in children:
                total = total + slots[child, :, here].astype(jnp.float32)
            if out:
                self.outs[array][:, pl.ds(lower + first, width)] = total
            else:
                pair[rank, :, here] = total.astype(pair.dtype)
            return carry

        lax.fori_loop(0, columns // width, one, 0)

    def combine(self, p, at, number):
        grid = self.grid
        order = ORDERS[self.pieces[p][3]]
        rank = self.rank(p, at)
        self.to_sibling(p, at).wait_recv()
        self.fetch(p, at, number).wait()

        def arrived(slot):
            there = self.slot[p].at[slot]
            pltpu.make_async_remote_copy(
                src_ref=there,
                dst_ref=there,
                send_sem=self.tree_send.at[p, rank],
                recv_sem=self.tree_recv.at[p, slot],
                device_id=grid.step("core", 1),
                device_id_type=MESH,
            ).wait_recv()
            return slot

        def level(j, children):
            if j < 0:
                self.add(p, at, number, children, True)
                return
            dim = order[j]
            n, me = grid.size[dim], grid.me[dim]
            if n == 1:
                level(j - 1, children)
                return
            same = at[dim] == me
            if n == 2:
                pl.when(jnp.logical_not(same))(lambda: self.add(p, at, number, children, False))
                pl.when(same)(lambda: level(j - 1, children + [arrived(grid.slot(order, j, 0, at))]))
                return
            up, down = me < n - 1, me > 0
            more = at[dim] > me
            behind = ((at[dim] < me) & up) | (more & down)

            @pl.when(jnp.logical_not(same) & behind)
            def _():
                w = jnp.where(more, 1, 0)
                self.add(p, at, number, children + [arrived(grid.slot(order, j, w, at))], False)

            pl.when(jnp.logical_not(same | behind))(lambda: self.add(p, at, number, children, False))

            def sides(*ways):
                level(j - 1, children + [arrived(grid.slot(order, j, w, at)) for w in ways])

            pl.when(same & up & down)(lambda: sides(0, 1))
            pl.when(same & up & jnp.logical_not(down))(lambda: sides(0))
            pl.when(same & jnp.logical_not(up) & down)(lambda: sides(1))

        level(2, [])

    def start(self):
        places = self.places

        def one(step, carry):
            self.each(places - 1 - step, lambda p, at: self.to_sibling(p, at).start())
            return carry

        self.each(places - 1, lambda p, at: self.fetch(p, at, places - 1).start())
        lax.fori_loop(0, places, one, 0)

    def climb(self, step):
        number = self.places - 1 - step
        self.each(number - 1, lambda p, at: self.fetch(p, at, number - 1).start())

        def work(p, at):
            self.combine(p, at, number)
            self.to_parent(p, at, lambda copy: copy.start())

        self.each(number, work)

    def finish(self):
        def root(p, at):
            self.combine(p, at, 0)

        self.each(0, root)

        def one(number, carry):
            def drain(p, at):
                self.to_sibling(p, at).wait_send()

                @pl.when(number > 0)
                def _():
                    self.to_parent(p, at, lambda copy: copy.wait_send())

            self.each(number, drain)
            return carry

        lax.fori_loop(0, self.places, one, 0)


def reduce_kernel(pieces, n_arrays, *refs):
    grid = Grid()
    grid.locate()
    tree = Reduce(grid, pieces, refs[:n_arrays], refs[n_arrays : 2 * n_arrays], refs[2 * n_arrays :])
    grid.barrier()
    tree.start()

    def climb(step, carry):
        tree.climb(step)
        return carry

    lax.fori_loop(0, tree.places - 1, climb, 0)
    tree.finish()


VMEM_LIMIT = 62 << 20


def summed_shapes(arrays):
    return [jax.ShapeDtypeStruct(a.shape[1:], jnp.float32) for a in arrays]


def reduce_all(arrays, pieces, ident):
    grid = Grid()
    n = len(arrays)
    moved = sum(a.size * a.dtype.itemsize for a in arrays)
    return pl.pallas_call(
        functools.partial(reduce_kernel, pieces, n),
        out_shape=summed_shapes(arrays),
        in_specs=[pl.BlockSpec(memory_space=pl.ANY)] * n,
        out_specs=[pl.BlockSpec(memory_space=pltpu.VMEM)] * n,
        scratch_shapes=Reduce.scratch(grid, pieces, arrays),
        compiler_params=pltpu.CompilerParams(
            collective_id=ident, has_side_effects=True, vmem_limit_bytes=VMEM_LIMIT
        ),
        cost_estimate=pl.CostEstimate(flops=0, bytes_accessed=2 * moved, transcendentals=0),
    )(*arrays)


HEADS = 16
HEAD_DIM = 64
UNIT = 128
NEGATIVE = -1e30


class Owners:
    def __init__(self, tokens):
        self.seq, self.fsdp = lax.axis_size("seq"), lax.axis_size("fsdp")
        self.total = self.seq * self.fsdp
        self.members = self.total // HEADS
        self.heads_here = HEADS // self.seq
        self.tokens = tokens
        self.halves = tokens // UNIT
        self.units = self.halves * self.total // self.members

    def locate(self):
        s, f = lax.axis_index("seq"), lax.axis_index("fsdp")
        self.s, self.f = s, f
        self.linear = s * self.fsdp + f
        self.block = f * self.seq + s
        self.head = s * self.heads_here + lax.div(f, self.members)
        self.member = lax.rem(f, self.members)

    def of_head(self, head, member):
        return {
            "seq": lax.div(head, self.heads_here),
            "fsdp": lax.rem(head, self.heads_here) * self.members + member,
        }

    def of_block(self, block):
        return {"seq": lax.rem(block, self.seq), "fsdp": lax.div(block, self.seq)}

    def barrier(self):
        sem = pltpu.get_barrier_semaphore()

        def greet(delta, carry):
            other = lax.rem(self.linear + delta, self.total)
            device = {"seq": lax.div(other, self.fsdp), "fsdp": lax.rem(other, self.fsdp)}
            pl.semaphore_signal(sem, inc=1, device_id=device, device_id_type=MESH)
            return carry

        lax.fori_loop(1, self.total, greet, 0)
        pl.semaphore_wait(sem, self.total - 1)


def remote(source, target, send_sem, recv_sem, device):
    return pltpu.make_async_remote_copy(
        src_ref=source,
        dst_ref=target,
        send_sem=send_sem,
        recv_sem=recv_sem,
        device_id=device,
        device_id_type=MESH,
    )


def head_rows(head):
    return pl.ds(pl.multiple_of(head * HEAD_DIM, HEAD_DIM), HEAD_DIM)


def lanes(number, width):
    return pl.ds(pl.multiple_of(number * width, width), width)


def spread_units(own, source, target, send, recv, local, act):
    def to_head(delta, carry):
        head = lax.rem(own.head + delta, HEADS)
        for half in range(own.halves):
            unit = own.halves * own.block + half
            member = lax.rem(unit, own.members)
            place = lax.div(unit, own.members)
            piece = source.at[head_rows(head), pl.ds(half * UNIT, UNIT)]
            there = target.at[:, lanes(place, UNIT)]
            here = (head == own.head) & (member == own.member)

            @pl.when(here)
            def _(piece=piece, there=there, half=half):
                copy = pltpu.make_async_copy(piece, there, local.at[half])
                copy.start() if act == "start" else copy.wait()

            @pl.when(jnp.logical_not(here))
            def _(piece=piece, there=there, half=half, member=member, place=place, head=head):
                copy = remote(
                    piece, there, send.at[head, half], recv.at[place], own.of_head(head, member)
                )
                copy.start() if act == "start" else copy.wait_send()

        return carry

    lax.fori_loop(0, HEADS, to_head, 0)


def await_units(own, target, send, recv):
    def one(place, carry):
        unit = place * own.members + own.member
        there = target.at[:, lanes(place, UNIT)]

        @pl.when(lax.div(unit, own.halves) != own.block)
        def _():
            remote(
                there, there, send.at[0, 0], recv.at[place], own.of_block(0)
            ).wait_recv()

        return carry

    lax.fori_loop(0, own.units, one, 0)


def collect_units(own, source, target, send, recv, local, act, first, count):
    def one(step, carry):
        place = first + step
        unit = place * own.members + own.member
        block, half = lax.div(unit, own.halves), lax.rem(unit, own.halves)
        piece = source.at[:, lanes(place, UNIT)]
        there = target.at[head_rows(own.head), lanes(half, UNIT)]

        @pl.when(block == own.block)
        def _():
            copy = pltpu.make_async_copy(piece, there, local.at[half])
            copy.start() if act == "start" else copy.wait()

        @pl.when(block != own.block)
        def _():
            copy = remote(
                piece, there, send.at[place], recv.at[own.head, half], own.of_block(block)
            )
            copy.start() if act == "start" else copy.wait_send()

        return carry

    lax.fori_loop(0, count, one, 0)


def await_heads(own, target, send, recv):
    def one(head, carry):
        for half in range(own.halves):
            unit = own.halves * own.block + half
            there = target.at[head_rows(head), pl.ds(half * UNIT, UNIT)]

            @pl.when((head != own.head) | (lax.rem(unit, own.members) != own.member))
            def _(there=there, half=half):
                remote(
                    there, there, send.at[0], recv.at[head, half], own.of_block(0)
                ).wait_recv()

        return carry

    lax.fori_loop(0, HEADS, one, 0)


QUERIES = 512
KEYS = 1024
BESIDE_PROJECT = 2
BESIDE_EXCHANGE = 3
BESIDE_TILES = 2
LATER_AT = 14
COLUMNS = 256
ANY = pl.BlockSpec(memory_space=pl.ANY)
WHOLE = pl.BlockSpec(memory_space=pltpu.VMEM)


def plain(left, right):
    return lax.dot_general(left, right, (((1,), (0,)), ((), ())), preferred_element_type=jnp.float32)


def first_dims(left, right):
    return lax.dot_general(left, right, (((0,), (0,)), ((), ())), preferred_element_type=jnp.float32)


def last_dims(left, right):
    return lax.dot_general(left, right, (((1,), (1,)), ((), ())), preferred_element_type=jnp.float32)


class Tiles:
    def __init__(self, own):
        self.span = QUERIES * own.members
        self.groups = own.units * UNIT // QUERIES
        self.longest = own.total * own.tokens // 2

    def fold(self, group, body, state):
        start = group * self.span
        low = lax.div(jnp.maximum(start - self.longest + 1, 0), KEYS)
        edge, high = lax.div(start, KEYS), lax.div(start + self.span + KEYS - 1, KEYS)
        state = lax.fori_loop(low, edge, lambda tile, s: body(tile, False, s), state)
        return lax.fori_loop(edge, high, lambda tile, s: body(tile, True, s), state)


def key_lanes(tile):
    return pl.ds(pl.multiple_of(tile * KEYS, KEYS), KEYS)


def group_lanes(group):
    return pl.ds(pl.multiple_of(group * QUERIES, QUERIES), QUERIES)


def shown(scores, tile, causal, pos, begin):
    number = tile * KEYS + lax.broadcasted_iota(jnp.int32, (KEYS, 1), 0)
    allowed = number >= begin
    if causal:
        allowed = allowed & (number <= pos)
    return jnp.where(allowed, scores, NEGATIVE)


def attend_group(tiles, group, q_ref, k_ref, v_ref, pos_ref, begin_ref, step, number):
    here = group_lanes(group)
    queries, pos, begin = q_ref[:, here], pos_ref[:, here], begin_ref[:, here]

    def body(tile, causal, current):
        number, top, total, summed = current
        number = now_and_then(tile, BESIDE_TILES, step, number)
        scores = shown(first_dims(k_ref[:, key_lanes(tile)], queries), tile, causal, pos, begin)
        new_top = jnp.maximum(top, jnp.max(scores, axis=0, keepdims=True))
        weights = jnp.exp(scores - new_top)
        shrink = jnp.exp(top - new_top)
        total = total * shrink + jnp.sum(weights, axis=0, keepdims=True)
        summed = summed * shrink + plain(v_ref[:, key_lanes(tile)], weights.astype(jnp.bfloat16))
        return number, new_top, total, summed

    number, top, total, summed = tiles.fold(
        group,
        body,
        (
            number,
            jnp.full((1, QUERIES), NEGATIVE, jnp.float32),
            jnp.zeros((1, QUERIES), jnp.float32),
            jnp.zeros((HEAD_DIM, QUERIES), jnp.float32),
        ),
    )
    return summed / total, top + jnp.log(total), number


class ToHeads:
    def __init__(self, own, sources, targets, sems):
        self.own = own
        self.q_ref, *pairs = sources
        self.q_out, *outs = targets
        self.pairs = tuple(zip(pairs, outs))
        self.q_send, self.q_recv, self.q_local, self.send, self.recv, self.local, self.hand_send = sems
        self.shares = own.total // own.members
        self.mine = lax.div(own.f, own.members) * own.seq + own.s

    @staticmethod
    def semaphores(own):
        dma = pltpu.SemaphoreType.DMA
        return [
            dma((HEADS, own.halves)),
            dma((own.units,)),
            dma((own.halves,)),
            dma((2, HEADS)),
            dma((2, own.total)),
            dma((2,)),
            dma((2, own.total // own.members * (own.members - 1))),
        ]

    def keys(self, i, act):
        own = self.own
        source, target = self.pairs[i]

        def to_head(delta, carry):
            head = lax.rem(own.head + delta, HEADS)
            piece = source.at[head_rows(head), :]
            there = target.at[:, lanes(own.block, own.tokens)]

            @pl.when(head == own.head)
            def _(piece=piece, there=there, i=i):
                copy = pltpu.make_async_copy(piece, there, self.local.at[i])
                copy.start() if act == "start" else copy.wait()

            @pl.when(head != own.head)
            def _(piece=piece, there=there, i=i):
                copy = remote(
                    piece,
                    there,
                    self.send.at[i, head],
                    self.recv.at[i, own.block],
                    own.of_head(head, own.member),
                )
                copy.start() if act == "start" else copy.wait_send()

            return carry

        lax.fori_loop(0, HEADS, to_head, 0)

    def hand(self, i, order, block, source, act):
        own = self.own
        for away in range(1, own.members):
            member = lax.rem(own.member + away, own.members)
            copy = remote(
                source,
                self.pairs[i][1].at[:, lanes(block, own.tokens)],
                self.hand_send.at[i, order * (own.members - 1) + away - 1],
                self.recv.at[i, block],
                own.of_head(own.head, member),
            )
            copy.start() if act == "start" else copy.wait_send()

    def hand_own(self, i, act):
        source = self.pairs[i][0].at[head_rows(self.own.head), :]
        self.hand(i, self.shares - 1, self.own.block, source, act)

    def block_of(self, step):
        order = lax.rem(self.mine + step, self.shares)
        f = self.own.member + self.own.members * lax.div(order, self.own.seq)
        return f * self.own.seq + lax.rem(order, self.own.seq)

    def arrive(self, i, block):
        there = self.pairs[i][1].at[:, lanes(block, self.own.tokens)]
        remote(
            there, there, self.send.at[i, 0], self.recv.at[i, block], self.own.of_block(0)
        ).wait_recv()
        return there

    def start_keys(self, i):
        self.keys(i, "start")
        self.hand_own(i, "start")

    def start_queries(self):
        spread_units(self.own, self.q_ref, self.q_out, self.q_send, self.q_recv, self.q_local, "start")

    def relay(self, step):
        block = self.block_of(step)
        for i in range(2):
            self.hand(i, step - 1, block, self.arrive(i, block), "start")

    def finish(self):
        own = self.own

        def rest(block, carry):
            @pl.when(lax.rem(lax.div(block, own.seq), own.members) != own.member)
            def _():
                for i in range(2):
                    self.arrive(i, block)

            return carry

        lax.fori_loop(0, own.total, rest, 0)
        await_units(own, self.q_out, self.q_send, self.q_recv)
        spread_units(own, self.q_ref, self.q_out, self.q_send, self.q_recv, self.q_local, "wait")
        for i in range(2):
            self.keys(i, "wait")
            self.hand_own(i, "wait")

        def settle(step, carry):
            block = self.block_of(step)
            for i, (_, target) in enumerate(self.pairs):
                self.hand(i, step - 1, block, target.at[:, lanes(block, own.tokens)], "wait")
            return carry

        lax.fori_loop(1, self.shares, settle, 0)


def now_and_then(index, every, act, number):
    return lax.cond(lax.rem(index, every) == 0, act, lambda x: x, number)


class Front:
    def __init__(self, grid, own, plan, sources, inputs, landed, tokens_of, outs, sems):
        self.grid, self.own = grid, own
        self.xn_ref, self.vf_ref, self.cos_ref, self.sin_ref, self.pos_ref = inputs
        self.landed, self.tokens_of = landed, tokens_of
        self.keep, (self.gain_ref, self.normed_ref, self.begin_ref) = outs[:3], outs[3:]
        self.keep_sem = sems[-1]
        self.tree = Gather(grid, plan, sources, landed, sems[:-1])

    def keeping(self, i):
        return pltpu.make_async_copy(self.landed[i], self.keep[i], self.keep_sem.at[i])

    def gather(self, between):
        def one(number, carry):
            self.tree.relay(number)
            between(number)
            return carry

        lax.fori_loop(1, self.tree.places, one, 0)
        self.tree.finish()
        for i in range(3):
            self.keeping(i).start()

    def prepare(self):
        gains, places = self.landed[3:]
        near = self.grid.total // 8
        rows = []
        for lane_block in range(8):
            rows.append(
                sum(
                    gains[lane_block * near + i, :8, :].astype(jnp.float32) for i in range(near)
                )
            )
        gain = jnp.concatenate(rows, axis=1)
        self.gain_ref[...] = gain
        self.normed_ref[...] = (self.xn_ref[...] * gain[:1]).astype(self.normed_ref.dtype)
        own = self.own

        def unit(place, carry):
            number = place * own.members + own.member
            block, half = lax.div(number, own.halves), lax.rem(number, own.halves)
            device = lax.rem(block, own.seq) * own.fsdp + lax.div(block, own.seq)
            here = lanes(place, UNIT)
            self.begin_ref[:, here] = self.pos_ref[:, here] - places[device, pl.ds(half, 1), :]
            return carry

        lax.fori_loop(0, own.units, unit, 0)

    def project(self, i, part):
        columns = pl.ds(pl.multiple_of(part * COLUMNS, COLUMNS), COLUMNS)
        weights = self.landed[i][:, :, columns].reshape(-1, COLUMNS)
        found = plain(self.normed_ref[...], weights).T
        target = self.tokens_of[i]
        if i == 2:
            mixed = 0.5 * found + 0.5 * self.vf_ref[columns, :].astype(jnp.float32)
            target[columns, :] = mixed.astype(target.dtype)
            return
        cosine, sine_tab = self.cos_ref[...], self.sin_ref[...]
        half, turned = HEAD_DIM // 2, []
        for first in range(0, COLUMNS, HEAD_DIM):
            front, back = found[first : first + half], found[first + half : first + HEAD_DIM]
            turned += [front * cosine - back * sine_tab, back * cosine + front * sine_tab]
        turned = jnp.concatenate(turned, axis=0).astype(target.dtype)
        target[columns, :] = turned * jnp.asarray(HEAD_DIM**-0.5, target.dtype) if i == 0 else turned


def forward_kernel(tokens, plans, counts, *refs):
    refs = list(refs)

    def take(count):
        taken = refs[:count]
        del refs[:count]
        return taken

    n_first, n = counts
    inputs, sources_first, sources = take(5), take(n_first), take(n)
    wholes, first_outs, keep = take(n), take(6), take(3)
    out_ref, lse_ref, back_ref = take(3)
    heads, (low_ref,) = take(3), take(1)
    landed, tokens_of = take(n_first), take(3)
    tree_sems, exchange_sems, (out_send, out_recv, out_local, keep_sem) = take(4), take(7), take(4)
    first_sems = take(5)
    grid, own = Grid(), Owners(tokens)
    grid.locate()
    own.locate()
    front = Front(
        grid, own, plans[0], sources_first, inputs, landed, tokens_of, first_outs, first_sems
    )
    tree = Gather(grid, plans[1], sources, wholes, tree_sems)
    exchange = ToHeads(own, tokens_of, heads, exchange_sems)
    tiles = Tiles(own)
    pos_ref, begin_ref = inputs[4], first_outs[5]

    own.barrier()
    front.tree.start()
    front.gather(lambda number: pl.when(number == LATER_AT)(tree.start))
    front.prepare()

    def advance(number):
        @pl.when(number < tree.places)
        def _():
            tree.relay(number)

        return number + 1

    number = jnp.int32(1)
    for i in (1, 2, 0):

        def part(index, number, i=i):
            front.project(i, index)
            return now_and_then(index, BESIDE_PROJECT, advance, number)

        number = lax.fori_loop(0, HEADS * HEAD_DIM // COLUMNS, part, number)
        if i:
            exchange.start_keys(i - 1)
        else:
            exchange.start_queries()

    def relay(step, number):
        exchange.relay(step)
        return now_and_then(step, BESIDE_EXCHANGE, advance, number)

    number = lax.fori_loop(1, exchange.shares, relay, number)
    exchange.finish()
    keeping = [pltpu.make_async_copy(heads[i], keep[i], keep_sem.at[i]) for i in range(3)]
    for copy in keeping:
        copy.start()
    units = QUERIES // UNIT

    def one_group(group, number):
        here = group_lanes(group)
        attended, lse, number = attend_group(
            tiles, group, *heads, pos_ref, begin_ref, advance, number
        )
        out_ref[:, here] = attended
        lse_ref[:, here] = lse
        low_ref[:, here] = attended.astype(low_ref.dtype)
        collect_units(
            own, low_ref, back_ref, out_send, out_recv, out_local, "start", group * units, units
        )
        return number

    number = lax.fori_loop(0, tiles.groups, one_group, number)

    def last(number, carry):
        tree.relay(number)
        return carry

    lax.fori_loop(number, tree.places, last, 0)
    await_heads(own, back_ref, out_send, out_recv)
    collect_units(own, low_ref, back_ref, out_send, out_recv, out_local, "wait", 0, own.units)
    tree.finish()
    for copy in keeping:
        copy.wait()
    for i in range(3):
        front.keeping(i).wait()


def forward(inputs, first, first_plan, later, later_plan, ident):
    tokens, features, kind = inputs[1].shape[1], inputs[1].shape[0], inputs[1].dtype
    grid, own = Grid(), Owners(tokens)
    n, n_first = len(later), len(first)
    count = own.units * UNIT
    dma = pltpu.SemaphoreType.DMA
    heads = [(HEAD_DIM, count)] + [(HEAD_DIM, own.total * tokens)] * 2
    pairs = count * own.total * tokens // 3
    moved = sum(a.size * a.dtype.itemsize for a in (*first, *later)) * grid.total
    landed = gathered_shapes(grid, first)
    outs = pl.pallas_call(
        functools.partial(forward_kernel, tokens, (first_plan, later_plan), (n_first, n)),
        out_shape=gathered_shapes(grid, later)
        + landed[:3]
        + [
            jax.ShapeDtypeStruct((8, features), jnp.float32),
            jax.ShapeDtypeStruct((tokens, features), kind),
            jax.ShapeDtypeStruct((1, count), jnp.int32),
        ]
        + [jax.ShapeDtypeStruct(s, kind) for s in heads]
        + [
            jax.ShapeDtypeStruct((HEAD_DIM, count), jnp.float32),
            jax.ShapeDtypeStruct((1, count), jnp.float32),
            jax.ShapeDtypeStruct((features, tokens), kind),
        ],
        in_specs=[WHOLE] * 5 + [ANY] * (n_first + n),
        out_specs=[ANY] * (n + 3) + [WHOLE] * 3 + [ANY] * 3 + [WHOLE] * 2 + [ANY],
        scratch_shapes=[pltpu.VMEM(s, kind) for s in heads]
        + [pltpu.VMEM((HEAD_DIM, count), kind)]
        + [pltpu.VMEM(a.shape, a.dtype) for a in landed]
        + [pltpu.VMEM((features, tokens), kind)] * 3
        + Gather.semaphores(grid, later_plan, n)
        + ToHeads.semaphores(own)
        + [dma((own.units,)), dma((HEADS, own.halves)), dma((own.halves,)), dma((3,))]
        + Gather.semaphores(grid, first_plan, n_first)
        + [dma((3,))],
        compiler_params=pltpu.CompilerParams(
            collective_id=ident, has_side_effects=True, vmem_limit_bytes=VMEM_LIMIT
        ),
        cost_estimate=pl.CostEstimate(
            flops=pairs * 4 * HEAD_DIM, bytes_accessed=moved, transcendentals=pairs
        ),
    )(*inputs, *first, *later)
    return outs[:n], outs[n : n + 3], outs[n + 3 : n + 6], outs[n + 6 : n + 9], outs[n + 9 :]


class GradsBack:
    def __init__(self, own, sums, outs, give_from, given, held, sems):
        self.own, self.sums, self.outs = own, sums, outs
        self.give_from, self.given, self.held = give_from, given, held
        self.give_send, self.give_recv, self.send, self.recv, self.local = sems
        self.others = own.members - 1

    @staticmethod
    def scratch(own, kind):
        shares, others = own.total // own.members, own.members - 1
        dma = pltpu.SemaphoreType.DMA
        blocks = (2, shares * others, HEAD_DIM, own.tokens)
        return [
            pltpu.VMEM(blocks, kind),
            pltpu.VMEM(blocks, kind),
            pltpu.VMEM((2, shares, HEAD_DIM, own.tokens), kind),
            dma((2, shares * others)),
            dma((2, shares * others)),
            dma((2, shares)),
            dma((2, HEADS)),
            dma((2,)),
        ]

    def split(self, block):
        f = lax.div(block, self.own.seq)
        order = lax.div(f, self.own.members) * self.own.seq + lax.rem(block, self.own.seq)
        return lax.rem(f, self.own.members), order

    def give(self, block, act):
        own = self.own
        member, order = self.split(block)
        away = lax.rem(member - own.member + own.members, own.members)

        @pl.when(away > 0)
        def _():
            columns = lanes(block, own.tokens)
            out = order * self.others + away - 1
            back = order * self.others + self.others - away
            for i in range(2):
                if act == "start":
                    self.give_from[i, out] = self.sums[i][:, columns].astype(self.held.dtype)
                copy = remote(
                    self.give_from.at[i, out],
                    self.given.at[i, back],
                    self.give_send.at[i, out],
                    self.give_recv.at[i, back],
                    own.of_head(own.head, member),
                )
                copy.start() if act == "start" else copy.wait_send()

    def back(self, block, order, i, act):
        own = self.own
        there = self.outs[i].at[head_rows(own.head), :]

        @pl.when(block == own.block)
        def _():
            copy = pltpu.make_async_copy(self.held.at[i, order], there, self.local.at[i])
            copy.start() if act == "start" else copy.wait()

        @pl.when(block != own.block)
        def _():
            copy = remote(
                self.held.at[i, order],
                there,
                self.send.at[i, order],
                self.recv.at[i, own.head],
                own.of_block(block),
            )
            copy.start() if act == "start" else copy.wait_send()

    def add(self, block):
        member, order = self.split(block)

        @pl.when(member == self.own.member)
        def _():
            columns = lanes(block, self.own.tokens)
            for i in range(2):
                total = self.sums[i][:, columns]
                for j in range(self.others):
                    slot = order * self.others + j
                    there = self.given.at[i, slot]
                    remote(
                        there,
                        there,
                        self.give_send.at[i, 0],
                        self.give_recv.at[i, slot],
                        self.own.of_block(0),
                    ).wait_recv()
                    total = total + self.given[i, slot].astype(jnp.float32)
                self.held[i, order] = total.astype(self.held.dtype)
                self.back(block, order, i, "start")

    def over(self, first, count, act):
        def one(step, carry):
            act(first + step)
            return carry

        lax.fori_loop(0, count, one, 0)

    def finish(self):
        def arrive(head, carry):
            @pl.when(head != self.own.head)
            def _():
                for i in range(2):
                    there = self.outs[i].at[head_rows(head), :]
                    remote(
                        there, there, self.send.at[i, 0], self.recv.at[i, head], self.own.of_block(0)
                    ).wait_recv()

            return carry

        lax.fori_loop(0, HEADS, arrive, 0)

        def settle(block):
            self.give(block, "wait")
            member, order = self.split(block)

            @pl.when(member == self.own.member)
            def _():
                for i in range(2):
                    self.back(block, order, i, "wait")

        self.over(0, self.own.total, settle)


class Tail:
    def __init__(self, grid, inputs, landed, outs, scratch):
        self.grid = grid
        self.normed_ref, self.xn_ref, self.cos_ref, self.sin_ref, self.ffn_ref = inputs[:5]
        self.weights = inputs[5:]
        self.landed = landed
        self.dh_ref, self.dv_ref = outs
        *self.terms, self.gain_terms, self.weight, self.turned, self.sem = scratch

    @staticmethod
    def scratch(grid, features, tokens, kind):
        rows = features // grid.total
        return (
            [pltpu.VMEM((grid.total, rows, features), kind)] * 3
            + [
                pltpu.VMEM((grid.total, 8, 128), jnp.float32),
                pltpu.VMEM((2, grid.total, rows, features), kind),
                pltpu.VMEM((tokens, features), kind),
                pltpu.SemaphoreType.DMA((2,)),
            ]
        )

    def load(self, step, i):
        return pltpu.make_async_copy(self.weights[i], self.weight.at[step % 2], self.sem.at[step % 2])

    def unrotate(self, i, part):
        columns = pl.ds(pl.multiple_of(part * COLUMNS, COLUMNS), COLUMNS)
        found = self.landed[i][columns, :].astype(jnp.float32)
        if i == 2:
            found = 0.5 * found
        else:
            cosine, sine_tab = self.cos_ref[...], self.sin_ref[...]
            half, turned = HEAD_DIM // 2, []
            for first in range(0, COLUMNS, HEAD_DIM):
                front, back = found[first : first + half], found[first + half : first + HEAD_DIM]
                turned += [front * cosine + back * sine_tab, back * cosine - front * sine_tab]
            found = jnp.concatenate(turned, axis=0)
        turned = found.T.astype(self.turned.dtype)
        self.turned[:, columns] = turned
        if i == 2:
            self.dv_ref[:, columns] = turned

    def project(self, i, step, part, first):
        columns = pl.ds(pl.multiple_of(part * COLUMNS, COLUMNS), COLUMNS)
        per = self.grid.total * COLUMNS // self.normed_ref.shape[1]
        blocks = pl.ds(part * per, per)
        terms = first_dims(self.normed_ref[:, columns], self.turned[...])
        self.terms[i][blocks] = terms.reshape(per, -1, terms.shape[1]).astype(self.terms[i].dtype)
        weights = self.weight[step % 2, blocks].reshape(COLUMNS, -1)
        term = last_dims(self.turned[...], weights)
        self.dh_ref[:, columns] = term if first else self.dh_ref[:, columns] + term

    def gains(self):
        attn = jnp.sum(self.dh_ref[...] * self.xn_ref[...], axis=0, keepdims=True)
        row = lax.broadcasted_iota(jnp.int32, (8, 1), 0)
        both = jnp.where(row == 0, attn, jnp.where(row == 1, self.ffn_ref[...], 0.0))
        near = self.grid.total // 8
        for block in range(8):
            for i in range(near):
                self.gain_terms[block * near + i] = both[:, block * 128 : (block + 1) * 128]


REDUCE_FIRST = 14
REDUCE_TILES = 3
REDUCE_TAIL = 1


def backward_kernel(tokens, plans, counts, *refs):
    refs = list(refs)

    def take(count):
        taken = refs[:count]
        del refs[:count]
        return taken

    n, n_tree, n_first = counts
    g_ref, q_ref, k_ref, v_ref, out_ref, lse_ref, pos_ref, begin_ref = take(8)
    tail_inputs = take(8) if n else None
    parts = take(n)
    outs = take(2 if n else 3)
    sums = take(n)
    first_sums = take(4 if n else 0)
    grads_ref, dq_ref, dk_sum, dv_sum = take(4)
    back_scratch = take(8)
    g_send, g_recv, g_local, dq_send, dq_recv, dq_local = take(6)
    own = Owners(tokens)
    own.locate()
    tree = None
    dq_out, dk_out, dv_out = landed = take(3) if n else outs
    if n:
        grid = Grid()
        grid.locate()
        tree = Reduce(grid, plans[0], parts, sums, take(n_tree))
        first_scratch = take(n_first)
        tail = Tail(grid, tail_inputs, landed, outs, refs)
        tree_first = Reduce(
            grid, plans[1], (*tail.terms, tail.gain_terms), first_sums, first_scratch
        )
    grads_back = GradsBack(own, (dk_sum, dv_sum), (dk_out, dv_out), *back_scratch[:3], back_scratch[3:])
    tiles = Tiles(own)

    own.barrier()
    spread_units(own, g_ref, grads_ref, g_send, g_recv, g_local, "start")
    if tree:
        tree.start()
    dk_sum[...] = jnp.zeros_like(dk_sum)
    dv_sum[...] = jnp.zeros_like(dv_sum)

    def advance(number):
        if tree:

            @pl.when(number < tree.places - 1)
            def _():
                tree.climb(number)

        return number + 1

    number = lax.fori_loop(0, REDUCE_FIRST, lambda step, number: advance(number), jnp.int32(0))
    await_units(own, grads_ref, g_send, g_recv)
    spread_units(own, g_ref, grads_ref, g_send, g_recv, g_local, "wait")
    units = QUERIES // UNIT
    blocks = tiles.span // tokens

    def one_group(step, number):
        group = tiles.groups - 1 - step
        here = group_lanes(group)
        queries, grads = q_ref[:, here], grads_ref[:, here]
        pos, begin, lse = pos_ref[:, here], begin_ref[:, here], lse_ref[:, here]
        delta = jnp.sum(grads.astype(jnp.float32) * out_ref[:, here], axis=0, keepdims=True)

        def body(tile, causal, current):
            number, dq = current
            number = now_and_then(tile, REDUCE_TILES, advance, number)
            there = key_lanes(tile)
            keys = k_ref[:, there]
            scores = shown(first_dims(keys, queries), tile, causal, pos, begin)
            probs = jnp.exp(scores - lse)
            dv_sum[:, there] += last_dims(grads, probs.astype(jnp.bfloat16))
            dscores = (probs * (first_dims(v_ref[:, there], grads) - delta)).astype(jnp.bfloat16)
            dk_sum[:, there] += last_dims(queries, dscores)
            return number, dq + plain(keys, dscores)

        number, dq = tiles.fold(
            group, body, (number, jnp.zeros((HEAD_DIM, QUERIES), jnp.float32))
        )
        dq_ref[:, here] = (dq * HEAD_DIM**-0.5).astype(dq_ref.dtype)
        collect_units(
            own, dq_ref, dq_out, dq_send, dq_recv, dq_local, "start", group * units, units
        )
        grads_back.over(group * blocks, blocks, lambda block: grads_back.give(block, "start"))

        @pl.when(step > 0)
        def _():
            grads_back.over((group + 1) * blocks, blocks, grads_back.add)

        return number

    number = lax.fori_loop(0, tiles.groups, one_group, number)
    grads_back.over(0, blocks, grads_back.add)
    await_heads(own, dq_out, dq_send, dq_recv)
    collect_units(own, dq_ref, dq_out, dq_send, dq_recv, dq_local, "wait", 0, own.units)
    grads_back.finish()
    if not tree:
        return

    parts_of = HEADS * HEAD_DIM // COLUMNS
    order = (0, 1, 2)
    tail.load(0, order[0]).start()
    for step, i in enumerate(order):
        tail.load(step, i).wait()
        if step < 2:
            tail.load(step + 1, order[step + 1]).start()

        def turn(part, number, i=i):
            tail.unrotate(i, part)
            return now_and_then(part, REDUCE_TAIL, advance, number)

        def project(part, number, i=i, step=step):
            tail.project(i, step, part, step == 0)
            return now_and_then(part, REDUCE_TAIL, advance, number)

        number = lax.fori_loop(0, parts_of, turn, number)
        number = lax.fori_loop(0, parts_of, project, number)
    tail.gains()
    tree_first.start()

    def climb(step, number):
        tree_first.climb(step)
        return advance(number)

    number = lax.fori_loop(0, tree_first.places - 1, climb, number)

    def last(number, carry):
        tree.climb(number)
        return carry

    lax.fori_loop(number, tree.places - 1, last, 0)
    tree_first.finish()
    tree.finish()


def backward(grads, q, k, v, out, lse, pos, begin, ident, tail=(), arrays=(), plans=((), ())):
    tokens, features, kind = grads.shape[1], grads.shape[0], grads.dtype
    grid, own = Grid(), Owners(tokens)
    n = len(arrays)
    count = own.units * UNIT
    dma = pltpu.SemaphoreType.DMA
    pairs = count * own.total * tokens // 3
    moved = sum(a.size * a.dtype.itemsize for a in arrays) + 6 * k.size
    back = jax.ShapeDtypeStruct(grads.shape, kind)
    scratch = (
        [pltpu.VMEM((HEAD_DIM, count), kind)] * 2
        + [pltpu.VMEM(k.shape, jnp.float32)] * 2
        + GradsBack.scratch(own, kind)
        + [dma((HEADS, own.halves)), dma((own.units,)), dma((own.halves,))]
        + [dma((own.units,)), dma((HEADS, own.halves)), dma((own.halves,))]
    )
    tree_scratch = first_scratch = []
    if n:
        tail_scratch = Tail.scratch(grid, features, tokens, kind)
        first = [jax.ShapeDtypeStruct((grid.total, features // grid.total, features), kind)] * 3
        first.append(jax.ShapeDtypeStruct((grid.total, 8, 128), jnp.float32))
        tree_scratch = Reduce.scratch(grid, plans[0], arrays)
        first_scratch = Reduce.scratch(grid, plans[1], first)
        scratch += [pltpu.VMEM(grads.shape, kind)] * 3 + tree_scratch + first_scratch + tail_scratch
        out_shape = [
            jax.ShapeDtypeStruct((tokens, features), jnp.float32),
            jax.ShapeDtypeStruct((tokens, features), kind),
        ]
        out_shape += summed_shapes(arrays) + summed_shapes(first)
        out_specs = [WHOLE] * len(out_shape)
        in_specs = [ANY] + [WHOLE] * 12 + [ANY] * (3 + n)
    else:
        out_shape, out_specs = [back] * 3, [ANY] * 3
        in_specs = [ANY] + [WHOLE] * 7
    outs = pl.pallas_call(
        functools.partial(
            backward_kernel, tokens, plans, (n, len(tree_scratch), len(first_scratch))
        ),
        out_shape=out_shape,
        in_specs=in_specs,
        out_specs=out_specs,
        scratch_shapes=scratch,
        compiler_params=pltpu.CompilerParams(
            collective_id=ident, has_side_effects=True, vmem_limit_bytes=VMEM_LIMIT
        ),
        cost_estimate=pl.CostEstimate(
            flops=pairs * 10 * HEAD_DIM, bytes_accessed=moved, transcendentals=pairs
        ),
    )(grads, q, k, v, out, lse, pos, begin, *tail, *arrays)
    return (outs[:2], outs[2 : 2 + n], outs[2 + n :]) if n else outs


def publish_kernel(*refs):
    half = len(refs) // 2
    for source, target in zip(refs[:half], refs[half:]):
        target[...] = source[...]


def publish(arrays):
    return pl.pallas_call(
        publish_kernel,
        out_shape=[jax.ShapeDtypeStruct(a.shape, a.dtype) for a in arrays],
        in_specs=[WHOLE] * len(arrays),
        out_specs=[WHOLE] * len(arrays),
        compiler_params=pltpu.CompilerParams(vmem_limit_bytes=VMEM_LIMIT),
    )(*arrays)


def plan(columns, *pieces):
    found, used = [], [0] * len(columns)
    for array, part, order in pieces:
        left = columns[array] - used[array]
        if not left:
            continue
        count = left if part is None else min(part, left)
        found.append((array, used[array], count, order))
        used[array] += count
    return found


def rms_scale(tensor):
    return lax.rsqrt(jnp.mean(tensor * tensor, axis=-1, keepdims=True) + EPSILON)


def angle_tables(offsets):
    half_dim = HEAD_DIM // 2
    frequency = jnp.power(10000.0, -jnp.arange(half_dim, dtype=jnp.float32) / half_dim)
    angles = frequency[:, None] * offsets.astype(jnp.float32)[None, :]
    return jnp.cos(angles)[None], jnp.sin(angles)[None]


def rotate(tensor, cosine, sine_tab):
    pairs = tensor.reshape(HEADS, 2, HEAD_DIM // 2, -1)
    front, back = pairs[:, 0], pairs[:, 1]
    turned = jnp.stack([front * cosine - back * sine_tab, back * cosine + front * sine_tab], axis=1)
    return turned.reshape(tensor.shape)


def matmul(left, right):
    return jnp.dot(left, right, preferred_element_type=jnp.float32)


def contract(left, right, left_dim, right_dim):
    return lax.dot_general(
        left, right, (((left_dim,), (right_dim,)), ((), ())), preferred_element_type=jnp.float32
    )


def per_device(
    layer_input,
    v_first,
    offsets,
    g_attn,
    w_query,
    w_key,
    w_value,
    w_out,
    g_ffn,
    w_gate,
    w_up,
    w_down,
    out_cot,
):
    low = jnp.bfloat16
    tokens = layer_input.shape[0]
    seq, fsdp = lax.axis_size("seq"), lax.axis_size("fsdp")
    devices = seq * fsdp
    seq_index = lax.axis_index("seq")
    own_offsets = lax.dynamic_slice_in_dim(offsets, seq_index * tokens, tokens, 0)

    share = g_attn.shape[0]
    neighbours = 128 // share
    turn = lax.rem(seq_index * fsdp + lax.axis_index("fsdp"), neighbours) * share
    gains = jnp.zeros((16, 128), low)
    gains = lax.dynamic_update_slice(gains, jnp.stack([g_attn, g_ffn]), (0, turn))
    places = jnp.zeros((8, 128), jnp.int32)
    places = lax.dynamic_update_slice(places, own_offsets.reshape(-1, 128), (0, 0))
    first = (w_query, w_key, w_value, gains, places)
    half = w_key.shape[1] // 2 if devices <= 32 else None
    first_plan = plan(
        [shard.shape[1] for shard in first],
        (0, None, "A"), (1, half, "A"), (1, half, "B"), (2, None, "C"), (3, None, "C"), (4, None, "C"),
    )
    later = (w_gate, w_up, w_down, w_out)
    later_plan = plan(
        [shard.shape[1] for shard in later],
        (0, None, "A"), (1, None, "A"), (2, None, "C"), (3, half, "A"), (3, half, "B"),
    )

    own = Owners(tokens)
    member = lax.rem(lax.axis_index("fsdp"), own.members)
    pos = (
        (jnp.arange(own.units, dtype=jnp.int32)[:, None] * own.members + member) * UNIT
        + jnp.arange(UNIT, dtype=jnp.int32)[None]
    ).reshape(1, -1)
    cosine, sine_tab = angle_tables(own_offsets)
    input_f32 = layer_input.astype(jnp.float32)
    norm_attn = rms_scale(input_f32)
    normed_input = input_f32 * norm_attn
    wholes, first_wholes, front, heads, (attended, lse, attn_tokens) = forward(
        (normed_input, v_first.T, cosine[0], sine_tab[0], pos),
        first, first_plan, later, later_plan, 0,
    )
    gain_rows, normed_a, begin = front
    gain_attn, gain_ffn = gain_rows[0], gain_rows[1]
    proj_query, proj_key, proj_value = (whole.reshape(-1, whole.shape[2]) for whole in first_wholes)
    proj_gate, proj_up, proj_down, proj_out = (whole.reshape(-1, whole.shape[2]) for whole in wholes)

    after_attn = input_f32 + contract(attn_tokens, proj_out, 0, 0)
    norm_ffn = rms_scale(after_attn)
    normed_f = (after_attn * norm_ffn * gain_ffn).astype(low)
    gate_act = matmul(normed_f, proj_gate)
    up_act = matmul(normed_f, proj_up)
    sigmoid_gate = jax.nn.sigmoid(gate_act)
    silu_gate = gate_act * sigmoid_gate
    hidden = (silu_gate * up_act).astype(low)
    result = (after_attn + matmul(hidden, proj_down)).astype(low)

    grad_down = contract(hidden, out_cot, 0, 0)
    grad_hidden = contract(out_cot, proj_down, 1, 1)
    grad_gate_low = (
        grad_hidden * up_act * sigmoid_gate * (1.0 + gate_act * (1.0 - sigmoid_gate))
    ).astype(low)
    grad_up_low = (grad_hidden * silu_gate).astype(low)
    grad_gate_w = contract(normed_f, grad_gate_low, 0, 0)
    grad_up_w = contract(normed_f, grad_up_low, 0, 0)
    grad_normed_f = contract(grad_gate_low, proj_gate, 1, 1) + contract(grad_up_low, proj_up, 1, 1)
    grad_gain_ffn = jnp.sum(grad_normed_f * after_attn * norm_ffn, axis=0)
    scaled_ffn = grad_normed_f * gain_ffn
    grad_after = (
        out_cot.astype(jnp.float32)
        + norm_ffn * scaled_ffn
        - after_attn * norm_ffn**3 * jnp.mean(scaled_ffn * after_attn, axis=-1, keepdims=True)
    )
    grad_attn_low = grad_after.astype(low)
    grad_out_w = contract(attn_tokens, grad_attn_low, 1, 0)
    grad_attended = contract(proj_out, grad_attn_low, 1, 1).astype(low)

    def terms(*grads):
        return [grad.astype(low).reshape(devices, -1, grad.shape[1]) for grad in grads]

    later_terms = terms(grad_gate_w, grad_up_w, grad_down, grad_out_w)
    attention = (grad_attended, *heads, attended, lse, pos, begin)
    if devices <= 32:
        (grad_normed_a, grad_v), later_sums, first_sums = backward(
            *attention, 1,
            (
                normed_a, normed_input, cosine[0], sine_tab[0], grad_gain_ffn[None],
                *first_wholes,
            ),
            later_terms, (later_plan, first_plan[:-1]),
        )
        grad_first = grad_v.astype(jnp.float32)
    else:
        dq_rot, dk_rot, grad_mixed = backward(*attention, 1)
        grad_q = rotate(dq_rot.astype(jnp.float32), cosine, -sine_tab).astype(low)
        grad_k = rotate(dk_rot.astype(jnp.float32), cosine, -sine_tab).astype(low)
        grad_v = grad_mixed * jnp.asarray(0.5, low)
        grad_first = grad_v.T.astype(jnp.float32)
        grad_query_w = contract(normed_a, grad_q, 0, 1)
        grad_key_w = contract(normed_a, grad_k, 0, 1)
        grad_value_w = contract(normed_a, grad_v, 0, 1)
        grad_normed_a = (
            contract(grad_q, proj_query, 0, 1)
            + contract(grad_k, proj_key, 0, 1)
            + contract(grad_v, proj_value, 0, 1)
        )
        grad_gain_attn = jnp.sum(grad_normed_a * normed_input, axis=0)
        gain_terms = jnp.pad(jnp.stack([grad_gain_attn, grad_gain_ffn]), ((0, 6), (0, 0)))
        gain_terms = jnp.repeat(gain_terms.reshape(8, -1, 128).transpose(1, 0, 2), neighbours, axis=0)
        first_terms = [*terms(grad_query_w, grad_key_w, grad_value_w), gain_terms]
        every = plan(
            [term.shape[2] for term in first_terms + later_terms],
            (0, None, "A"), (1, None, "B"), (2, None, "C"), (3, None, "C"),
            (4, None, "A"), (5, None, "A"), (6, None, "C"), (7, None, "C"),
        )
        all_sums = reduce_all(first_terms + later_terms, every, 2)
        first_sums, later_sums = all_sums[:4], all_sums[4:]
    scaled_attn = grad_normed_a * gain_attn
    grad_layer = (
        grad_after
        + norm_attn * scaled_attn
        - input_f32 * norm_attn**3 * jnp.mean(scaled_attn * input_f32, axis=-1, keepdims=True)
    )

    *sums, sum_gains = publish([*first_sums[:3], *later_sums, first_sums[3]])
    sum_query, sum_key, sum_value, sum_gate, sum_up, sum_down, sum_out = sums
    sum_gains = lax.dynamic_slice_in_dim(sum_gains, turn, share, 1)
    return (
        result,
        grad_layer,
        grad_first,
        sum_gains[0],
        sum_query,
        sum_key,
        sum_value,
        sum_out,
        sum_gains[1],
        sum_gate,
        sum_up,
        sum_down,
    )


def solution(mesh):
    return jax.shard_map(
        per_device,
        mesh=mesh,
        in_specs=(
            P(("fsdp", "seq"), None),
            P(("fsdp", "seq"), None),
            P("fsdp"),
            P(("seq", "fsdp")),
            P(("seq", "fsdp"), None),
            P(("seq", "fsdp"), None),
            P(("seq", "fsdp"), None),
            P(("seq", "fsdp"), None),
            P(("seq", "fsdp")),
            P(("seq", "fsdp"), None),
            P(("seq", "fsdp"), None),
            P(("seq", "fsdp"), None),
            P(("fsdp", "seq"), None),
        ),
        out_specs=(
            P(("fsdp", "seq"), None),
            P(("fsdp", "seq"), None),
            P(("fsdp", "seq"), None),
            P(("seq", "fsdp")),
            P(("seq", "fsdp"), None),
            P(("seq", "fsdp"), None),
            P(("seq", "fsdp"), None),
            P(("seq", "fsdp"), None),
            P(("seq", "fsdp")),
            P(("seq", "fsdp"), None),
            P(("seq", "fsdp"), None),
            P(("seq", "fsdp"), None),
        ),
        check_vma=False,
    )
```

```python
import functools, math
import jax
import jax.numpy as jnp
from jax import lax
from jax.experimental import pallas as pl
from jax.experimental.pallas import tpu as pltpu
from jax.sharding import PartitionSpec as P

EPSILON = 1e-06
MESH = pl.DeviceIdType.MESH


class Grid:
    def __init__(self):
        self.seq = lax.axis_size("seq")
        self.fsdp = lax.axis_size("fsdp")
        self.size = {"z": self.seq, "y": 2, "x": self.fsdp // 4}
        self.stride = {"x": 2, "y": 2 * (self.fsdp // 4)}
        self.total = self.seq * self.fsdp
        self.plane = self.total // 2

    def locate(self):
        z, f = lax.axis_index("seq"), lax.axis_index("fsdp")
        nx = self.size["x"]
        self.f, self.zi = f, z
        self.core = lax.rem(f, 2)
        self.me = {"z": z, "y": lax.div(f, 2 * nx), "x": lax.rem(lax.div(f, 2), nx)}

    def step(self, dim, delta):
        if dim == "z":
            return {"seq": self.zi + delta}
        if dim == "core":
            return {"fsdp": self.f + 1 - 2 * self.core}
        return {"fsdp": self.f + delta * self.stride[dim]}

    def partner(self, dim):
        return self.step(dim, 1 - 2 * self.me[dim])

    def dirs(self, dim):
        return (0,) if self.size[dim] == 2 else (1, -1)

    def linear(self, at, core):
        nx = self.size["x"]
        return at["z"] * self.fsdp + (at["y"] * nx + at["x"]) * 2 + core

    def neighbours(self):
        found = [(None, self.step("core", 1))]
        for dim in ("z", "y", "x"):
            n = self.size[dim]
            if n == 1:
                continue
            if n == 2:
                found.append((None, self.partner(dim)))
            else:
                found.append((self.me[dim] < n - 1, self.step(dim, 1)))
                found.append((self.me[dim] > 0, self.step(dim, -1)))
        return found

    def barrier(self):
        sem = pltpu.get_barrier_semaphore()
        count = 0
        for exists, device in self.neighbours():
            if exists is None:
                pl.semaphore_signal(sem, inc=1, device_id=device, device_id_type=MESH)
                count = count + 1
            else:

                @pl.when(exists)
                def _(device=device):
                    pl.semaphore_signal(sem, inc=1, device_id=device, device_id_type=MESH)

                count = count + exists.astype(jnp.int32)
        pl.semaphore_wait(sem, count)

    def digits(self, order, number):
        at, rest = {}, number
        for dim in order:
            n, me = self.size[dim], self.me[dim]
            digit = lax.rem(rest, n)
            rest = lax.div(rest, n)
            if n == 2:
                at[dim] = lax.rem(me + digit, 2)
                continue
            both = jnp.minimum(me, n - 1 - me)
            away = lax.div(digit + 1, 2)
            side = jnp.where(lax.rem(digit, 2) == 1, me - away, me + away)
            far = jnp.where(me > both, me - (digit - both), me + (digit - both))
            at[dim] = jnp.where(digit <= 2 * both, side, far)
        return at

    def spaced_digits(self, order, number):
        at, ok = {}, None
        rest = number
        for dim in order:
            n = self.size[dim]
            base = 2 if n == 2 else 2 * n - 1
            digit = lax.rem(rest, base)
            rest = lax.div(rest, base)
            if n == 2:
                at[dim] = lax.rem(self.me[dim] + digit, 2)
            elif n == 1:
                at[dim] = self.me[dim]
            else:
                away = lax.div(digit + 1, 2)
                at[dim] = jnp.where(lax.rem(digit, 2) == 1, self.me[dim] - away, self.me[dim] + away)
                inside = (at[dim] >= 0) & (at[dim] < n)
                ok = inside if ok is None else ok & inside
        return at, ok

    def spaced_places(self):
        return math.prod(2 if n == 2 else 2 * n - 1 for n in self.size.values())

    def rank(self, order, at, upto):
        value, width = 0, 1
        for dim in order[:upto]:
            value = value + at[dim] * width
            width *= self.size[dim]
        return value

    def slots(self, order):
        first, count, width = [], 0, 1
        for dim in order:
            n = self.size[dim]
            first.append(count)
            count += width * {1: 0, 2: 1}.get(n, n + 1)
            width *= n
        return first, count

    def slot(self, order, j, w, at):
        first, _ = self.slots(order)
        dim = order[j]
        place = self.rank(order, at, j)
        if self.size[dim] == 2:
            return first[j] + place
        width = math.prod(self.size[d] for d in order[:j])
        return first[j] + place + width * (at[dim] + w)

    def branch(self, order, j, way, at):
        dim = order[j]
        n = self.size[dim]
        ok = None
        for later in order[j + 1 :]:
            same = at[later] == self.me[later]
            ok = same if ok is None else ok & same
        if n == 2:
            here = at[dim] == self.me[dim]
        elif way == 1:
            here = (at[dim] <= self.me[dim]) & (self.me[dim] < n - 1)
        else:
            here = (at[dim] >= self.me[dim]) & (self.me[dim] > 0)
        return here if ok is None else ok & here


ORDERS = {"A": ("z", "x", "y"), "B": ("x", "y", "z"), "C": ("y", "z", "x")}


class Gather:
    def __init__(self, grid, pieces, sources, outs, sems):
        self.grid, self.pieces, self.sources, self.outs = grid, pieces, sources, outs
        self.recv, self.send, self.core_send, self.own_sem = sems
        self.base, slots = [], 0
        for piece in pieces:
            self.base.append(slots)
            slots += grid.slots(ORDERS[piece[3]])[1]
        self.places = grid.plane

    @staticmethod
    def semaphores(grid, pieces, arrays):
        slots = sum(grid.slots(ORDERS[piece[3]])[1] for piece in pieces)
        dma = pltpu.SemaphoreType.DMA
        return [
            dma((len(pieces), grid.total)),
            dma((slots,)),
            dma((len(pieces), grid.plane)),
            dma((arrays,)),
        ]

    def own(self, i):
        mine = self.grid.linear(self.grid.me, self.grid.core)
        return pltpu.make_async_copy(self.sources[i], self.outs[i].at[mine], self.own_sem.at[i])

    def view(self, ref, p):
        return ref.at[:, pl.ds(self.pieces[p][1], self.pieces[p][2])]

    def sends(self, p, at, source, act):
        grid = self.grid
        order = ORDERS[self.pieces[p][3]]
        number = grid.linear(at, grid.core)
        target = self.view(self.outs[self.pieces[p][0]].at[number], p)

        def copy(sem, device):
            return pltpu.make_async_remote_copy(
                src_ref=source,
                dst_ref=target,
                send_sem=sem,
                recv_sem=self.recv.at[p, number],
                device_id=device,
                device_id_type=MESH,
            )

        for j, dim in enumerate(order):
            if grid.size[dim] == 1:
                continue
            ways = grid.dirs(dim)
            for w, way in enumerate(ways):
                slot = grid.slot(order, j, w, at)
                device = grid.partner(dim) if way == 0 else grid.step(dim, way)

                @pl.when(grid.branch(order, j, way, at))
                def _(device=device, slot=slot):
                    act(copy(self.send.at[self.base[p] + slot], device))

        act(copy(self.core_send.at[p, grid.rank(order, at, 3)], grid.step("core", 1)))

    def arrive(self, p, number):
        there = self.view(self.outs[self.pieces[p][0]].at[number], p)
        pltpu.make_async_remote_copy(
            src_ref=there,
            dst_ref=there,
            send_sem=self.core_send.at[p, 0],
            recv_sem=self.recv.at[p, number],
            device_id=self.grid.step("core", 1),
            device_id_type=MESH,
        ).wait_recv()

    def each(self, number, act):
        used = sorted({piece[3] for piece in self.pieces})
        at = {order: self.grid.digits(ORDERS[order], number) for order in used}
        for p, piece in enumerate(self.pieces):
            act(p, at[piece[3]])

    def start(self):
        for i in range(len(self.sources)):
            self.own(i).start()
        for p in range(len(self.pieces)):
            self.sends(
                p, self.grid.me, self.view(self.sources[self.pieces[p][0]], p), lambda c: c.start()
            )

    def relay(self, number):
        def act(p, at):
            where = self.grid.linear(at, self.grid.core)
            self.arrive(p, where)
            self.sends(p, at, self.view(self.outs[self.pieces[p][0]].at[where], p), lambda c: c.start())

        self.each(number, act)

    def finish(self):
        def act(p, at):
            self.arrive(p, self.grid.linear(at, 1 - self.grid.core))
            where = self.grid.linear(at, self.grid.core)
            self.sends(
                p, at, self.view(self.outs[self.pieces[p][0]].at[where], p), lambda c: c.wait_send()
            )

        def one(number, carry):
            self.each(number, act)
            return carry

        lax.fori_loop(0, self.places, one, 0)
        for i in range(len(self.sources)):
            self.own(i).wait()


def gather_kernel(pieces, n_arrays, *refs):
    grid = Grid()
    grid.locate()
    tree = Gather(grid, pieces, refs[:n_arrays], refs[n_arrays : 2 * n_arrays], refs[2 * n_arrays :])
    grid.barrier()
    tree.start()

    def forward(number, carry):
        tree.relay(number)
        return carry

    lax.fori_loop(1, tree.places, forward, 0)
    tree.finish()


def gathered_shapes(grid, arrays):
    return [jax.ShapeDtypeStruct((grid.total, *a.shape), a.dtype) for a in arrays]


def gather_all(arrays, pieces, ident):
    grid = Grid()
    n = len(arrays)
    moved = sum(a.size * a.dtype.itemsize for a in arrays) * grid.total
    return pl.pallas_call(
        functools.partial(gather_kernel, pieces, n),
        out_shape=gathered_shapes(grid, arrays),
        in_specs=[pl.BlockSpec(memory_space=pl.ANY)] * n,
        out_specs=[pl.BlockSpec(memory_space=pl.ANY)] * n,
        scratch_shapes=Gather.semaphores(grid, pieces, n),
        compiler_params=pltpu.CompilerParams(collective_id=ident, has_side_effects=True),
        cost_estimate=pl.CostEstimate(flops=0, bytes_accessed=moved, transcendentals=0),
    )(*arrays)


class Reduce:
    def __init__(self, grid, pieces, parts, outs, scratch):
        n = len(pieces)
        self.grid, self.pieces, self.parts, self.outs = grid, pieces, parts, outs
        self.pair, self.slot, self.held = (scratch[i * n : (i + 1) * n] for i in range(3))
        sems = scratch[3 * n :]
        self.core_send, self.core_recv, self.tree_send, self.tree_recv, self.own_sem = sems
        self.places = grid.spaced_places()

    @staticmethod
    def scratch(grid, pieces, arrays):
        most = max(grid.slots(order)[1] for order in ORDERS.values())
        shape = [(arrays[p[0]].shape[1], p[2]) for p in pieces]
        kind = [arrays[p[0]].dtype for p in pieces]
        count = [grid.slots(ORDERS[p[3]])[1] for p in pieces]
        dma = pltpu.SemaphoreType.DMA
        n = len(pieces)
        return (
            [pltpu.VMEM((grid.plane, *s), k) for s, k in zip(shape, kind)]
            + [pltpu.VMEM((c, *s), k) for c, s, k in zip(count, shape, kind)]
            + [pltpu.VMEM((2, *s), k) for s, k in zip(shape, kind)]
            + [dma((n, grid.plane)), dma((n, grid.plane)), dma((n, grid.plane)), dma((n, most)), dma((n, 2))]
        )

    def each(self, number, act):
        used = {piece[3] for piece in self.pieces}
        places = {order: self.grid.spaced_digits(ORDERS[order], number) for order in sorted(used)}
        for p, piece in enumerate(self.pieces):
            at, ok = places[piece[3]]

            def run(p=p, at=at):
                act(p, at)

            if ok is None:
                run()
            else:
                pl.when(ok)(run)

    def block(self, p, at, core):
        array, lower, count, _ = self.pieces[p]
        return self.parts[array].at[self.grid.linear(at, core), :, pl.ds(lower, count)]

    def rank(self, p, at):
        return self.grid.rank(ORDERS[self.pieces[p][3]], at, 3)

    def to_sibling(self, p, at):
        rank = self.rank(p, at)
        return pltpu.make_async_remote_copy(
            src_ref=self.block(p, at, 1 - self.grid.core),
            dst_ref=self.pair[p].at[rank],
            send_sem=self.core_send.at[p, rank],
            recv_sem=self.core_recv.at[p, rank],
            device_id=self.grid.step("core", 1),
            device_id_type=MESH,
        )

    def fetch(self, p, at, number):
        slot = lax.rem(number, 2)
        return pltpu.make_async_copy(
            self.block(p, at, self.grid.core), self.held[p].at[slot], self.own_sem.at[p, slot]
        )

    def to_parent(self, p, at, act):
        grid = self.grid
        order = ORDERS[self.pieces[p][3]]
        rank = self.rank(p, at)
        for j, dim in enumerate(order):
            if grid.size[dim] == 1:
                continue
            ways = grid.dirs(dim)
            ok = None
            for later in order[j + 1 :]:
                same = at[later] == grid.me[later]
                ok = same if ok is None else ok & same
            for w, way in enumerate(ways):
                slot = grid.slot(order, j, w, at)
                if way == 0:
                    here, device = at[dim] != grid.me[dim], grid.partner(dim)
                elif way == 1:
                    here, device = at[dim] < grid.me[dim], grid.step(dim, -1)
                else:
                    here, device = at[dim] > grid.me[dim], grid.step(dim, 1)
                here = here if ok is None else ok & here

                @pl.when(here)
                def _(slot=slot, device=device):
                    act(
                        pltpu.make_async_remote_copy(
                            src_ref=self.pair[p].at[rank],
                            dst_ref=self.slot[p].at[slot],
                            send_sem=self.tree_send.at[p, rank],
                            recv_sem=self.tree_recv.at[p, slot],
                            device_id=device,
                            device_id_type=MESH,
                        )
                    )

    def add(self, p, at, number, children, out):
        held, pair, slots = self.held[p], self.pair[p], self.slot[p]
        slot, rank = lax.rem(number, 2), self.rank(p, at)
        rows, columns = held.shape[1:]
        width = max(
            w for w in range(128, columns + 1, 128) if columns % w == 0 and (w == 128 or rows * w <= 49152)
        )
        array, lower, _, _ = self.pieces[p]

        def one(step, carry):
            first = pl.multiple_of(step * width, 128)
            here = pl.ds(first, width)
            total = held[slot, :, here].astype(jnp.float32) + pair[rank, :, here].astype(jnp.float32)
            for child in children:
                total = total + slots[child, :, here].astype(jnp.float32)
            if out:
                self.outs[array][:, pl.ds(lower + first, width)] = total
            else:
                pair[rank, :, here] = total.astype(pair.dtype)
            return carry

        lax.fori_loop(0, columns // width, one, 0)

    def combine(self, p, at, number):
        grid = self.grid
        order = ORDERS[self.pieces[p][3]]
        rank = self.rank(p, at)
        self.to_sibling(p, at).wait_recv()
        self.fetch(p, at, number).wait()

        def arrived(slot):
            there = self.slot[p].at[slot]
            pltpu.make_async_remote_copy(
                src_ref=there,
                dst_ref=there,
                send_sem=self.tree_send.at[p, rank],
                recv_sem=self.tree_recv.at[p, slot],
                device_id=grid.step("core", 1),
                device_id_type=MESH,
            ).wait_recv()
            return slot

        def level(j, children):
            if j < 0:
                self.add(p, at, number, children, True)
                return
            dim = order[j]
            n, me = grid.size[dim], grid.me[dim]
            if n == 1:
                level(j - 1, children)
                return
            same = at[dim] == me
            if n == 2:
                pl.when(jnp.logical_not(same))(lambda: self.add(p, at, number, children, False))
                pl.when(same)(lambda: level(j - 1, children + [arrived(grid.slot(order, j, 0, at))]))
                return
            up, down = me < n - 1, me > 0
            more = at[dim] > me
            behind = ((at[dim] < me) & up) | (more & down)

            @pl.when(jnp.logical_not(same) & behind)
            def _():
                w = jnp.where(more, 1, 0)
                self.add(p, at, number, children + [arrived(grid.slot(order, j, w, at))], False)

            pl.when(jnp.logical_not(same | behind))(lambda: self.add(p, at, number, children, False))

            def sides(*ways):
                level(j - 1, children + [arrived(grid.slot(order, j, w, at)) for w in ways])

            pl.when(same & up & down)(lambda: sides(0, 1))
            pl.when(same & up & jnp.logical_not(down))(lambda: sides(0))
            pl.when(same & jnp.logical_not(up) & down)(lambda: sides(1))

        level(2, [])

    def start(self):
        places = self.places

        def one(step, carry):
            self.each(places - 1 - step, lambda p, at: self.to_sibling(p, at).start())
            return carry

        self.each(places - 1, lambda p, at: self.fetch(p, at, places - 1).start())
        lax.fori_loop(0, places, one, 0)

    def climb(self, step):
        number = self.places - 1 - step
        self.each(number - 1, lambda p, at: self.fetch(p, at, number - 1).start())

        def work(p, at):
            self.combine(p, at, number)
            self.to_parent(p, at, lambda copy: copy.start())

        self.each(number, work)

    def finish(self):
        def root(p, at):
            self.combine(p, at, 0)

        self.each(0, root)

        def one(number, carry):
            def drain(p, at):
                self.to_sibling(p, at).wait_send()

                @pl.when(number > 0)
                def _():
                    self.to_parent(p, at, lambda copy: copy.wait_send())

            self.each(number, drain)
            return carry

        lax.fori_loop(0, self.places, one, 0)


def reduce_kernel(pieces, n_arrays, *refs):
    grid = Grid()
    grid.locate()
    tree = Reduce(grid, pieces, refs[:n_arrays], refs[n_arrays : 2 * n_arrays], refs[2 * n_arrays :])
    grid.barrier()
    tree.start()

    def climb(step, carry):
        tree.climb(step)
        return carry

    lax.fori_loop(0, tree.places - 1, climb, 0)
    tree.finish()


VMEM_LIMIT = 62 << 20


def summed_shapes(arrays):
    return [jax.ShapeDtypeStruct(a.shape[1:], jnp.float32) for a in arrays]


def reduce_all(arrays, pieces, ident):
    grid = Grid()
    n = len(arrays)
    moved = sum(a.size * a.dtype.itemsize for a in arrays)
    return pl.pallas_call(
        functools.partial(reduce_kernel, pieces, n),
        out_shape=summed_shapes(arrays),
        in_specs=[pl.BlockSpec(memory_space=pl.ANY)] * n,
        out_specs=[pl.BlockSpec(memory_space=pltpu.VMEM)] * n,
        scratch_shapes=Reduce.scratch(grid, pieces, arrays),
        compiler_params=pltpu.CompilerParams(
            collective_id=ident, has_side_effects=True, vmem_limit_bytes=VMEM_LIMIT
        ),
        cost_estimate=pl.CostEstimate(flops=0, bytes_accessed=2 * moved, transcendentals=0),
    )(*arrays)


HEADS = 16
HEAD_DIM = 64
UNIT = 128
NEGATIVE = -1e30


class Owners:
    def __init__(self, tokens):
        self.seq, self.fsdp = lax.axis_size("seq"), lax.axis_size("fsdp")
        self.total = self.seq * self.fsdp
        self.members = self.total // HEADS
        self.heads_here = HEADS // self.seq
        self.tokens = tokens
        self.halves = tokens // UNIT
        self.units = self.halves * self.total // self.members

    def locate(self):
        s, f = lax.axis_index("seq"), lax.axis_index("fsdp")
        self.s, self.f = s, f
        self.linear = s * self.fsdp + f
        self.block = f * self.seq + s
        self.head = s * self.heads_here + lax.div(f, self.members)
        self.member = lax.rem(f, self.members)

    def of_head(self, head, member):
        return {
            "seq": lax.div(head, self.heads_here),
            "fsdp": lax.rem(head, self.heads_here) * self.members + member,
        }

    def of_block(self, block):
        return {"seq": lax.rem(block, self.seq), "fsdp": lax.div(block, self.seq)}

    def barrier(self):
        sem = pltpu.get_barrier_semaphore()

        def greet(delta, carry):
            other = lax.rem(self.linear + delta, self.total)
            device = {"seq": lax.div(other, self.fsdp), "fsdp": lax.rem(other, self.fsdp)}
            pl.semaphore_signal(sem, inc=1, device_id=device, device_id_type=MESH)
            return carry

        lax.fori_loop(1, self.total, greet, 0)
        pl.semaphore_wait(sem, self.total - 1)


def remote(source, target, send_sem, recv_sem, device):
    return pltpu.make_async_remote_copy(
        src_ref=source,
        dst_ref=target,
        send_sem=send_sem,
        recv_sem=recv_sem,
        device_id=device,
        device_id_type=MESH,
    )


def head_rows(head):
    return pl.ds(pl.multiple_of(head * HEAD_DIM, HEAD_DIM), HEAD_DIM)


def lanes(number, width):
    return pl.ds(pl.multiple_of(number * width, width), width)


def spread_units(own, source, target, send, recv, local, act):
    def to_head(delta, carry):
        head = lax.rem(own.head + delta, HEADS)
        for half in range(own.halves):
            unit = own.halves * own.block + half
            member = lax.rem(unit, own.members)
            place = lax.div(unit, own.members)
            piece = source.at[head_rows(head), pl.ds(half * UNIT, UNIT)]
            there = target.at[:, lanes(place, UNIT)]
            here = (head == own.head) & (member == own.member)

            @pl.when(here)
            def _(piece=piece, there=there, half=half):
                copy = pltpu.make_async_copy(piece, there, local.at[half])
                copy.start() if act == "start" else copy.wait()

            @pl.when(jnp.logical_not(here))
            def _(piece=piece, there=there, half=half, member=member, place=place, head=head):
                copy = remote(
                    piece, there, send.at[head, half], recv.at[place], own.of_head(head, member)
                )
                copy.start() if act == "start" else copy.wait_send()

        return carry

    lax.fori_loop(0, HEADS, to_head, 0)


def await_units(own, target, send, recv):
    def one(place, carry):
        unit = place * own.members + own.member
        there = target.at[:, lanes(place, UNIT)]

        @pl.when(lax.div(unit, own.halves) != own.block)
        def _():
            remote(
                there, there, send.at[0, 0], recv.at[place], own.of_block(0)
            ).wait_recv()

        return carry

    lax.fori_loop(0, own.units, one, 0)


def collect_units(own, source, target, send, recv, local, act, first, count):
    def one(step, carry):
        place = first + step
        unit = place * own.members + own.member
        block, half = lax.div(unit, own.halves), lax.rem(unit, own.halves)
        piece = source.at[:, lanes(place, UNIT)]
        there = target.at[head_rows(own.head), lanes(half, UNIT)]

        @pl.when(block == own.block)
        def _():
            copy = pltpu.make_async_copy(piece, there, local.at[half])
            copy.start() if act == "start" else copy.wait()

        @pl.when(block != own.block)
        def _():
            copy = remote(
                piece, there, send.at[place], recv.at[own.head, half], own.of_block(block)
            )
            copy.start() if act == "start" else copy.wait_send()

        return carry

    lax.fori_loop(0, count, one, 0)


def await_heads(own, target, send, recv):
    def one(head, carry):
        for half in range(own.halves):
            unit = own.halves * own.block + half
            there = target.at[head_rows(head), pl.ds(half * UNIT, UNIT)]

            @pl.when((head != own.head) | (lax.rem(unit, own.members) != own.member))
            def _(there=there, half=half):
                remote(
                    there, there, send.at[0], recv.at[head, half], own.of_block(0)
                ).wait_recv()

        return carry

    lax.fori_loop(0, HEADS, one, 0)


QUERIES = 512
KEYS = 1024
BESIDE_PROJECT = 4
BESIDE_EXCHANGE = 5
BESIDE_TILES = 5
LATER_AT = 4
COLUMNS = 256
ANY = pl.BlockSpec(memory_space=pl.ANY)
WHOLE = pl.BlockSpec(memory_space=pltpu.VMEM)


def plain(left, right):
    return lax.dot_general(left, right, (((1,), (0,)), ((), ())), preferred_element_type=jnp.float32)


def first_dims(left, right):
    return lax.dot_general(left, right, (((0,), (0,)), ((), ())), preferred_element_type=jnp.float32)


def last_dims(left, right):
    return lax.dot_general(left, right, (((1,), (1,)), ((), ())), preferred_element_type=jnp.float32)


class Tiles:
    def __init__(self, own):
        self.span = QUERIES * own.members
        self.groups = own.units * UNIT // QUERIES
        self.longest = own.total * own.tokens // 2

    def fold(self, group, body, state):
        start = group * self.span
        low = lax.div(jnp.maximum(start - self.longest + 1, 0), KEYS)
        edge, high = lax.div(start, KEYS), lax.div(start + self.span + KEYS - 1, KEYS)
        state = lax.fori_loop(low, edge, lambda tile, s: body(tile, False, s), state)
        return lax.fori_loop(edge, high, lambda tile, s: body(tile, True, s), state)


def key_lanes(tile):
    return pl.ds(pl.multiple_of(tile * KEYS, KEYS), KEYS)


def group_lanes(group):
    return pl.ds(pl.multiple_of(group * QUERIES, QUERIES), QUERIES)


def shown(scores, tile, causal, pos, begin):
    number = tile * KEYS + lax.broadcasted_iota(jnp.int32, (KEYS, 1), 0)
    allowed = number >= begin
    if causal:
        allowed = allowed & (number <= pos)
    return jnp.where(allowed, scores, NEGATIVE)


def attend_group(tiles, group, q_ref, k_ref, v_ref, pos_ref, begin_ref, step, number):
    here = group_lanes(group)
    queries, pos, begin = q_ref[:, here], pos_ref[:, here], begin_ref[:, here]

    def body(tile, causal, current):
        number, top, total, summed = current
        number = now_and_then(tile, BESIDE_TILES, step, number)
        scores = shown(first_dims(k_ref[:, key_lanes(tile)], queries), tile, causal, pos, begin)
        new_top = jnp.maximum(top, jnp.max(scores, axis=0, keepdims=True))
        weights = jnp.exp(scores - new_top)
        shrink = jnp.exp(top - new_top)
        total = total * shrink + jnp.sum(weights, axis=0, keepdims=True)
        summed = summed * shrink + plain(v_ref[:, key_lanes(tile)], weights.astype(jnp.bfloat16))
        return number, new_top, total, summed

    number, top, total, summed = tiles.fold(
        group,
        body,
        (
            number,
            jnp.full((1, QUERIES), NEGATIVE, jnp.float32),
            jnp.zeros((1, QUERIES), jnp.float32),
            jnp.zeros((HEAD_DIM, QUERIES), jnp.float32),
        ),
    )
    return summed / total, top + jnp.log(total), number


class ToHeads:
    def __init__(self, own, sources, targets, sems):
        self.own = own
        self.q_ref, *pairs = sources
        self.q_out, *outs = targets
        self.pairs = tuple(zip(pairs, outs))
        self.q_send, self.q_recv, self.q_local, self.send, self.recv, self.local, self.hand_send = sems
        self.shares = own.total // own.members
        self.mine = lax.div(own.f, own.members) * own.seq + own.s

    @staticmethod
    def semaphores(own):
        dma = pltpu.SemaphoreType.DMA
        return [
            dma((HEADS, own.halves)),
            dma((own.units,)),
            dma((own.halves,)),
            dma((2, HEADS)),
            dma((2, own.total)),
            dma((2,)),
            dma((2, own.total // own.members * (own.members - 1))),
        ]

    def keys(self, i, act):
        own = self.own
        source, target = self.pairs[i]

        def to_head(delta, carry):
            head = lax.rem(own.head + delta, HEADS)
            piece = source.at[head_rows(head), :]
            there = target.at[:, lanes(own.block, own.tokens)]

            @pl.when(head == own.head)
            def _(piece=piece, there=there, i=i):
                copy = pltpu.make_async_copy(piece, there, self.local.at[i])
                copy.start() if act == "start" else copy.wait()

            @pl.when(head != own.head)
            def _(piece=piece, there=there, i=i):
                copy = remote(
                    piece,
                    there,
                    self.send.at[i, head],
                    self.recv.at[i, own.block],
                    own.of_head(head, own.member),
                )
                copy.start() if act == "start" else copy.wait_send()

            return carry

        lax.fori_loop(0, HEADS, to_head, 0)

    def hand(self, i, order, block, source, act):
        own = self.own
        for away in range(1, own.members):
            member = lax.rem(own.member + away, own.members)
            copy = remote(
                source,
                self.pairs[i][1].at[:, lanes(block, own.tokens)],
                self.hand_send.at[i, order * (own.members - 1) + away - 1],
                self.recv.at[i, block],
                own.of_head(own.head, member),
            )
            copy.start() if act == "start" else copy.wait_send()

    def hand_own(self, i, act):
        source = self.pairs[i][0].at[head_rows(self.own.head), :]
        self.hand(i, self.shares - 1, self.own.block, source, act)

    def block_of(self, step):
        order = lax.rem(self.mine + step, self.shares)
        f = self.own.member + self.own.members * lax.div(order, self.own.seq)
        return f * self.own.seq + lax.rem(order, self.own.seq)

    def arrive(self, i, block):
        there = self.pairs[i][1].at[:, lanes(block, self.own.tokens)]
        remote(
            there, there, self.send.at[i, 0], self.recv.at[i, block], self.own.of_block(0)
        ).wait_recv()
        return there

    def start_keys(self, i):
        self.keys(i, "start")
        self.hand_own(i, "start")

    def start_queries(self):
        spread_units(self.own, self.q_ref, self.q_out, self.q_send, self.q_recv, self.q_local, "start")

    def relay(self, step):
        block = self.block_of(step)
        for i in range(2):
            self.hand(i, step - 1, block, self.arrive(i, block), "start")

    def finish(self):
        own = self.own

        def rest(block, carry):
            @pl.when(lax.rem(lax.div(block, own.seq), own.members) != own.member)
            def _():
                for i in range(2):
                    self.arrive(i, block)

            return carry

        lax.fori_loop(0, own.total, rest, 0)
        await_units(own, self.q_out, self.q_send, self.q_recv)
        spread_units(own, self.q_ref, self.q_out, self.q_send, self.q_recv, self.q_local, "wait")
        for i in range(2):
            self.keys(i, "wait")
            self.hand_own(i, "wait")

        def settle(step, carry):
            block = self.block_of(step)
            for i, (_, target) in enumerate(self.pairs):
                self.hand(i, step - 1, block, target.at[:, lanes(block, own.tokens)], "wait")
            return carry

        lax.fori_loop(1, self.shares, settle, 0)


def now_and_then(index, every, act, number):
    return lax.cond(lax.rem(index, every) == 0, act, lambda x: x, number)


def rms_scale(tensor):
    return lax.rsqrt(jnp.mean(tensor * tensor, axis=-1, keepdims=True) + EPSILON)


class Front:
    def __init__(self, grid, own, plan, sources, inputs, landed, tokens_of, outs, sems):
        self.grid, self.own = grid, own
        self.x_ref, self.vf_ref, self.cos_ref, self.sin_ref, self.pos_ref = inputs
        self.landed, self.tokens_of = landed, tokens_of
        self.keep, (self.gain_ref, self.normed_ref, self.begin_ref, self.xn_ref) = outs[:3], outs[3:]
        self.keep_sem = sems[-1]
        self.tree = Gather(grid, plan, sources, landed, sems[:-1])

    def keeping(self, i):
        return pltpu.make_async_copy(self.landed[i], self.keep[i], self.keep_sem.at[i])

    def gather(self, between):
        def one(number, carry):
            self.tree.relay(number)
            between(number)
            return carry

        lax.fori_loop(1, self.tree.places, one, 0)
        self.tree.finish()
        for i in range(3):
            self.keeping(i).start()

    def norm(self):
        x = self.x_ref[...].astype(jnp.float32)
        self.xn_ref[...] = x * rms_scale(x)

    def prepare(self):
        gains, places = self.landed[3:]
        near = self.grid.total // 8
        rows = []
        for lane_block in range(8):
            rows.append(
                sum(
                    gains[lane_block * near + i, :8, :].astype(jnp.float32) for i in range(near)
                )
            )
        gain = jnp.concatenate(rows, axis=1)
        self.gain_ref[...] = gain
        self.normed_ref[...] = (self.xn_ref[...] * gain[:1]).astype(self.normed_ref.dtype)
        own = self.own

        def unit(place, carry):
            number = place * own.members + own.member
            block, half = lax.div(number, own.halves), lax.rem(number, own.halves)
            device = lax.rem(block, own.seq) * own.fsdp + lax.div(block, own.seq)
            here = lanes(place, UNIT)
            self.begin_ref[:, here] = self.pos_ref[:, here] - places[device, pl.ds(half, 1), :]
            return carry

        lax.fori_loop(0, own.units, unit, 0)

    def project(self, i, part):
        columns = pl.ds(pl.multiple_of(part * COLUMNS, COLUMNS), COLUMNS)
        weights = self.landed[i][:, :, columns].reshape(-1, COLUMNS)
        found = plain(self.normed_ref[...], weights)
        target = self.tokens_of[i]
        if i == 2:
            mixed = 0.5 * found + 0.5 * self.vf_ref[:, columns].astype(jnp.float32)
            target[columns, :] = mixed.T.astype(target.dtype)
            return
        found = found.T
        cosine, sine_tab = self.cos_ref[...], self.sin_ref[...]
        half, turned = HEAD_DIM // 2, []
        for first in range(0, COLUMNS, HEAD_DIM):
            front, back = found[first : first + half], found[first + half : first + HEAD_DIM]
            turned += [front * cosine - back * sine_tab, back * cosine + front * sine_tab]
        turned = jnp.concatenate(turned, axis=0).astype(target.dtype)
        target[columns, :] = turned * jnp.asarray(HEAD_DIM**-0.5, target.dtype) if i == 0 else turned


def forward_kernel(tokens, plans, counts, *refs):
    refs = list(refs)

    def take(count):
        taken = refs[:count]
        del refs[:count]
        return taken

    n_first, n = counts
    inputs, sources_first, sources = take(5), take(n_first), take(n)
    wholes, first_outs, keep = take(n), take(7), take(3)
    out_ref, lse_ref, back_ref = take(3)
    heads, (low_ref,) = take(3), take(1)
    landed, tokens_of = take(n_first), take(3)
    tree_sems, exchange_sems, (out_send, out_recv, out_local, keep_sem) = take(4), take(7), take(4)
    first_sems = take(5)
    grid, own = Grid(), Owners(tokens)
    grid.locate()
    own.locate()
    front = Front(
        grid, own, plans[0], sources_first, inputs, landed, tokens_of, first_outs, first_sems
    )
    tree = Gather(grid, plans[1], sources, wholes, tree_sems)
    exchange = ToHeads(own, tokens_of, heads, exchange_sems)
    tiles = Tiles(own)
    pos_ref, begin_ref = inputs[4], first_outs[5]

    own.barrier()
    front.tree.start()
    front.norm()
    front.gather(lambda number: pl.when(number == LATER_AT)(tree.start))
    front.prepare()

    def advance(number):
        @pl.when(number < tree.places)
        def _():
            tree.relay(number)

        return number + 1

    number = jnp.int32(1)
    for i in (1, 2, 0):

        def part(index, number, i=i):
            front.project(i, index)
            return now_and_then(index, BESIDE_PROJECT, advance, number)

        number = lax.fori_loop(0, HEADS * HEAD_DIM // COLUMNS, part, number)
        if i:
            exchange.start_keys(i - 1)
        else:
            exchange.start_queries()

    def relay(step, number):
        exchange.relay(step)
        return now_and_then(step, BESIDE_EXCHANGE, advance, number)

    number = lax.fori_loop(1, exchange.shares, relay, number)
    exchange.finish()
    keeping = [pltpu.make_async_copy(heads[i], keep[i], keep_sem.at[i]) for i in range(3)]
    for copy in keeping:
        copy.start()
    units = QUERIES // UNIT

    def one_group(group, number):
        here = group_lanes(group)
        attended, lse, number = attend_group(
            tiles, group, *heads, pos_ref, begin_ref, advance, number
        )
        out_ref[:, here] = attended
        lse_ref[:, here] = lse
        low_ref[:, here] = attended.astype(low_ref.dtype)
        collect_units(
            own, low_ref, back_ref, out_send, out_recv, out_local, "start", group * units, units
        )
        return number

    number = lax.fori_loop(0, tiles.groups, one_group, number)

    def last(number, carry):
        tree.relay(number)
        return carry

    lax.fori_loop(number, tree.places, last, 0)
    await_heads(own, back_ref, out_send, out_recv)
    collect_units(own, low_ref, back_ref, out_send, out_recv, out_local, "wait", 0, own.units)
    tree.finish()
    for copy in keeping:
        copy.wait()
    for i in range(3):
        front.keeping(i).wait()


def forward(inputs, first, first_plan, later, later_plan, ident):
    (tokens, features), kind = inputs[1].shape, inputs[1].dtype
    grid, own = Grid(), Owners(tokens)
    n, n_first = len(later), len(first)
    count = own.units * UNIT
    dma = pltpu.SemaphoreType.DMA
    heads = [(HEAD_DIM, count)] + [(HEAD_DIM, own.total * tokens)] * 2
    pairs = count * own.total * tokens // 3
    moved = sum(a.size * a.dtype.itemsize for a in (*first, *later)) * grid.total
    landed = gathered_shapes(grid, first)
    outs = pl.pallas_call(
        functools.partial(forward_kernel, tokens, (first_plan, later_plan), (n_first, n)),
        out_shape=gathered_shapes(grid, later)
        + landed[:3]
        + [
            jax.ShapeDtypeStruct((8, features), jnp.float32),
            jax.ShapeDtypeStruct((tokens, features), kind),
            jax.ShapeDtypeStruct((1, count), jnp.int32),
            jax.ShapeDtypeStruct((tokens, features), jnp.float32),
        ]
        + [jax.ShapeDtypeStruct(s, kind) for s in heads]
        + [
            jax.ShapeDtypeStruct((HEAD_DIM, count), jnp.float32),
            jax.ShapeDtypeStruct((1, count), jnp.float32),
            jax.ShapeDtypeStruct((features, tokens), kind),
        ],
        in_specs=[WHOLE] * 5 + [ANY] * (n_first + n),
        out_specs=[ANY] * (n + 3) + [WHOLE] * 4 + [ANY] * 3 + [WHOLE] * 2 + [ANY],
        scratch_shapes=[pltpu.VMEM(s, kind) for s in heads]
        + [pltpu.VMEM((HEAD_DIM, count), kind)]
        + [pltpu.VMEM(a.shape, a.dtype) for a in landed]
        + [pltpu.VMEM((features, tokens), kind)] * 3
        + Gather.semaphores(grid, later_plan, n)
        + ToHeads.semaphores(own)
        + [dma((own.units,)), dma((HEADS, own.halves)), dma((own.halves,)), dma((3,))]
        + Gather.semaphores(grid, first_plan, n_first)
        + [dma((3,))],
        compiler_params=pltpu.CompilerParams(
            collective_id=ident, has_side_effects=True, vmem_limit_bytes=VMEM_LIMIT
        ),
        cost_estimate=pl.CostEstimate(
            flops=pairs * 4 * HEAD_DIM, bytes_accessed=moved, transcendentals=pairs
        ),
    )(*inputs, *first, *later)
    return outs[:n], outs[n : n + 3], outs[n + 3 : n + 7], outs[n + 7 : n + 10], outs[n + 10 :]


class GradsBack:
    def __init__(self, own, sums, outs, give_from, given, held, sems):
        self.own, self.sums, self.outs = own, sums, outs
        self.give_from, self.given, self.held = give_from, given, held
        self.give_send, self.give_recv, self.send, self.recv, self.local = sems
        self.others = own.members - 1

    @staticmethod
    def scratch(own, kind):
        shares, others = own.total // own.members, own.members - 1
        dma = pltpu.SemaphoreType.DMA
        blocks = (2, shares * others, HEAD_DIM, own.tokens)
        return [
            pltpu.VMEM(blocks, kind),
            pltpu.VMEM(blocks, kind),
            pltpu.VMEM((2, shares, HEAD_DIM, own.tokens), kind),
            dma((2, shares * others)),
            dma((2, shares * others)),
            dma((2, shares)),
            dma((2, HEADS)),
            dma((2,)),
        ]

    def split(self, block):
        f = lax.div(block, self.own.seq)
        order = lax.div(f, self.own.members) * self.own.seq + lax.rem(block, self.own.seq)
        return lax.rem(f, self.own.members), order

    def give(self, block, act):
        own = self.own
        member, order = self.split(block)
        away = lax.rem(member - own.member + own.members, own.members)

        @pl.when(away > 0)
        def _():
            columns = lanes(block, own.tokens)
            out = order * self.others + away - 1
            back = order * self.others + self.others - away
            for i in range(2):
                if act == "start":
                    self.give_from[i, out] = self.sums[i][:, columns].astype(self.held.dtype)
                copy = remote(
                    self.give_from.at[i, out],
                    self.given.at[i, back],
                    self.give_send.at[i, out],
                    self.give_recv.at[i, back],
                    own.of_head(own.head, member),
                )
                copy.start() if act == "start" else copy.wait_send()

    def back(self, block, order, i, act):
        own = self.own
        there = self.outs[i].at[head_rows(own.head), :]

        @pl.when(block == own.block)
        def _():
            copy = pltpu.make_async_copy(self.held.at[i, order], there, self.local.at[i])
            copy.start() if act == "start" else copy.wait()

        @pl.when(block != own.block)
        def _():
            copy = remote(
                self.held.at[i, order],
                there,
                self.send.at[i, order],
                self.recv.at[i, own.head],
                own.of_block(block),
            )
            copy.start() if act == "start" else copy.wait_send()

    def add(self, block):
        member, order = self.split(block)

        @pl.when(member == self.own.member)
        def _():
            columns = lanes(block, self.own.tokens)
            for i in range(2):
                total = self.sums[i][:, columns]
                for j in range(self.others):
                    slot = order * self.others + j
                    there = self.given.at[i, slot]
                    remote(
                        there,
                        there,
                        self.give_send.at[i, 0],
                        self.give_recv.at[i, slot],
                        self.own.of_block(0),
                    ).wait_recv()
                    total = total + self.given[i, slot].astype(jnp.float32)
                self.held[i, order] = total.astype(self.held.dtype)
                self.back(block, order, i, "start")

    def over(self, first, count, act):
        def one(step, carry):
            act(first + step)
            return carry

        lax.fori_loop(0, count, one, 0)

    def finish(self):
        def arrive(head, carry):
            @pl.when(head != self.own.head)
            def _():
                for i in range(2):
                    there = self.outs[i].at[head_rows(head), :]
                    remote(
                        there, there, self.send.at[i, 0], self.recv.at[i, head], self.own.of_block(0)
                    ).wait_recv()

            return carry

        lax.fori_loop(0, HEADS, arrive, 0)

        def settle(block):
            self.give(block, "wait")
            member, order = self.split(block)

            @pl.when(member == self.own.member)
            def _():
                for i in range(2):
                    self.back(block, order, i, "wait")

        self.over(0, self.own.total, settle)


class Tail:
    def __init__(self, grid, inputs, landed, outs, scratch):
        self.grid = grid
        self.normed_ref, self.xn_ref, self.cos_ref, self.sin_ref, self.ffn_ref = inputs[:5]
        self.weights = inputs[5:]
        self.landed = landed
        self.dh_ref, self.dv_ref = outs
        *self.terms, self.gain_terms, self.weight, self.turned, self.sem = scratch

    @staticmethod
    def scratch(grid, features, tokens, kind):
        rows = features // grid.total
        return (
            [pltpu.VMEM((grid.total, rows, features), kind)] * 3
            + [
                pltpu.VMEM((grid.total, 8, 128), jnp.float32),
                pltpu.VMEM((2, grid.total, rows, features), kind),
                pltpu.VMEM((tokens, features), kind),
                pltpu.SemaphoreType.DMA((2,)),
            ]
        )

    def load(self, step, i):
        return pltpu.make_async_copy(self.weights[i], self.weight.at[step % 2], self.sem.at[step % 2])

    def unrotate(self, i, part):
        columns = pl.ds(pl.multiple_of(part * COLUMNS, COLUMNS), COLUMNS)
        found = self.landed[i][columns, :].astype(jnp.float32)
        if i == 2:
            found = 0.5 * found
        else:
            cosine, sine_tab = self.cos_ref[...], self.sin_ref[...]
            half, turned = HEAD_DIM // 2, []
            for first in range(0, COLUMNS, HEAD_DIM):
                front, back = found[first : first + half], found[first + half : first + HEAD_DIM]
                turned += [front * cosine + back * sine_tab, back * cosine - front * sine_tab]
            found = jnp.concatenate(turned, axis=0)
        turned = found.T.astype(self.turned.dtype)
        self.turned[:, columns] = turned
        if i == 2:
            self.dv_ref[:, columns] = turned

    def project(self, i, step, part, first):
        columns = pl.ds(pl.multiple_of(part * COLUMNS, COLUMNS), COLUMNS)
        per = self.grid.total * COLUMNS // self.normed_ref.shape[1]
        blocks = pl.ds(part * per, per)
        terms = first_dims(self.normed_ref[:, columns], self.turned[...])
        self.terms[i][blocks] = terms.reshape(per, -1, terms.shape[1]).astype(self.terms[i].dtype)
        weights = self.weight[step % 2, blocks].reshape(COLUMNS, -1)
        term = last_dims(self.turned[...], weights)
        self.dh_ref[:, columns] = term if first else self.dh_ref[:, columns] + term

    def gains(self):
        attn = jnp.sum(self.dh_ref[...] * self.xn_ref[...], axis=0, keepdims=True)
        row = lax.broadcasted_iota(jnp.int32, (8, 1), 0)
        both = jnp.where(row == 0, attn, jnp.where(row == 1, self.ffn_ref[...], 0.0))
        near = self.grid.total // 8
        for block in range(8):
            for i in range(near):
                self.gain_terms[block * near + i] = both[:, block * 128 : (block + 1) * 128]


REDUCE_FIRST = 14
REDUCE_TILES = 3
REDUCE_TAIL = 1


def backward_kernel(tokens, plans, counts, *refs):
    refs = list(refs)

    def take(count):
        taken = refs[:count]
        del refs[:count]
        return taken

    n, n_tree, first_counts = counts
    g_ref, q_ref, k_ref, v_ref, out_ref, lse_ref, pos_ref, begin_ref = take(8)
    tail_inputs = take(8) if n else None
    parts = take(n)
    outs = take(2 if n else 3)
    sums = take(n)
    first_sums = take(4 if n else 0)
    grads_ref, dq_ref, dk_sum, dv_sum = take(4)
    back_scratch = take(8)
    g_send, g_recv, g_local, dq_send, dq_recv, dq_local = take(6)
    own = Owners(tokens)
    own.locate()
    tree = None
    dq_out, dk_out, dv_out = landed = take(3) if n else outs
    if n:
        grid = Grid()
        grid.locate()
        tree = Reduce(grid, plans[0], parts, sums, take(n_tree))
        first_scratch = [take(count) for count in first_counts]
        tail = Tail(grid, tail_inputs, landed, outs, refs)
        parts_first = (*tail.terms, tail.gain_terms)
        trees = [
            Reduce(grid, plan, parts_first, first_sums, scratch)
            for plan, scratch in zip(plans[1], first_scratch)
        ]
    grads_back = GradsBack(own, (dk_sum, dv_sum), (dk_out, dv_out), *back_scratch[:3], back_scratch[3:])
    tiles = Tiles(own)

    own.barrier()
    spread_units(own, g_ref, grads_ref, g_send, g_recv, g_local, "start")
    if tree:
        tree.start()
    dk_sum[...] = jnp.zeros_like(dk_sum)
    dv_sum[...] = jnp.zeros_like(dv_sum)

    def advance(number):
        if tree:

            @pl.when(number < tree.places - 1)
            def _():
                tree.climb(number)

        return number + 1

    number = lax.fori_loop(0, REDUCE_FIRST, lambda step, number: advance(number), jnp.int32(0))
    await_units(own, grads_ref, g_send, g_recv)
    spread_units(own, g_ref, grads_ref, g_send, g_recv, g_local, "wait")
    units = QUERIES // UNIT
    blocks = tiles.span // tokens

    def one_group(step, number):
        group = tiles.groups - 1 - step
        here = group_lanes(group)
        queries, grads = q_ref[:, here], grads_ref[:, here]
        pos, begin, lse = pos_ref[:, here], begin_ref[:, here], lse_ref[:, here]
        delta = jnp.sum(grads.astype(jnp.float32) * out_ref[:, here], axis=0, keepdims=True)

        def body(tile, causal, current):
            number, dq = current
            number = now_and_then(tile, REDUCE_TILES, advance, number)
            there = key_lanes(tile)
            keys = k_ref[:, there]
            scores = shown(first_dims(keys, queries), tile, causal, pos, begin)
            probs = jnp.exp(scores - lse)
            dv_sum[:, there] += last_dims(grads, probs.astype(jnp.bfloat16))
            dscores = (probs * (first_dims(v_ref[:, there], grads) - delta)).astype(jnp.bfloat16)
            dk_sum[:, there] += last_dims(queries, dscores)
            return number, dq + plain(keys, dscores)

        number, dq = tiles.fold(
            group, body, (number, jnp.zeros((HEAD_DIM, QUERIES), jnp.float32))
        )
        dq_ref[:, here] = (dq * HEAD_DIM**-0.5).astype(dq_ref.dtype)
        collect_units(
            own, dq_ref, dq_out, dq_send, dq_recv, dq_local, "start", group * units, units
        )
        grads_back.over(group * blocks, blocks, lambda block: grads_back.give(block, "start"))

        @pl.when(step > 0)
        def _():
            grads_back.over((group + 1) * blocks, blocks, grads_back.add)

        return number

    number = lax.fori_loop(0, tiles.groups, one_group, number)
    grads_back.over(0, blocks, grads_back.add)
    await_heads(own, dq_out, dq_send, dq_recv)
    collect_units(own, dq_ref, dq_out, dq_send, dq_recv, dq_local, "wait", 0, own.units)
    grads_back.finish()
    if not tree:
        return

    parts_of = HEADS * HEAD_DIM // COLUMNS
    order = (0, 1, 2)
    tail.load(0, order[0]).start()
    for step, i in enumerate(order):
        tail.load(step, i).wait()
        if step < 2:
            tail.load(step + 1, order[step + 1]).start()

        def turn(part, number, i=i):
            tail.unrotate(i, part)
            return now_and_then(part, REDUCE_TAIL, advance, number)

        def project(part, number, i=i, step=step):
            tail.project(i, step, part, step == 0)
            return now_and_then(part, REDUCE_TAIL, advance, number)

        number = lax.fori_loop(0, parts_of, turn, number)
        number = lax.fori_loop(0, parts_of, project, number)
    tail.gains()
    trees[0].start()

    def climb(step, number):
        trees[0].climb(step)
        return advance(number)

    number = lax.fori_loop(0, trees[0].places - 1, climb, number)

    def last(number, carry):
        tree.climb(number)
        return carry

    lax.fori_loop(number, tree.places - 1, last, 0)
    trees[0].finish()
    tree.finish()


def backward(grads, q, k, v, out, lse, pos, begin, ident, tail=(), arrays=(), plans=((), ())):
    tokens, features, kind = grads.shape[1], grads.shape[0], grads.dtype
    grid, own = Grid(), Owners(tokens)
    n = len(arrays)
    count = own.units * UNIT
    dma = pltpu.SemaphoreType.DMA
    pairs = count * own.total * tokens // 3
    moved = sum(a.size * a.dtype.itemsize for a in arrays) + 6 * k.size
    back = jax.ShapeDtypeStruct(grads.shape, kind)
    scratch = (
        [pltpu.VMEM((HEAD_DIM, count), kind)] * 2
        + [pltpu.VMEM(k.shape, jnp.float32)] * 2
        + GradsBack.scratch(own, kind)
        + [dma((HEADS, own.halves)), dma((own.units,)), dma((own.halves,))]
        + [dma((own.units,)), dma((HEADS, own.halves)), dma((own.halves,))]
    )
    tree_scratch = first_scratch = []
    if n:
        tail_scratch = Tail.scratch(grid, features, tokens, kind)
        first = [jax.ShapeDtypeStruct((grid.total, features // grid.total, features), kind)] * 3
        first.append(jax.ShapeDtypeStruct((grid.total, 8, 128), jnp.float32))
        tree_scratch = Reduce.scratch(grid, plans[0], arrays)
        first_scratch = [Reduce.scratch(grid, plan, first) for plan in plans[1]]
        scratch += [pltpu.VMEM(grads.shape, kind)] * 3 + tree_scratch + sum(first_scratch, [])
        scratch += tail_scratch
        out_shape = [
            jax.ShapeDtypeStruct((tokens, features), jnp.float32),
            jax.ShapeDtypeStruct((tokens, features), kind),
        ]
        out_shape += summed_shapes(arrays) + summed_shapes(first)
        out_specs = [WHOLE] * len(out_shape)
        in_specs = [ANY] + [WHOLE] * 12 + [ANY] * (3 + n)
    else:
        out_shape, out_specs = [back] * 3, [ANY] * 3
        in_specs = [ANY] + [WHOLE] * 7
    outs = pl.pallas_call(
        functools.partial(
            backward_kernel, tokens, plans, (n, len(tree_scratch), [len(one) for one in first_scratch])
        ),
        out_shape=out_shape,
        in_specs=in_specs,
        out_specs=out_specs,
        scratch_shapes=scratch,
        compiler_params=pltpu.CompilerParams(
            collective_id=ident, has_side_effects=True, vmem_limit_bytes=VMEM_LIMIT
        ),
        cost_estimate=pl.CostEstimate(
            flops=pairs * 10 * HEAD_DIM, bytes_accessed=moved, transcendentals=pairs
        ),
    )(grads, q, k, v, out, lse, pos, begin, *tail, *arrays)
    return (outs[:2], outs[2 : 2 + n], outs[2 + n :]) if n else outs


def publish_kernel(x_ref, gain_ref, dh_ref, dy_ref, dv_ref, *refs):
    grad_ref, first_ref = refs[len(refs) // 2 - 1 : len(refs) // 2 + 1]
    sources, targets = refs[: len(refs) // 2 - 1], refs[len(refs) // 2 + 1 :]
    for source, target in zip(sources, targets):
        target[...] = source[...]
    x = x_ref[...].astype(jnp.float32)
    norm = rms_scale(x)
    scaled = dh_ref[...] * gain_ref[:1]
    normed = x * norm
    grad_ref[...] = dy_ref[...] + norm * (
        scaled - normed * jnp.mean(scaled * normed, axis=-1, keepdims=True)
    )
    first_ref[...] = dv_ref[...].astype(jnp.float32)


def publish(x, gains, grad_normed, grad_after, grad_v, arrays):
    wide = jax.ShapeDtypeStruct(x.shape, jnp.float32)
    return pl.pallas_call(
        publish_kernel,
        out_shape=[wide, wide] + [jax.ShapeDtypeStruct(a.shape, a.dtype) for a in arrays],
        in_specs=[WHOLE] * (5 + len(arrays)),
        out_specs=[WHOLE] * (2 + len(arrays)),
        compiler_params=pltpu.CompilerParams(vmem_limit_bytes=VMEM_LIMIT),
    )(x, gains, grad_normed, grad_after, grad_v, *arrays)


def plan(columns, *pieces):
    found, used = [], [0] * len(columns)
    for array, part, order in pieces:
        left = columns[array] - used[array]
        if not left:
            continue
        count = left if part is None else min(part, left)
        found.append((array, used[array], count, order))
        used[array] += count
    return found


def angle_tables(offsets):
    half_dim = HEAD_DIM // 2
    frequency = jnp.power(10000.0, -jnp.arange(half_dim, dtype=jnp.float32) / half_dim)
    angles = frequency[:, None] * offsets.astype(jnp.float32)[None, :]
    return jnp.cos(angles)[None], jnp.sin(angles)[None]


def rotate(tensor, cosine, sine_tab):
    pairs = tensor.reshape(HEADS, 2, HEAD_DIM // 2, -1)
    front, back = pairs[:, 0], pairs[:, 1]
    turned = jnp.stack([front * cosine - back * sine_tab, back * cosine + front * sine_tab], axis=1)
    return turned.reshape(tensor.shape)


def matmul(left, right):
    return jnp.dot(left, right, preferred_element_type=jnp.float32)


def contract(left, right, left_dim, right_dim):
    return lax.dot_general(
        left, right, (((left_dim,), (right_dim,)), ((), ())), preferred_element_type=jnp.float32
    )


def per_device(
    layer_input,
    v_first,
    offsets,
    g_attn,
    w_query,
    w_key,
    w_value,
    w_out,
    g_ffn,
    w_gate,
    w_up,
    w_down,
    out_cot,
):
    low = jnp.bfloat16
    tokens = layer_input.shape[0]
    seq, fsdp = lax.axis_size("seq"), lax.axis_size("fsdp")
    devices = seq * fsdp
    seq_index = lax.axis_index("seq")
    own_offsets = lax.dynamic_slice_in_dim(offsets, seq_index * tokens, tokens, 0)

    share = g_attn.shape[0]
    neighbours = 128 // share
    turn = lax.rem(seq_index * fsdp + lax.axis_index("fsdp"), neighbours) * share
    gains = jnp.zeros((16, 128), low)
    gains = lax.dynamic_update_slice(gains, jnp.stack([g_attn, g_ffn]), (0, turn))
    places = jnp.zeros((8, 128), jnp.int32)
    places = lax.dynamic_update_slice(places, own_offsets.reshape(-1, 128), (0, 0))
    first = (w_query, w_key, w_value, gains, places)
    half = w_key.shape[1] // 2 if devices <= 32 else None
    first_plan = plan(
        [shard.shape[1] for shard in first],
        (0, None, "A"), (1, half, "A"), (1, half, "B"), (2, None, "C"), (3, None, "C"), (4, None, "C"),
    )
    later = (w_gate, w_up, w_down, w_out)
    later_plan = plan(
        [shard.shape[1] for shard in later],
        (0, None, "A"), (1, None, "A"), (2, None, "C"), (3, half, "A"), (3, half, "B"),
    )

    own = Owners(tokens)
    member = lax.rem(lax.axis_index("fsdp"), own.members)
    pos = (
        (jnp.arange(own.units, dtype=jnp.int32)[:, None] * own.members + member) * UNIT
        + jnp.arange(UNIT, dtype=jnp.int32)[None]
    ).reshape(1, -1)
    cosine, sine_tab = angle_tables(own_offsets)
    input_f32 = layer_input.astype(jnp.float32)
    wholes, first_wholes, front, heads, (attended, lse, attn_tokens) = forward(
        (layer_input, v_first, cosine[0], sine_tab[0], pos),
        first, first_plan, later, later_plan, 0,
    )
    gain_rows, normed_a, begin, normed_input = front
    gain_ffn = gain_rows[1]
    proj_query, proj_key, proj_value = (whole.reshape(-1, whole.shape[2]) for whole in first_wholes)
    proj_gate, proj_up, proj_down, proj_out = (whole.reshape(-1, whole.shape[2]) for whole in wholes)

    after_attn = input_f32 + contract(attn_tokens, proj_out, 0, 0)
    norm_ffn = rms_scale(after_attn)
    normed_f = (after_attn * norm_ffn * gain_ffn).astype(low)
    gate_act = matmul(normed_f, proj_gate)
    up_act = matmul(normed_f, proj_up)
    sigmoid_gate = jax.nn.sigmoid(gate_act)
    silu_gate = gate_act * sigmoid_gate
    hidden = (silu_gate * up_act).astype(low)
    result = (after_attn + matmul(hidden, proj_down)).astype(low)

    grad_hidden = contract(out_cot, proj_down, 1, 1)
    grad_gate_low = (
        grad_hidden * up_act * sigmoid_gate * (1.0 + gate_act * (1.0 - sigmoid_gate))
    ).astype(low)
    grad_up_low = (grad_hidden * silu_gate).astype(low)
    grad_normed_f = contract(grad_gate_low, proj_gate, 1, 1) + contract(grad_up_low, proj_up, 1, 1)
    grad_gain_ffn = jnp.sum(grad_normed_f * after_attn * norm_ffn, axis=0)
    scaled_ffn = grad_normed_f * gain_ffn
    grad_after = (
        out_cot.astype(jnp.float32)
        + norm_ffn * scaled_ffn
        - after_attn * norm_ffn**3 * jnp.mean(scaled_ffn * after_attn, axis=-1, keepdims=True)
    )
    grad_attn_low = grad_after.astype(low)
    grad_attended = contract(proj_out, grad_attn_low, 1, 1).astype(low)

    def terms(*grads):
        return [grad.astype(low).reshape(devices, -1, grad.shape[1]) for grad in grads]

    later_terms = terms(
        contract(normed_f, grad_gate_low, 0, 0), contract(normed_f, grad_up_low, 0, 0),
        contract(hidden, out_cot, 0, 0), contract(attn_tokens, grad_attn_low, 1, 0),
    )
    attention = (grad_attended, *heads, attended, lse, pos, begin)
    if devices <= 32:
        (grad_normed_a, grad_v), later_sums, first_sums = backward(
            *attention, 1,
            (
                normed_a, normed_input, cosine[0], sine_tab[0], grad_gain_ffn[None],
                *first_wholes,
            ),
            later_terms, (later_plan, [first_plan[:-1]]),
        )
    else:
        dq_rot, dk_rot, grad_mixed = backward(*attention, 1)
        grad_q = rotate(dq_rot.astype(jnp.float32), cosine, -sine_tab).astype(low)
        grad_k = rotate(dk_rot.astype(jnp.float32), cosine, -sine_tab).astype(low)
        grad_v = grad_mixed * jnp.asarray(0.5, low)
        grad_query_w = contract(normed_a, grad_q, 0, 1)
        grad_key_w = contract(normed_a, grad_k, 0, 1)
        grad_value_w = contract(normed_a, grad_v, 0, 1)
        grad_normed_a = (
            contract(grad_q, proj_query, 0, 1)
            + contract(grad_k, proj_key, 0, 1)
            + contract(grad_v, proj_value, 0, 1)
        )
        grad_gain_attn = jnp.sum(grad_normed_a * normed_input, axis=0)
        grad_v = grad_v.T
        gain_terms = jnp.pad(jnp.stack([grad_gain_attn, grad_gain_ffn]), ((0, 6), (0, 0)))
        gain_terms = jnp.repeat(gain_terms.reshape(8, -1, 128).transpose(1, 0, 2), neighbours, axis=0)
        first_terms = [*terms(grad_query_w, grad_key_w, grad_value_w), gain_terms]
        every = plan(
            [term.shape[2] for term in first_terms + later_terms],
            (0, None, "A"), (1, None, "B"), (2, None, "C"), (3, None, "C"),
            (4, None, "A"), (5, None, "A"), (6, None, "C"), (7, None, "C"),
        )
        all_sums = reduce_all(first_terms + later_terms, every, 2)
        first_sums, later_sums = all_sums[:4], all_sums[4:]
    grad_layer, grad_first, *sums, sum_gains = publish(
        layer_input, gain_rows, grad_normed_a, grad_after, grad_v,
        [*first_sums[:3], *later_sums, first_sums[3]],
    )
    sum_query, sum_key, sum_value, sum_gate, sum_up, sum_down, sum_out = sums
    sum_gains = lax.dynamic_slice_in_dim(sum_gains, turn, share, 1)
    return (
        result,
        grad_layer,
        grad_first,
        sum_gains[0],
        sum_query,
        sum_key,
        sum_value,
        sum_out,
        sum_gains[1],
        sum_gate,
        sum_up,
        sum_down,
    )


def solution(mesh):
    return jax.shard_map(
        per_device,
        mesh=mesh,
        in_specs=(
            P(("fsdp", "seq"), None),
            P(("fsdp", "seq"), None),
            P("fsdp"),
            P(("seq", "fsdp")),
            P(("seq", "fsdp"), None),
            P(("seq", "fsdp"), None),
            P(("seq", "fsdp"), None),
            P(("seq", "fsdp"), None),
            P(("seq", "fsdp")),
            P(("seq", "fsdp"), None),
            P(("seq", "fsdp"), None),
            P(("seq", "fsdp"), None),
            P(("fsdp", "seq"), None),
        ),
        out_specs=(
            P(("fsdp", "seq"), None),
            P(("fsdp", "seq"), None),
            P(("fsdp", "seq"), None),
            P(("seq", "fsdp")),
            P(("seq", "fsdp"), None),
            P(("seq", "fsdp"), None),
            P(("seq", "fsdp"), None),
            P(("seq", "fsdp"), None),
            P(("seq", "fsdp")),
            P(("seq", "fsdp"), None),
            P(("seq", "fsdp"), None),
            P(("seq", "fsdp"), None),
        ),
        check_vma=False,
    )
```

```python
import functools, math
import jax
import jax.numpy as jnp
from jax import lax
from jax.experimental import pallas as pl
from jax.experimental.pallas import tpu as pltpu
from jax.sharding import PartitionSpec as P

EPSILON = 1e-06
MESH = pl.DeviceIdType.MESH


class Grid:
    def __init__(self):
        self.seq = lax.axis_size("seq")
        self.fsdp = lax.axis_size("fsdp")
        self.size = {"z": self.seq, "y": 2, "x": self.fsdp // 4}
        self.stride = {"x": 2, "y": 2 * (self.fsdp // 4)}
        self.total = self.seq * self.fsdp
        self.plane = self.total // 2

    def locate(self):
        z, f = lax.axis_index("seq"), lax.axis_index("fsdp")
        nx = self.size["x"]
        self.f, self.zi = f, z
        self.core = lax.rem(f, 2)
        self.me = {"z": z, "y": lax.div(f, 2 * nx), "x": lax.rem(lax.div(f, 2), nx)}

    def step(self, dim, delta):
        if dim == "z":
            return {"seq": self.zi + delta}
        if dim == "core":
            return {"fsdp": self.f + 1 - 2 * self.core}
        return {"fsdp": self.f + delta * self.stride[dim]}

    def partner(self, dim):
        return self.step(dim, 1 - 2 * self.me[dim])

    def dirs(self, dim):
        return (0,) if self.size[dim] == 2 else (1, -1)

    def linear(self, at, core):
        nx = self.size["x"]
        return at["z"] * self.fsdp + (at["y"] * nx + at["x"]) * 2 + core

    def neighbours(self):
        found = [(None, self.step("core", 1))]
        for dim in ("z", "y", "x"):
            n = self.size[dim]
            if n == 1:
                continue
            if n == 2:
                found.append((None, self.partner(dim)))
            else:
                found.append((self.me[dim] < n - 1, self.step(dim, 1)))
                found.append((self.me[dim] > 0, self.step(dim, -1)))
        return found

    def barrier(self):
        sem = pltpu.get_barrier_semaphore()
        count = 0
        for exists, device in self.neighbours():
            if exists is None:
                pl.semaphore_signal(sem, inc=1, device_id=device, device_id_type=MESH)
                count = count + 1
            else:

                @pl.when(exists)
                def _(device=device):
                    pl.semaphore_signal(sem, inc=1, device_id=device, device_id_type=MESH)

                count = count + exists.astype(jnp.int32)
        pl.semaphore_wait(sem, count)

    def digits(self, order, number):
        at, rest = {}, number
        for dim in order:
            n, me = self.size[dim], self.me[dim]
            digit = lax.rem(rest, n)
            rest = lax.div(rest, n)
            if n == 2:
                at[dim] = lax.rem(me + digit, 2)
                continue
            both = jnp.minimum(me, n - 1 - me)
            away = lax.div(digit + 1, 2)
            side = jnp.where(lax.rem(digit, 2) == 1, me - away, me + away)
            far = jnp.where(me > both, me - (digit - both), me + (digit - both))
            at[dim] = jnp.where(digit <= 2 * both, side, far)
        return at

    def spaced_digits(self, order, number):
        at, ok = {}, None
        rest = number
        for dim in order:
            n = self.size[dim]
            base = 2 if n == 2 else 2 * n - 1
            digit = lax.rem(rest, base)
            rest = lax.div(rest, base)
            if n == 2:
                at[dim] = lax.rem(self.me[dim] + digit, 2)
            elif n == 1:
                at[dim] = self.me[dim]
            else:
                away = lax.div(digit + 1, 2)
                at[dim] = jnp.where(lax.rem(digit, 2) == 1, self.me[dim] - away, self.me[dim] + away)
                inside = (at[dim] >= 0) & (at[dim] < n)
                ok = inside if ok is None else ok & inside
        return at, ok

    def spaced_places(self):
        return math.prod(2 if n == 2 else 2 * n - 1 for n in self.size.values())

    def rank(self, order, at, upto):
        value, width = 0, 1
        for dim in order[:upto]:
            value = value + at[dim] * width
            width *= self.size[dim]
        return value

    def slots(self, order):
        first, count, width = [], 0, 1
        for dim in order:
            n = self.size[dim]
            first.append(count)
            count += width * {1: 0, 2: 1}.get(n, n + 1)
            width *= n
        return first, count

    def slot(self, order, j, w, at):
        first, _ = self.slots(order)
        dim = order[j]
        place = self.rank(order, at, j)
        if self.size[dim] == 2:
            return first[j] + place
        width = math.prod(self.size[d] for d in order[:j])
        return first[j] + place + width * (at[dim] + w)

    def branch(self, order, j, way, at):
        dim = order[j]
        n = self.size[dim]
        ok = None
        for later in order[j + 1 :]:
            same = at[later] == self.me[later]
            ok = same if ok is None else ok & same
        if n == 2:
            here = at[dim] == self.me[dim]
        elif way == 1:
            here = (at[dim] <= self.me[dim]) & (self.me[dim] < n - 1)
        else:
            here = (at[dim] >= self.me[dim]) & (self.me[dim] > 0)
        return here if ok is None else ok & here


ORDERS = {"A": ("z", "x", "y"), "B": ("x", "y", "z"), "C": ("y", "z", "x")}


class Gather:
    def __init__(self, grid, pieces, sources, outs, sems):
        self.grid, self.pieces, self.sources, self.outs = grid, pieces, sources, outs
        self.recv, self.send, self.core_send, self.own_sem = sems
        self.base, slots = [], 0
        for piece in pieces:
            self.base.append(slots)
            slots += grid.slots(ORDERS[piece[3]])[1]
        self.places = grid.plane

    @staticmethod
    def semaphores(grid, pieces, arrays):
        slots = sum(grid.slots(ORDERS[piece[3]])[1] for piece in pieces)
        dma = pltpu.SemaphoreType.DMA
        return [
            dma((len(pieces), grid.total)),
            dma((slots,)),
            dma((len(pieces), grid.plane)),
            dma((arrays,)),
        ]

    def own(self, i):
        mine = self.grid.linear(self.grid.me, self.grid.core)
        return pltpu.make_async_copy(self.sources[i], self.outs[i].at[mine], self.own_sem.at[i])

    def view(self, ref, p):
        return ref.at[:, pl.ds(self.pieces[p][1], self.pieces[p][2])]

    def sends(self, p, at, source, act):
        grid = self.grid
        order = ORDERS[self.pieces[p][3]]
        number = grid.linear(at, grid.core)
        target = self.view(self.outs[self.pieces[p][0]].at[number], p)

        def copy(sem, device):
            return pltpu.make_async_remote_copy(
                src_ref=source,
                dst_ref=target,
                send_sem=sem,
                recv_sem=self.recv.at[p, number],
                device_id=device,
                device_id_type=MESH,
            )

        for j, dim in enumerate(order):
            if grid.size[dim] == 1:
                continue
            ways = grid.dirs(dim)
            for w, way in enumerate(ways):
                slot = grid.slot(order, j, w, at)
                device = grid.partner(dim) if way == 0 else grid.step(dim, way)

                @pl.when(grid.branch(order, j, way, at))
                def _(device=device, slot=slot):
                    act(copy(self.send.at[self.base[p] + slot], device))

        act(copy(self.core_send.at[p, grid.rank(order, at, 3)], grid.step("core", 1)))

    def arrive(self, p, number):
        there = self.view(self.outs[self.pieces[p][0]].at[number], p)
        pltpu.make_async_remote_copy(
            src_ref=there,
            dst_ref=there,
            send_sem=self.core_send.at[p, 0],
            recv_sem=self.recv.at[p, number],
            device_id=self.grid.step("core", 1),
            device_id_type=MESH,
        ).wait_recv()

    def each(self, number, act):
        used = sorted({piece[3] for piece in self.pieces})
        at = {order: self.grid.digits(ORDERS[order], number) for order in used}
        for p, piece in enumerate(self.pieces):
            act(p, at[piece[3]])

    def start(self):
        for i in range(len(self.sources)):
            self.own(i).start()
        for p in range(len(self.pieces)):
            self.sends(
                p, self.grid.me, self.view(self.sources[self.pieces[p][0]], p), lambda c: c.start()
            )

    def relay(self, number):
        def act(p, at):
            where = self.grid.linear(at, self.grid.core)
            self.arrive(p, where)
            self.sends(p, at, self.view(self.outs[self.pieces[p][0]].at[where], p), lambda c: c.start())

        self.each(number, act)

    def finish(self):
        def act(p, at):
            self.arrive(p, self.grid.linear(at, 1 - self.grid.core))
            where = self.grid.linear(at, self.grid.core)
            self.sends(
                p, at, self.view(self.outs[self.pieces[p][0]].at[where], p), lambda c: c.wait_send()
            )

        def one(number, carry):
            self.each(number, act)
            return carry

        lax.fori_loop(0, self.places, one, 0)
        for i in range(len(self.sources)):
            self.own(i).wait()


def gather_kernel(pieces, n_arrays, *refs):
    grid = Grid()
    grid.locate()
    tree = Gather(grid, pieces, refs[:n_arrays], refs[n_arrays : 2 * n_arrays], refs[2 * n_arrays :])
    grid.barrier()
    tree.start()

    def forward(number, carry):
        tree.relay(number)
        return carry

    lax.fori_loop(1, tree.places, forward, 0)
    tree.finish()


def gathered_shapes(grid, arrays):
    return [jax.ShapeDtypeStruct((grid.total, *a.shape), a.dtype) for a in arrays]


def gather_all(arrays, pieces, ident):
    grid = Grid()
    n = len(arrays)
    moved = sum(a.size * a.dtype.itemsize for a in arrays) * grid.total
    return pl.pallas_call(
        functools.partial(gather_kernel, pieces, n),
        out_shape=gathered_shapes(grid, arrays),
        in_specs=[pl.BlockSpec(memory_space=pl.ANY)] * n,
        out_specs=[pl.BlockSpec(memory_space=pl.ANY)] * n,
        scratch_shapes=Gather.semaphores(grid, pieces, n),
        compiler_params=pltpu.CompilerParams(collective_id=ident, has_side_effects=True),
        cost_estimate=pl.CostEstimate(flops=0, bytes_accessed=moved, transcendentals=0),
    )(*arrays)


class Reduce:
    def __init__(self, grid, pieces, parts, outs, scratch):
        n = len(pieces)
        self.grid, self.pieces, self.parts, self.outs = grid, pieces, parts, outs
        self.pair, self.slot, self.held = (scratch[i * n : (i + 1) * n] for i in range(3))
        sems = scratch[3 * n :]
        self.core_send, self.core_recv, self.tree_send, self.tree_recv, self.own_sem = sems
        self.places = grid.spaced_places()

    @staticmethod
    def scratch(grid, pieces, arrays):
        most = max(grid.slots(order)[1] for order in ORDERS.values())
        shape = [(arrays[p[0]].shape[1], p[2]) for p in pieces]
        kind = [arrays[p[0]].dtype for p in pieces]
        count = [grid.slots(ORDERS[p[3]])[1] for p in pieces]
        dma = pltpu.SemaphoreType.DMA
        n = len(pieces)
        return (
            [pltpu.VMEM((grid.plane, *s), k) for s, k in zip(shape, kind)]
            + [pltpu.VMEM((c, *s), k) for c, s, k in zip(count, shape, kind)]
            + [pltpu.VMEM((2, *s), k) for s, k in zip(shape, kind)]
            + [dma((n, grid.plane)), dma((n, grid.plane)), dma((n, grid.plane)), dma((n, most)), dma((n, 2))]
        )

    def each(self, number, act):
        used = {piece[3] for piece in self.pieces}
        places = {order: self.grid.spaced_digits(ORDERS[order], number) for order in sorted(used)}
        for p, piece in enumerate(self.pieces):
            at, ok = places[piece[3]]

            def run(p=p, at=at):
                act(p, at)

            if ok is None:
                run()
            else:
                pl.when(ok)(run)

    def block(self, p, at, core):
        array, lower, count, _ = self.pieces[p]
        return self.parts[array].at[self.grid.linear(at, core), :, pl.ds(lower, count)]

    def rank(self, p, at):
        return self.grid.rank(ORDERS[self.pieces[p][3]], at, 3)

    def to_sibling(self, p, at):
        rank = self.rank(p, at)
        return pltpu.make_async_remote_copy(
            src_ref=self.block(p, at, 1 - self.grid.core),
            dst_ref=self.pair[p].at[rank],
            send_sem=self.core_send.at[p, rank],
            recv_sem=self.core_recv.at[p, rank],
            device_id=self.grid.step("core", 1),
            device_id_type=MESH,
        )

    def fetch(self, p, at, number):
        slot = lax.rem(number, 2)
        return pltpu.make_async_copy(
            self.block(p, at, self.grid.core), self.held[p].at[slot], self.own_sem.at[p, slot]
        )

    def to_parent(self, p, at, act):
        grid = self.grid
        order = ORDERS[self.pieces[p][3]]
        rank = self.rank(p, at)
        for j, dim in enumerate(order):
            if grid.size[dim] == 1:
                continue
            ways = grid.dirs(dim)
            ok = None
            for later in order[j + 1 :]:
                same = at[later] == grid.me[later]
                ok = same if ok is None else ok & same
            for w, way in enumerate(ways):
                slot = grid.slot(order, j, w, at)
                if way == 0:
                    here, device = at[dim] != grid.me[dim], grid.partner(dim)
                elif way == 1:
                    here, device = at[dim] < grid.me[dim], grid.step(dim, -1)
                else:
                    here, device = at[dim] > grid.me[dim], grid.step(dim, 1)
                here = here if ok is None else ok & here

                @pl.when(here)
                def _(slot=slot, device=device):
                    act(
                        pltpu.make_async_remote_copy(
                            src_ref=self.pair[p].at[rank],
                            dst_ref=self.slot[p].at[slot],
                            send_sem=self.tree_send.at[p, rank],
                            recv_sem=self.tree_recv.at[p, slot],
                            device_id=device,
                            device_id_type=MESH,
                        )
                    )

    def add(self, p, at, number, children, out):
        held, pair, slots = self.held[p], self.pair[p], self.slot[p]
        slot, rank = lax.rem(number, 2), self.rank(p, at)
        rows, columns = held.shape[1:]
        width = max(
            w for w in range(128, columns + 1, 128) if columns % w == 0 and (w == 128 or rows * w <= 49152)
        )
        array, lower, _, _ = self.pieces[p]

        def one(step, carry):
            first = pl.multiple_of(step * width, 128)
            here = pl.ds(first, width)
            total = held[slot, :, here].astype(jnp.float32) + pair[rank, :, here].astype(jnp.float32)
            for child in children:
                total = total + slots[child, :, here].astype(jnp.float32)
            if out:
                self.outs[array][:, pl.ds(lower + first, width)] = total
            else:
                pair[rank, :, here] = total.astype(pair.dtype)
            return carry

        lax.fori_loop(0, columns // width, one, 0)

    def combine(self, p, at, number):
        grid = self.grid
        order = ORDERS[self.pieces[p][3]]
        rank = self.rank(p, at)
        self.to_sibling(p, at).wait_recv()
        self.fetch(p, at, number).wait()

        def arrived(slot):
            there = self.slot[p].at[slot]
            pltpu.make_async_remote_copy(
                src_ref=there,
                dst_ref=there,
                send_sem=self.tree_send.at[p, rank],
                recv_sem=self.tree_recv.at[p, slot],
                device_id=grid.step("core", 1),
                device_id_type=MESH,
            ).wait_recv()
            return slot

        def level(j, children):
            if j < 0:
                self.add(p, at, number, children, True)
                return
            dim = order[j]
            n, me = grid.size[dim], grid.me[dim]
            if n == 1:
                level(j - 1, children)
                return
            same = at[dim] == me
            if n == 2:
                pl.when(jnp.logical_not(same))(lambda: self.add(p, at, number, children, False))
                pl.when(same)(lambda: level(j - 1, children + [arrived(grid.slot(order, j, 0, at))]))
                return
            up, down = me < n - 1, me > 0
            more = at[dim] > me
            behind = ((at[dim] < me) & up) | (more & down)

            @pl.when(jnp.logical_not(same) & behind)
            def _():
                w = jnp.where(more, 1, 0)
                self.add(p, at, number, children + [arrived(grid.slot(order, j, w, at))], False)

            pl.when(jnp.logical_not(same | behind))(lambda: self.add(p, at, number, children, False))

            def sides(*ways):
                level(j - 1, children + [arrived(grid.slot(order, j, w, at)) for w in ways])

            pl.when(same & up & down)(lambda: sides(0, 1))
            pl.when(same & up & jnp.logical_not(down))(lambda: sides(0))
            pl.when(same & jnp.logical_not(up) & down)(lambda: sides(1))

        level(2, [])

    def start(self):
        places = self.places

        def one(step, carry):
            self.each(places - 1 - step, lambda p, at: self.to_sibling(p, at).start())
            return carry

        self.each(places - 1, lambda p, at: self.fetch(p, at, places - 1).start())
        lax.fori_loop(0, places, one, 0)

    def climb(self, step):
        number = self.places - 1 - step
        self.each(number - 1, lambda p, at: self.fetch(p, at, number - 1).start())

        def work(p, at):
            self.combine(p, at, number)
            self.to_parent(p, at, lambda copy: copy.start())

        self.each(number, work)

    def finish(self):
        def root(p, at):
            self.combine(p, at, 0)

        self.each(0, root)

        def one(number, carry):
            def drain(p, at):
                self.to_sibling(p, at).wait_send()

                @pl.when(number > 0)
                def _():
                    self.to_parent(p, at, lambda copy: copy.wait_send())

            self.each(number, drain)
            return carry

        lax.fori_loop(0, self.places, one, 0)


def reduce_kernel(pieces, n_arrays, *refs):
    grid = Grid()
    grid.locate()
    tree = Reduce(grid, pieces, refs[:n_arrays], refs[n_arrays : 2 * n_arrays], refs[2 * n_arrays :])
    grid.barrier()
    tree.start()

    def climb(step, carry):
        tree.climb(step)
        return carry

    lax.fori_loop(0, tree.places - 1, climb, 0)
    tree.finish()


VMEM_LIMIT = 62 << 20


def summed_shapes(arrays):
    return [jax.ShapeDtypeStruct(a.shape[1:], jnp.float32) for a in arrays]


def reduce_all(arrays, pieces, ident):
    grid = Grid()
    n = len(arrays)
    moved = sum(a.size * a.dtype.itemsize for a in arrays)
    return pl.pallas_call(
        functools.partial(reduce_kernel, pieces, n),
        out_shape=summed_shapes(arrays),
        in_specs=[pl.BlockSpec(memory_space=pl.ANY)] * n,
        out_specs=[pl.BlockSpec(memory_space=pltpu.VMEM)] * n,
        scratch_shapes=Reduce.scratch(grid, pieces, arrays),
        compiler_params=pltpu.CompilerParams(
            collective_id=ident, has_side_effects=True, vmem_limit_bytes=VMEM_LIMIT
        ),
        cost_estimate=pl.CostEstimate(flops=0, bytes_accessed=2 * moved, transcendentals=0),
    )(*arrays)


HEADS = 16
HEAD_DIM = 64
UNIT = 128
NEGATIVE = -1e30


class Owners:
    def __init__(self, tokens):
        self.seq, self.fsdp = lax.axis_size("seq"), lax.axis_size("fsdp")
        self.total = self.seq * self.fsdp
        self.members = self.total // HEADS
        self.heads_here = HEADS // self.seq
        self.tokens = tokens
        self.halves = tokens // UNIT
        self.units = self.halves * self.total // self.members

    def locate(self):
        s, f = lax.axis_index("seq"), lax.axis_index("fsdp")
        self.s, self.f = s, f
        self.linear = s * self.fsdp + f
        self.block = f * self.seq + s
        self.head = s * self.heads_here + lax.div(f, self.members)
        self.member = lax.rem(f, self.members)

    def of_head(self, head, member):
        return {
            "seq": lax.div(head, self.heads_here),
            "fsdp": lax.rem(head, self.heads_here) * self.members + member,
        }

    def of_block(self, block):
        return {"seq": lax.rem(block, self.seq), "fsdp": lax.div(block, self.seq)}

    def barrier(self):
        sem = pltpu.get_barrier_semaphore()

        def greet(delta, carry):
            other = lax.rem(self.linear + delta, self.total)
            device = {"seq": lax.div(other, self.fsdp), "fsdp": lax.rem(other, self.fsdp)}
            pl.semaphore_signal(sem, inc=1, device_id=device, device_id_type=MESH)
            return carry

        lax.fori_loop(1, self.total, greet, 0)
        pl.semaphore_wait(sem, self.total - 1)


def remote(source, target, send_sem, recv_sem, device):
    return pltpu.make_async_remote_copy(
        src_ref=source,
        dst_ref=target,
        send_sem=send_sem,
        recv_sem=recv_sem,
        device_id=device,
        device_id_type=MESH,
    )


def head_rows(head):
    return pl.ds(pl.multiple_of(head * HEAD_DIM, HEAD_DIM), HEAD_DIM)


def lanes(number, width):
    return pl.ds(pl.multiple_of(number * width, width), width)


def spread_units(own, source, target, send, recv, local, act):
    def to_head(delta, carry):
        head = lax.rem(own.head + delta, HEADS)
        for half in range(own.halves):
            unit = own.halves * own.block + half
            member = lax.rem(unit, own.members)
            place = lax.div(unit, own.members)
            piece = source.at[head_rows(head), pl.ds(half * UNIT, UNIT)]
            there = target.at[:, lanes(place, UNIT)]
            here = (head == own.head) & (member == own.member)

            @pl.when(here)
            def _(piece=piece, there=there, half=half):
                copy = pltpu.make_async_copy(piece, there, local.at[half])
                copy.start() if act == "start" else copy.wait()

            @pl.when(jnp.logical_not(here))
            def _(piece=piece, there=there, half=half, member=member, place=place, head=head):
                copy = remote(
                    piece, there, send.at[head, half], recv.at[place], own.of_head(head, member)
                )
                copy.start() if act == "start" else copy.wait_send()

        return carry

    lax.fori_loop(0, HEADS, to_head, 0)


def await_units(own, target, send, recv):
    def one(place, carry):
        unit = place * own.members + own.member
        there = target.at[:, lanes(place, UNIT)]

        @pl.when(lax.div(unit, own.halves) != own.block)
        def _():
            remote(
                there, there, send.at[0, 0], recv.at[place], own.of_block(0)
            ).wait_recv()

        return carry

    lax.fori_loop(0, own.units, one, 0)


def collect_units(own, source, target, send, recv, local, act, first, count):
    def one(step, carry):
        place = first + step
        unit = place * own.members + own.member
        block, half = lax.div(unit, own.halves), lax.rem(unit, own.halves)
        piece = source.at[:, lanes(place, UNIT)]
        there = target.at[head_rows(own.head), lanes(half, UNIT)]

        @pl.when(block == own.block)
        def _():
            copy = pltpu.make_async_copy(piece, there, local.at[half])
            copy.start() if act == "start" else copy.wait()

        @pl.when(block != own.block)
        def _():
            copy = remote(
                piece, there, send.at[place], recv.at[own.head, half], own.of_block(block)
            )
            copy.start() if act == "start" else copy.wait_send()

        return carry

    lax.fori_loop(0, count, one, 0)


def await_heads(own, target, send, recv):
    def one(head, carry):
        for half in range(own.halves):
            unit = own.halves * own.block + half
            there = target.at[head_rows(head), pl.ds(half * UNIT, UNIT)]

            @pl.when((head != own.head) | (lax.rem(unit, own.members) != own.member))
            def _(there=there, half=half):
                remote(
                    there, there, send.at[0], recv.at[head, half], own.of_block(0)
                ).wait_recv()

        return carry

    lax.fori_loop(0, HEADS, one, 0)


QUERIES = 512
KEYS = 1024
BESIDE_PROJECT = 4
BESIDE_EXCHANGE = 5
BESIDE_TILES = 5
LATER_AT = 4
COLUMNS = 256
ANY = pl.BlockSpec(memory_space=pl.ANY)
WHOLE = pl.BlockSpec(memory_space=pltpu.VMEM)


def plain(left, right):
    return lax.dot_general(left, right, (((1,), (0,)), ((), ())), preferred_element_type=jnp.float32)


def first_dims(left, right):
    return lax.dot_general(left, right, (((0,), (0,)), ((), ())), preferred_element_type=jnp.float32)


def last_dims(left, right):
    return lax.dot_general(left, right, (((1,), (1,)), ((), ())), preferred_element_type=jnp.float32)


class Tiles:
    def __init__(self, own):
        self.span = QUERIES * own.members
        self.groups = own.units * UNIT // QUERIES
        self.longest = own.total * own.tokens // 2

    def fold(self, group, body, state):
        start = group * self.span
        low = lax.div(jnp.maximum(start - self.longest + 1, 0), KEYS)
        edge, high = lax.div(start, KEYS), lax.div(start + self.span + KEYS - 1, KEYS)
        state = lax.fori_loop(low, edge, lambda tile, s: body(tile, False, s), state)
        return lax.fori_loop(edge, high, lambda tile, s: body(tile, True, s), state)


def key_lanes(tile):
    return pl.ds(pl.multiple_of(tile * KEYS, KEYS), KEYS)


def group_lanes(group):
    return pl.ds(pl.multiple_of(group * QUERIES, QUERIES), QUERIES)


def shown(scores, tile, causal, pos, begin):
    number = tile * KEYS + lax.broadcasted_iota(jnp.int32, (KEYS, 1), 0)
    allowed = number >= begin
    if causal:
        allowed = allowed & (number <= pos)
    return jnp.where(allowed, scores, NEGATIVE)


def attend_group(tiles, group, q_ref, k_ref, v_ref, pos_ref, begin_ref, step, number):
    here = group_lanes(group)
    queries, pos, begin = q_ref[:, here], pos_ref[:, here], begin_ref[:, here]

    def body(tile, causal, current):
        number, top, total, summed = current
        number = now_and_then(tile, BESIDE_TILES, step, number)
        scores = shown(first_dims(k_ref[:, key_lanes(tile)], queries), tile, causal, pos, begin)
        new_top = jnp.maximum(top, jnp.max(scores, axis=0, keepdims=True))
        weights = jnp.exp(scores - new_top)
        shrink = jnp.exp(top - new_top)
        total = total * shrink + jnp.sum(weights, axis=0, keepdims=True)
        summed = summed * shrink + plain(v_ref[:, key_lanes(tile)], weights.astype(jnp.bfloat16))
        return number, new_top, total, summed

    number, top, total, summed = tiles.fold(
        group,
        body,
        (
            number,
            jnp.full((1, QUERIES), NEGATIVE, jnp.float32),
            jnp.zeros((1, QUERIES), jnp.float32),
            jnp.zeros((HEAD_DIM, QUERIES), jnp.float32),
        ),
    )
    return summed / total, top + jnp.log(total), number


class ToHeads:
    def __init__(self, own, sources, targets, sems):
        self.own = own
        self.q_ref, *pairs = sources
        self.q_out, *outs = targets
        self.pairs = tuple(zip(pairs, outs))
        self.q_send, self.q_recv, self.q_local, self.send, self.recv, self.local, self.hand_send = sems
        self.shares = own.total // own.members
        self.mine = lax.div(own.f, own.members) * own.seq + own.s

    @staticmethod
    def semaphores(own):
        dma = pltpu.SemaphoreType.DMA
        return [
            dma((HEADS, own.halves)),
            dma((own.units,)),
            dma((own.halves,)),
            dma((2, HEADS)),
            dma((2, own.total)),
            dma((2,)),
            dma((2, own.total // own.members * (own.members - 1))),
        ]

    def keys(self, i, act):
        own = self.own
        source, target = self.pairs[i]

        def to_head(delta, carry):
            head = lax.rem(own.head + delta, HEADS)
            piece = source.at[head_rows(head), :]
            there = target.at[:, lanes(own.block, own.tokens)]

            @pl.when(head == own.head)
            def _(piece=piece, there=there, i=i):
                copy = pltpu.make_async_copy(piece, there, self.local.at[i])
                copy.start() if act == "start" else copy.wait()

            @pl.when(head != own.head)
            def _(piece=piece, there=there, i=i):
                copy = remote(
                    piece,
                    there,
                    self.send.at[i, head],
                    self.recv.at[i, own.block],
                    own.of_head(head, own.member),
                )
                copy.start() if act == "start" else copy.wait_send()

            return carry

        lax.fori_loop(0, HEADS, to_head, 0)

    def hand(self, i, order, block, source, act):
        own = self.own
        for away in range(1, own.members):
            member = lax.rem(own.member + away, own.members)
            copy = remote(
                source,
                self.pairs[i][1].at[:, lanes(block, own.tokens)],
                self.hand_send.at[i, order * (own.members - 1) + away - 1],
                self.recv.at[i, block],
                own.of_head(own.head, member),
            )
            copy.start() if act == "start" else copy.wait_send()

    def hand_own(self, i, act):
        source = self.pairs[i][0].at[head_rows(self.own.head), :]
        self.hand(i, self.shares - 1, self.own.block, source, act)

    def block_of(self, step):
        order = lax.rem(self.mine + step, self.shares)
        f = self.own.member + self.own.members * lax.div(order, self.own.seq)
        return f * self.own.seq + lax.rem(order, self.own.seq)

    def arrive(self, i, block):
        there = self.pairs[i][1].at[:, lanes(block, self.own.tokens)]
        remote(
            there, there, self.send.at[i, 0], self.recv.at[i, block], self.own.of_block(0)
        ).wait_recv()
        return there

    def start_keys(self, i):
        self.keys(i, "start")
        self.hand_own(i, "start")

    def start_queries(self):
        spread_units(self.own, self.q_ref, self.q_out, self.q_send, self.q_recv, self.q_local, "start")

    def relay(self, step):
        block = self.block_of(step)
        for i in range(2):
            self.hand(i, step - 1, block, self.arrive(i, block), "start")

    def finish(self):
        own = self.own

        def rest(block, carry):
            @pl.when(lax.rem(lax.div(block, own.seq), own.members) != own.member)
            def _():
                for i in range(2):
                    self.arrive(i, block)

            return carry

        lax.fori_loop(0, own.total, rest, 0)
        await_units(own, self.q_out, self.q_send, self.q_recv)
        spread_units(own, self.q_ref, self.q_out, self.q_send, self.q_recv, self.q_local, "wait")
        for i in range(2):
            self.keys(i, "wait")
            self.hand_own(i, "wait")

        def settle(step, carry):
            block = self.block_of(step)
            for i, (_, target) in enumerate(self.pairs):
                self.hand(i, step - 1, block, target.at[:, lanes(block, own.tokens)], "wait")
            return carry

        lax.fori_loop(1, self.shares, settle, 0)


def now_and_then(index, every, act, number):
    return lax.cond(lax.rem(index, every) == 0, act, lambda x: x, number)


def rms_scale(tensor):
    return lax.rsqrt(jnp.mean(tensor * tensor, axis=-1, keepdims=True) + EPSILON)


class Front:
    def __init__(self, grid, own, plan, sources, inputs, landed, tokens_of, outs, sems):
        self.grid, self.own = grid, own
        self.x_ref, self.vf_ref, self.cos_ref, self.sin_ref, self.pos_ref = inputs
        self.landed, self.tokens_of = landed, tokens_of
        self.keep, (self.gain_ref, self.normed_ref, self.begin_ref, self.xn_ref) = outs[:3], outs[3:]
        self.keep_sem = sems[-1]
        self.tree = Gather(grid, plan, sources, landed, sems[:-1])

    def keeping(self, i):
        return pltpu.make_async_copy(self.landed[i], self.keep[i], self.keep_sem.at[i])

    def gather(self, between):
        def one(number, carry):
            self.tree.relay(number)
            between(number)
            return carry

        lax.fori_loop(1, self.tree.places, one, 0)
        self.tree.finish()
        for i in range(3):
            self.keeping(i).start()

    def norm(self):
        x = self.x_ref[...].astype(jnp.float32)
        self.xn_ref[...] = x * rms_scale(x)

    def prepare(self):
        gains, places = self.landed[3:]
        near = self.grid.total // 8
        rows = []
        for lane_block in range(8):
            rows.append(
                sum(
                    gains[lane_block * near + i, :8, :].astype(jnp.float32) for i in range(near)
                )
            )
        gain = jnp.concatenate(rows, axis=1)
        self.gain_ref[...] = gain
        self.normed_ref[...] = (self.xn_ref[...] * gain[:1]).astype(self.normed_ref.dtype)
        own = self.own

        def unit(place, carry):
            number = place * own.members + own.member
            block, half = lax.div(number, own.halves), lax.rem(number, own.halves)
            device = lax.rem(block, own.seq) * own.fsdp + lax.div(block, own.seq)
            here = lanes(place, UNIT)
            self.begin_ref[:, here] = self.pos_ref[:, here] - places[device, pl.ds(half, 1), :]
            return carry

        lax.fori_loop(0, own.units, unit, 0)

    def project(self, i, part):
        columns = pl.ds(pl.multiple_of(part * COLUMNS, COLUMNS), COLUMNS)
        weights = self.landed[i][:, :, columns].reshape(-1, COLUMNS)
        found = plain(self.normed_ref[...], weights)
        target = self.tokens_of[i]
        if i == 2:
            mixed = 0.5 * found + 0.5 * self.vf_ref[:, columns].astype(jnp.float32)
            target[columns, :] = mixed.T.astype(target.dtype)
            return
        found = found.T
        cosine, sine_tab = self.cos_ref[...], self.sin_ref[...]
        half, turned = HEAD_DIM // 2, []
        for first in range(0, COLUMNS, HEAD_DIM):
            front, back = found[first : first + half], found[first + half : first + HEAD_DIM]
            turned += [front * cosine - back * sine_tab, back * cosine + front * sine_tab]
        turned = jnp.concatenate(turned, axis=0).astype(target.dtype)
        target[columns, :] = turned * jnp.asarray(HEAD_DIM**-0.5, target.dtype) if i == 0 else turned


def forward_kernel(tokens, plans, counts, *refs):
    refs = list(refs)

    def take(count):
        taken = refs[:count]
        del refs[:count]
        return taken

    n_first, n = counts
    inputs, sources_first, sources = take(5), take(n_first), take(n)
    wholes, first_outs, keep = take(n), take(7), take(3)
    out_ref, lse_ref, back_ref = take(3)
    heads, (low_ref,) = take(3), take(1)
    landed, tokens_of = take(n_first), take(3)
    tree_sems, exchange_sems, (out_send, out_recv, out_local, keep_sem) = take(4), take(7), take(4)
    first_sems = take(5)
    grid, own = Grid(), Owners(tokens)
    grid.locate()
    own.locate()
    front = Front(
        grid, own, plans[0], sources_first, inputs, landed, tokens_of, first_outs, first_sems
    )
    tree = Gather(grid, plans[1], sources, wholes, tree_sems)
    exchange = ToHeads(own, tokens_of, heads, exchange_sems)
    tiles = Tiles(own)
    pos_ref, begin_ref = inputs[4], first_outs[5]

    own.barrier()
    front.tree.start()
    front.norm()
    front.gather(lambda number: pl.when(number == LATER_AT)(tree.start))
    front.prepare()

    def advance(number):
        @pl.when(number < tree.places)
        def _():
            tree.relay(number)

        return number + 1

    number = jnp.int32(1)
    for i in (1, 2, 0):

        def part(index, number, i=i):
            front.project(i, index)
            return now_and_then(index, BESIDE_PROJECT, advance, number)

        number = lax.fori_loop(0, HEADS * HEAD_DIM // COLUMNS, part, number)
        if i:
            exchange.start_keys(i - 1)
        else:
            exchange.start_queries()

    def relay(step, number):
        exchange.relay(step)
        return now_and_then(step, BESIDE_EXCHANGE, advance, number)

    number = lax.fori_loop(1, exchange.shares, relay, number)
    exchange.finish()
    keeping = [pltpu.make_async_copy(heads[i], keep[i], keep_sem.at[i]) for i in range(3)]
    for copy in keeping:
        copy.start()
    units = QUERIES // UNIT

    def one_group(group, number):
        here = group_lanes(group)
        attended, lse, number = attend_group(
            tiles, group, *heads, pos_ref, begin_ref, advance, number
        )
        out_ref[:, here] = attended
        lse_ref[:, here] = lse
        low_ref[:, here] = attended.astype(low_ref.dtype)
        collect_units(
            own, low_ref, back_ref, out_send, out_recv, out_local, "start", group * units, units
        )
        return number

    number = lax.fori_loop(0, tiles.groups, one_group, number)

    def last(number, carry):
        tree.relay(number)
        return carry

    lax.fori_loop(number, tree.places, last, 0)
    await_heads(own, back_ref, out_send, out_recv)
    collect_units(own, low_ref, back_ref, out_send, out_recv, out_local, "wait", 0, own.units)
    tree.finish()
    for copy in keeping:
        copy.wait()
    for i in range(3):
        front.keeping(i).wait()


def forward(inputs, first, first_plan, later, later_plan, ident):
    (tokens, features), kind = inputs[1].shape, inputs[1].dtype
    grid, own = Grid(), Owners(tokens)
    n, n_first = len(later), len(first)
    count = own.units * UNIT
    dma = pltpu.SemaphoreType.DMA
    heads = [(HEAD_DIM, count)] + [(HEAD_DIM, own.total * tokens)] * 2
    pairs = count * own.total * tokens // 3
    moved = sum(a.size * a.dtype.itemsize for a in (*first, *later)) * grid.total
    landed = gathered_shapes(grid, first)
    outs = pl.pallas_call(
        functools.partial(forward_kernel, tokens, (first_plan, later_plan), (n_first, n)),
        out_shape=gathered_shapes(grid, later)
        + landed[:3]
        + [
            jax.ShapeDtypeStruct((8, features), jnp.float32),
            jax.ShapeDtypeStruct((tokens, features), kind),
            jax.ShapeDtypeStruct((1, count), jnp.int32),
            jax.ShapeDtypeStruct((tokens, features), jnp.float32),
        ]
        + [jax.ShapeDtypeStruct(s, kind) for s in heads]
        + [
            jax.ShapeDtypeStruct((HEAD_DIM, count), jnp.float32),
            jax.ShapeDtypeStruct((1, count), jnp.float32),
            jax.ShapeDtypeStruct((features, tokens), kind),
        ],
        in_specs=[WHOLE] * 5 + [ANY] * (n_first + n),
        out_specs=[ANY] * (n + 3) + [WHOLE] * 4 + [ANY] * 3 + [WHOLE] * 2 + [ANY],
        scratch_shapes=[pltpu.VMEM(s, kind) for s in heads]
        + [pltpu.VMEM((HEAD_DIM, count), kind)]
        + [pltpu.VMEM(a.shape, a.dtype) for a in landed]
        + [pltpu.VMEM((features, tokens), kind)] * 3
        + Gather.semaphores(grid, later_plan, n)
        + ToHeads.semaphores(own)
        + [dma((own.units,)), dma((HEADS, own.halves)), dma((own.halves,)), dma((3,))]
        + Gather.semaphores(grid, first_plan, n_first)
        + [dma((3,))],
        compiler_params=pltpu.CompilerParams(
            collective_id=ident, has_side_effects=True, vmem_limit_bytes=VMEM_LIMIT
        ),
        cost_estimate=pl.CostEstimate(
            flops=pairs * 4 * HEAD_DIM, bytes_accessed=moved, transcendentals=pairs
        ),
    )(*inputs, *first, *later)
    return outs[:n], outs[n : n + 3], outs[n + 3 : n + 7], outs[n + 7 : n + 10], outs[n + 10 :]


class GradsBack:
    def __init__(self, own, sums, outs, give_from, given, held, sems):
        self.own, self.sums, self.outs = own, sums, outs
        self.give_from, self.given, self.held = give_from, given, held
        self.give_send, self.give_recv, self.send, self.recv, self.local = sems
        self.others = own.members - 1

    @staticmethod
    def scratch(own, kind):
        shares, others = own.total // own.members, own.members - 1
        dma = pltpu.SemaphoreType.DMA
        blocks = (2, shares * others, HEAD_DIM, own.tokens)
        return [
            pltpu.VMEM(blocks, kind),
            pltpu.VMEM(blocks, kind),
            pltpu.VMEM((2, shares, HEAD_DIM, own.tokens), kind),
            dma((2, shares * others)),
            dma((2, shares * others)),
            dma((2, shares)),
            dma((2, HEADS)),
            dma((2,)),
        ]

    def split(self, block):
        f = lax.div(block, self.own.seq)
        order = lax.div(f, self.own.members) * self.own.seq + lax.rem(block, self.own.seq)
        return lax.rem(f, self.own.members), order

    def give(self, block, act):
        own = self.own
        member, order = self.split(block)
        away = lax.rem(member - own.member + own.members, own.members)

        @pl.when(away > 0)
        def _():
            columns = lanes(block, own.tokens)
            out = order * self.others + away - 1
            back = order * self.others + self.others - away
            for i in range(2):
                if act == "start":
                    self.give_from[i, out] = self.sums[i][:, columns].astype(self.held.dtype)
                copy = remote(
                    self.give_from.at[i, out],
                    self.given.at[i, back],
                    self.give_send.at[i, out],
                    self.give_recv.at[i, back],
                    own.of_head(own.head, member),
                )
                copy.start() if act == "start" else copy.wait_send()

    def back(self, block, order, i, act):
        own = self.own
        there = self.outs[i].at[head_rows(own.head), :]

        @pl.when(block == own.block)
        def _():
            copy = pltpu.make_async_copy(self.held.at[i, order], there, self.local.at[i])
            copy.start() if act == "start" else copy.wait()

        @pl.when(block != own.block)
        def _():
            copy = remote(
                self.held.at[i, order],
                there,
                self.send.at[i, order],
                self.recv.at[i, own.head],
                own.of_block(block),
            )
            copy.start() if act == "start" else copy.wait_send()

    def add(self, block):
        member, order = self.split(block)

        @pl.when(member == self.own.member)
        def _():
            columns = lanes(block, self.own.tokens)
            for i in range(2):
                total = self.sums[i][:, columns]
                for j in range(self.others):
                    slot = order * self.others + j
                    there = self.given.at[i, slot]
                    remote(
                        there,
                        there,
                        self.give_send.at[i, 0],
                        self.give_recv.at[i, slot],
                        self.own.of_block(0),
                    ).wait_recv()
                    total = total + self.given[i, slot].astype(jnp.float32)
                self.held[i, order] = total.astype(self.held.dtype)
                self.back(block, order, i, "start")

    def over(self, first, count, act):
        def one(step, carry):
            act(first + step)
            return carry

        lax.fori_loop(0, count, one, 0)

    def finish(self):
        def arrive(head, carry):
            @pl.when(head != self.own.head)
            def _():
                for i in range(2):
                    there = self.outs[i].at[head_rows(head), :]
                    remote(
                        there, there, self.send.at[i, 0], self.recv.at[i, head], self.own.of_block(0)
                    ).wait_recv()

            return carry

        lax.fori_loop(0, HEADS, arrive, 0)

        def settle(block):
            self.give(block, "wait")
            member, order = self.split(block)

            @pl.when(member == self.own.member)
            def _():
                for i in range(2):
                    self.back(block, order, i, "wait")

        self.over(0, self.own.total, settle)


class Tail:
    def __init__(self, grid, inputs, landed, outs, scratch):
        self.grid = grid
        self.normed_ref, self.xn_ref, self.cos_ref, self.sin_ref, self.ffn_ref = inputs[:5]
        self.weights = inputs[5:]
        self.landed = landed
        self.dh_ref, self.dv_ref = outs
        *self.terms, self.gain_terms, self.weight, self.turned, self.sem = scratch

    @staticmethod
    def scratch(grid, features, tokens, kind):
        rows = features // grid.total
        return (
            [pltpu.VMEM((grid.total, rows, features), kind)] * 3
            + [
                pltpu.VMEM((grid.total, 8, 128), jnp.float32),
                pltpu.VMEM((2, grid.total, rows, features), kind),
                pltpu.VMEM((tokens, features), kind),
                pltpu.SemaphoreType.DMA((2,)),
            ]
        )

    def load(self, step, i):
        return pltpu.make_async_copy(self.weights[i], self.weight.at[step % 2], self.sem.at[step % 2])

    def unrotate(self, i, part):
        columns = pl.ds(pl.multiple_of(part * COLUMNS, COLUMNS), COLUMNS)
        found = self.landed[i][columns, :].astype(jnp.float32)
        if i == 2:
            found = 0.5 * found
        else:
            cosine, sine_tab = self.cos_ref[...], self.sin_ref[...]
            half, turned = HEAD_DIM // 2, []
            for first in range(0, COLUMNS, HEAD_DIM):
                front, back = found[first : first + half], found[first + half : first + HEAD_DIM]
                turned += [front * cosine + back * sine_tab, back * cosine - front * sine_tab]
            found = jnp.concatenate(turned, axis=0)
        turned = found.T.astype(self.turned.dtype)
        self.turned[:, columns] = turned
        if i == 2:
            self.dv_ref[:, columns] = turned

    def project(self, i, step, part, first):
        columns = pl.ds(pl.multiple_of(part * COLUMNS, COLUMNS), COLUMNS)
        per = self.grid.total * COLUMNS // self.normed_ref.shape[1]
        blocks = pl.ds(part * per, per)
        terms = first_dims(self.normed_ref[:, columns], self.turned[...])
        self.terms[i][blocks] = terms.reshape(per, -1, terms.shape[1]).astype(self.terms[i].dtype)
        weights = self.weight[step % 2, blocks].reshape(COLUMNS, -1)
        term = last_dims(self.turned[...], weights)
        self.dh_ref[:, columns] = term if first else self.dh_ref[:, columns] + term

    def gains(self):
        attn = jnp.sum(self.dh_ref[...] * self.xn_ref[...], axis=0, keepdims=True)
        row = lax.broadcasted_iota(jnp.int32, (8, 1), 0)
        both = jnp.where(row == 0, attn, jnp.where(row == 1, self.ffn_ref[...], 0.0))
        near = self.grid.total // 8
        for block in range(8):
            for i in range(near):
                self.gain_terms[block * near + i] = both[:, block * 128 : (block + 1) * 128]


REDUCE_FIRST = 11
REDUCE_TILES = 3
REDUCE_TAIL = 1


def backward_kernel(tokens, plans, counts, *refs):
    refs = list(refs)

    def take(count):
        taken = refs[:count]
        del refs[:count]
        return taken

    n, n_tree, first_counts = counts
    g_ref, q_ref, k_ref, v_ref, out_ref, lse_ref, pos_ref, begin_ref = take(8)
    tail_inputs = take(8) if n else None
    parts = take(n)
    outs = take(2 if n else 3)
    sums = take(n)
    first_sums = take(4 if n else 0)
    grads_ref, dq_ref, dk_sum, dv_sum = take(4)
    back_scratch = take(8)
    g_send, g_recv, g_local, dq_send, dq_recv, dq_local = take(6)
    own = Owners(tokens)
    own.locate()
    tree = None
    dq_out, dk_out, dv_out = landed = take(3) if n else outs
    if n:
        grid = Grid()
        grid.locate()
        tree = Reduce(grid, plans[0], parts, sums, take(n_tree))
        first_scratch = [take(count) for count in first_counts]
        tail = Tail(grid, tail_inputs, landed, outs, refs)
        parts_first = (*tail.terms, tail.gain_terms)
        trees = [
            Reduce(grid, plan, parts_first, first_sums, scratch)
            for plan, scratch in zip(plans[1], first_scratch)
        ]
    grads_back = GradsBack(own, (dk_sum, dv_sum), (dk_out, dv_out), *back_scratch[:3], back_scratch[3:])
    tiles = Tiles(own)

    own.barrier()
    spread_units(own, g_ref, grads_ref, g_send, g_recv, g_local, "start")
    if tree:
        tree.start()
    dk_sum[...] = jnp.zeros_like(dk_sum)
    dv_sum[...] = jnp.zeros_like(dv_sum)

    def advance(number):
        if tree:

            @pl.when(number < tree.places - 1)
            def _():
                tree.climb(number)

        return number + 1

    number = lax.fori_loop(0, REDUCE_FIRST, lambda step, number: advance(number), jnp.int32(0))
    await_units(own, grads_ref, g_send, g_recv)
    spread_units(own, g_ref, grads_ref, g_send, g_recv, g_local, "wait")
    units = QUERIES // UNIT
    blocks = tiles.span // tokens

    def one_group(step, number):
        group = tiles.groups - 1 - step
        here = group_lanes(group)
        queries, grads = q_ref[:, here], grads_ref[:, here]
        pos, begin, lse = pos_ref[:, here], begin_ref[:, here], lse_ref[:, here]
        delta = jnp.sum(grads.astype(jnp.float32) * out_ref[:, here], axis=0, keepdims=True)

        def body(tile, causal, current):
            number, dq = current
            number = now_and_then(tile, REDUCE_TILES, advance, number)
            there = key_lanes(tile)
            keys = k_ref[:, there]
            scores = shown(first_dims(keys, queries), tile, causal, pos, begin)
            probs = jnp.exp(scores - lse)
            dv_sum[:, there] += last_dims(grads, probs.astype(jnp.bfloat16))
            dscores = (probs * (first_dims(v_ref[:, there], grads) - delta)).astype(jnp.bfloat16)
            dk_sum[:, there] += last_dims(queries, dscores)
            return number, dq + plain(keys, dscores)

        number, dq = tiles.fold(
            group, body, (number, jnp.zeros((HEAD_DIM, QUERIES), jnp.float32))
        )
        dq_ref[:, here] = (dq * HEAD_DIM**-0.5).astype(dq_ref.dtype)
        collect_units(
            own, dq_ref, dq_out, dq_send, dq_recv, dq_local, "start", group * units, units
        )
        grads_back.over(group * blocks, blocks, lambda block: grads_back.give(block, "start"))

        @pl.when(step > 0)
        def _():
            grads_back.over((group + 1) * blocks, blocks, grads_back.add)

        return number

    number = lax.fori_loop(0, tiles.groups, one_group, number)
    grads_back.over(0, blocks, grads_back.add)
    await_heads(own, dq_out, dq_send, dq_recv)
    collect_units(own, dq_ref, dq_out, dq_send, dq_recv, dq_local, "wait", 0, own.units)
    grads_back.finish()
    if not tree:
        return

    parts_of = HEADS * HEAD_DIM // COLUMNS
    order = (0, 1, 2)
    tail.load(0, order[0]).start()
    for step, i in enumerate(order):
        tail.load(step, i).wait()
        if step < 2:
            tail.load(step + 1, order[step + 1]).start()

        def turn(part, number, i=i):
            tail.unrotate(i, part)
            return now_and_then(part, REDUCE_TAIL, advance, number)

        def project(part, number, i=i, step=step):
            tail.project(i, step, part, step == 0)
            return now_and_then(part, REDUCE_TAIL, advance, number)

        number = lax.fori_loop(0, parts_of, turn, number)
        number = lax.fori_loop(0, parts_of, project, number)
    tail.gains()
    trees[0].start()

    def climb(step, number):
        trees[0].climb(step)
        return advance(number)

    number = lax.fori_loop(0, trees[0].places - 1, climb, number)

    def last(number, carry):
        tree.climb(number)
        return carry

    lax.fori_loop(number, tree.places - 1, last, 0)
    trees[0].finish()
    tree.finish()


def backward(grads, q, k, v, out, lse, pos, begin, ident, tail=(), arrays=(), plans=((), ())):
    tokens, features, kind = grads.shape[1], grads.shape[0], grads.dtype
    grid, own = Grid(), Owners(tokens)
    n = len(arrays)
    count = own.units * UNIT
    dma = pltpu.SemaphoreType.DMA
    pairs = count * own.total * tokens // 3
    moved = sum(a.size * a.dtype.itemsize for a in arrays) + 6 * k.size
    back = jax.ShapeDtypeStruct(grads.shape, kind)
    scratch = (
        [pltpu.VMEM((HEAD_DIM, count), kind)] * 2
        + [pltpu.VMEM(k.shape, jnp.float32)] * 2
        + GradsBack.scratch(own, kind)
        + [dma((HEADS, own.halves)), dma((own.units,)), dma((own.halves,))]
        + [dma((own.units,)), dma((HEADS, own.halves)), dma((own.halves,))]
    )
    tree_scratch = first_scratch = []
    if n:
        tail_scratch = Tail.scratch(grid, features, tokens, kind)
        first = [jax.ShapeDtypeStruct((grid.total, features // grid.total, features), kind)] * 3
        first.append(jax.ShapeDtypeStruct((grid.total, 8, 128), jnp.float32))
        tree_scratch = Reduce.scratch(grid, plans[0], arrays)
        first_scratch = [Reduce.scratch(grid, plan, first) for plan in plans[1]]
        scratch += [pltpu.VMEM(grads.shape, kind)] * 3 + tree_scratch + sum(first_scratch, [])
        scratch += tail_scratch
        out_shape = [
            jax.ShapeDtypeStruct((tokens, features), jnp.float32),
            jax.ShapeDtypeStruct((tokens, features), kind),
        ]
        out_shape += summed_shapes(arrays) + summed_shapes(first)
        out_specs = [WHOLE] * len(out_shape)
        in_specs = [ANY] + [WHOLE] * 12 + [ANY] * (3 + n)
    else:
        out_shape, out_specs = [back] * 3, [ANY] * 3
        in_specs = [ANY] + [WHOLE] * 7
    outs = pl.pallas_call(
        functools.partial(
            backward_kernel, tokens, plans, (n, len(tree_scratch), [len(one) for one in first_scratch])
        ),
        out_shape=out_shape,
        in_specs=in_specs,
        out_specs=out_specs,
        scratch_shapes=scratch,
        compiler_params=pltpu.CompilerParams(
            collective_id=ident, has_side_effects=True, vmem_limit_bytes=VMEM_LIMIT
        ),
        cost_estimate=pl.CostEstimate(
            flops=pairs * 10 * HEAD_DIM, bytes_accessed=moved, transcendentals=pairs
        ),
    )(grads, q, k, v, out, lse, pos, begin, *tail, *arrays)
    return (outs[:2], outs[2 : 2 + n], outs[2 + n :]) if n else outs


def publish_kernel(x_ref, gain_ref, dh_ref, dy_ref, dv_ref, *refs):
    grad_ref, first_ref = refs[len(refs) // 2 - 1 : len(refs) // 2 + 1]
    sources, targets = refs[: len(refs) // 2 - 1], refs[len(refs) // 2 + 1 :]
    for source, target in zip(sources, targets):
        target[...] = source[...]
    x = x_ref[...].astype(jnp.float32)
    norm = rms_scale(x)
    scaled = dh_ref[...] * gain_ref[:1]
    normed = x * norm
    grad_ref[...] = dy_ref[...] + norm * (
        scaled - normed * jnp.mean(scaled * normed, axis=-1, keepdims=True)
    )
    first_ref[...] = dv_ref[...].astype(jnp.float32)


def publish(x, gains, grad_normed, grad_after, grad_v, arrays):
    wide = jax.ShapeDtypeStruct(x.shape, jnp.float32)
    return pl.pallas_call(
        publish_kernel,
        out_shape=[wide, wide] + [jax.ShapeDtypeStruct(a.shape, a.dtype) for a in arrays],
        in_specs=[WHOLE] * (5 + len(arrays)),
        out_specs=[WHOLE] * (2 + len(arrays)),
        compiler_params=pltpu.CompilerParams(vmem_limit_bytes=VMEM_LIMIT),
    )(x, gains, grad_normed, grad_after, grad_v, *arrays)


def plan(columns, *pieces):
    found, used = [], [0] * len(columns)
    for array, part, order in pieces:
        left = columns[array] - used[array]
        if not left:
            continue
        count = left if part is None else min(part, left)
        found.append((array, used[array], count, order))
        used[array] += count
    return found


def angle_tables(offsets):
    half_dim = HEAD_DIM // 2
    frequency = jnp.power(10000.0, -jnp.arange(half_dim, dtype=jnp.float32) / half_dim)
    angles = frequency[:, None] * offsets.astype(jnp.float32)[None, :]
    return jnp.cos(angles)[None], jnp.sin(angles)[None]


def rotate(tensor, cosine, sine_tab):
    pairs = tensor.reshape(HEADS, 2, HEAD_DIM // 2, -1)
    front, back = pairs[:, 0], pairs[:, 1]
    turned = jnp.stack([front * cosine - back * sine_tab, back * cosine + front * sine_tab], axis=1)
    return turned.reshape(tensor.shape)


def matmul(left, right):
    return jnp.dot(left, right, preferred_element_type=jnp.float32)


def contract(left, right, left_dim, right_dim):
    return lax.dot_general(
        left, right, (((left_dim,), (right_dim,)), ((), ())), preferred_element_type=jnp.float32
    )


def per_device(
    layer_input,
    v_first,
    offsets,
    g_attn,
    w_query,
    w_key,
    w_value,
    w_out,
    g_ffn,
    w_gate,
    w_up,
    w_down,
    out_cot,
):
    low = jnp.bfloat16
    tokens = layer_input.shape[0]
    seq, fsdp = lax.axis_size("seq"), lax.axis_size("fsdp")
    devices = seq * fsdp
    seq_index = lax.axis_index("seq")
    own_offsets = lax.dynamic_slice_in_dim(offsets, seq_index * tokens, tokens, 0)

    share = g_attn.shape[0]
    neighbours = 128 // share
    turn = lax.rem(seq_index * fsdp + lax.axis_index("fsdp"), neighbours) * share
    gains = jnp.zeros((16, 128), low)
    gains = lax.dynamic_update_slice(gains, jnp.stack([g_attn, g_ffn]), (0, turn))
    places = jnp.zeros((8, 128), jnp.int32)
    places = lax.dynamic_update_slice(places, own_offsets.reshape(-1, 128), (0, 0))
    first = (w_query, w_key, w_value, gains, places)
    half = w_key.shape[1] // 2 if devices <= 32 else None
    first_plan = plan(
        [shard.shape[1] for shard in first],
        (0, None, "A"), (1, half, "A"), (1, half, "B"), (2, None, "C"), (3, None, "C"), (4, None, "C"),
    )
    later = (w_gate, w_up, w_down, w_out)
    later_plan = plan(
        [shard.shape[1] for shard in later],
        (0, None, "A"), (1, None, "A"), (2, None, "C"), (3, half, "A"), (3, half, "B"),
    )

    own = Owners(tokens)
    member = lax.rem(lax.axis_index("fsdp"), own.members)
    pos = (
        (jnp.arange(own.units, dtype=jnp.int32)[:, None] * own.members + member) * UNIT
        + jnp.arange(UNIT, dtype=jnp.int32)[None]
    ).reshape(1, -1)
    cosine, sine_tab = angle_tables(own_offsets)
    input_f32 = layer_input.astype(jnp.float32)
    wholes, first_wholes, front, heads, (attended, lse, attn_tokens) = forward(
        (layer_input, v_first, cosine[0], sine_tab[0], pos),
        first, first_plan, later, later_plan, 0,
    )
    gain_rows, normed_a, begin, normed_input = front
    gain_ffn = gain_rows[1]
    proj_query, proj_key, proj_value = (whole.reshape(-1, whole.shape[2]) for whole in first_wholes)
    proj_gate, proj_up, proj_down, proj_out = (whole.reshape(-1, whole.shape[2]) for whole in wholes)

    after_attn = input_f32 + contract(attn_tokens, proj_out, 0, 0)
    norm_ffn = rms_scale(after_attn)
    normed_f = (after_attn * norm_ffn * gain_ffn).astype(low)
    gate_act = matmul(normed_f, proj_gate)
    up_act = matmul(normed_f, proj_up)
    sigmoid_gate = jax.nn.sigmoid(gate_act)
    silu_gate = gate_act * sigmoid_gate
    hidden = (silu_gate * up_act).astype(low)
    result = (after_attn + matmul(hidden, proj_down)).astype(low)

    grad_hidden = contract(out_cot, proj_down, 1, 1)
    grad_gate_low = (
        grad_hidden * up_act * sigmoid_gate * (1.0 + gate_act * (1.0 - sigmoid_gate))
    ).astype(low)
    grad_up_low = (grad_hidden * silu_gate).astype(low)
    grad_normed_f = contract(grad_gate_low, proj_gate, 1, 1) + contract(grad_up_low, proj_up, 1, 1)
    grad_gain_ffn = jnp.sum(grad_normed_f * after_attn * norm_ffn, axis=0)
    scaled_ffn = grad_normed_f * gain_ffn
    grad_after = (
        out_cot.astype(jnp.float32)
        + norm_ffn * scaled_ffn
        - after_attn * norm_ffn**3 * jnp.mean(scaled_ffn * after_attn, axis=-1, keepdims=True)
    )
    grad_attn_low = grad_after.astype(low)
    grad_attended = contract(proj_out, grad_attn_low, 1, 1).astype(low)

    def terms(*grads):
        return [grad.astype(low).reshape(devices, -1, grad.shape[1]) for grad in grads]

    later_terms = terms(
        contract(normed_f, grad_gate_low, 0, 0), contract(normed_f, grad_up_low, 0, 0),
        contract(hidden, out_cot, 0, 0), contract(attn_tokens, grad_attn_low, 1, 0),
    )
    attention = (grad_attended, *heads, attended, lse, pos, begin)
    if devices <= 32:
        (grad_normed_a, grad_v), later_sums, first_sums = backward(
            *attention, 1,
            (
                normed_a, normed_input, cosine[0], sine_tab[0], grad_gain_ffn[None],
                *first_wholes,
            ),
            later_terms, (later_plan, [first_plan[:-1]]),
        )
    else:
        dq_rot, dk_rot, grad_mixed = backward(*attention, 1)
        grad_q = rotate(dq_rot.astype(jnp.float32), cosine, -sine_tab).astype(low)
        grad_k = rotate(dk_rot.astype(jnp.float32), cosine, -sine_tab).astype(low)
        grad_v = grad_mixed * jnp.asarray(0.5, low)
        grad_query_w = contract(normed_a, grad_q, 0, 1)
        grad_key_w = contract(normed_a, grad_k, 0, 1)
        grad_value_w = contract(normed_a, grad_v, 0, 1)
        grad_normed_a = (
            contract(grad_q, proj_query, 0, 1)
            + contract(grad_k, proj_key, 0, 1)
            + contract(grad_v, proj_value, 0, 1)
        )
        grad_gain_attn = jnp.sum(grad_normed_a * normed_input, axis=0)
        grad_v = grad_v.T
        gain_terms = jnp.pad(jnp.stack([grad_gain_attn, grad_gain_ffn]), ((0, 6), (0, 0)))
        gain_terms = jnp.repeat(gain_terms.reshape(8, -1, 128).transpose(1, 0, 2), neighbours, axis=0)
        first_terms = [*terms(grad_query_w, grad_key_w, grad_value_w), gain_terms]
        every = plan(
            [term.shape[2] for term in first_terms + later_terms],
            (0, None, "A"), (1, None, "B"), (2, None, "C"), (3, None, "C"),
            (4, None, "A"), (5, None, "A"), (6, None, "C"), (7, None, "C"),
        )
        all_sums = reduce_all(first_terms + later_terms, every, 2)
        first_sums, later_sums = all_sums[:4], all_sums[4:]
    grad_layer, grad_first, *sums, sum_gains = publish(
        layer_input, gain_rows, grad_normed_a, grad_after, grad_v,
        [*first_sums[:3], *later_sums, first_sums[3]],
    )
    sum_query, sum_key, sum_value, sum_gate, sum_up, sum_down, sum_out = sums
    sum_gains = lax.dynamic_slice_in_dim(sum_gains, turn, share, 1)
    return (
        result,
        grad_layer,
        grad_first,
        sum_gains[0],
        sum_query,
        sum_key,
        sum_value,
        sum_out,
        sum_gains[1],
        sum_gate,
        sum_up,
        sum_down,
    )


def solution(mesh):
    return jax.shard_map(
        per_device,
        mesh=mesh,
        in_specs=(
            P(("fsdp", "seq"), None),
            P(("fsdp", "seq"), None),
            P("fsdp"),
            P(("seq", "fsdp")),
            P(("seq", "fsdp"), None),
            P(("seq", "fsdp"), None),
            P(("seq", "fsdp"), None),
            P(("seq", "fsdp"), None),
            P(("seq", "fsdp")),
            P(("seq", "fsdp"), None),
            P(("seq", "fsdp"), None),
            P(("seq", "fsdp"), None),
            P(("fsdp", "seq"), None),
        ),
        out_specs=(
            P(("fsdp", "seq"), None),
            P(("fsdp", "seq"), None),
            P(("fsdp", "seq"), None),
            P(("seq", "fsdp")),
            P(("seq", "fsdp"), None),
            P(("seq", "fsdp"), None),
            P(("seq", "fsdp"), None),
            P(("seq", "fsdp"), None),
            P(("seq", "fsdp")),
            P(("seq", "fsdp"), None),
            P(("seq", "fsdp"), None),
            P(("seq", "fsdp"), None),
        ),
        check_vma=False,
    )
```

```python
import functools, math
import jax
import jax.numpy as jnp
from jax import lax
from jax.experimental import pallas as pl
from jax.experimental.pallas import tpu as pltpu
from jax.sharding import PartitionSpec as P

EPSILON = 1e-06
MESH = pl.DeviceIdType.MESH


class Grid:
    def __init__(self):
        self.seq = lax.axis_size("seq")
        self.fsdp = lax.axis_size("fsdp")
        self.size = {"z": self.seq, "y": 2, "x": self.fsdp // 4}
        self.stride = {"x": 2, "y": 2 * (self.fsdp // 4)}
        self.total = self.seq * self.fsdp
        self.plane = self.total // 2

    def locate(self):
        z, f = lax.axis_index("seq"), lax.axis_index("fsdp")
        nx = self.size["x"]
        self.f, self.zi = f, z
        self.core = lax.rem(f, 2)
        self.me = {"z": z, "y": lax.div(f, 2 * nx), "x": lax.rem(lax.div(f, 2), nx)}

    def step(self, dim, delta):
        if dim == "z":
            return {"seq": self.zi + delta}
        if dim == "core":
            return {"fsdp": self.f + 1 - 2 * self.core}
        return {"fsdp": self.f + delta * self.stride[dim]}

    def partner(self, dim):
        return self.step(dim, 1 - 2 * self.me[dim])

    def dirs(self, dim):
        return (0,) if self.size[dim] == 2 else (1, -1)

    def linear(self, at, core):
        nx = self.size["x"]
        return at["z"] * self.fsdp + (at["y"] * nx + at["x"]) * 2 + core

    def neighbours(self):
        found = [(None, self.step("core", 1))]
        for dim in ("z", "y", "x"):
            n = self.size[dim]
            if n == 1:
                continue
            if n == 2:
                found.append((None, self.partner(dim)))
            else:
                found.append((self.me[dim] < n - 1, self.step(dim, 1)))
                found.append((self.me[dim] > 0, self.step(dim, -1)))
        return found

    def barrier(self):
        sem = pltpu.get_barrier_semaphore()
        count = 0
        for exists, device in self.neighbours():
            if exists is None:
                pl.semaphore_signal(sem, inc=1, device_id=device, device_id_type=MESH)
                count = count + 1
            else:

                @pl.when(exists)
                def _(device=device):
                    pl.semaphore_signal(sem, inc=1, device_id=device, device_id_type=MESH)

                count = count + exists.astype(jnp.int32)
        pl.semaphore_wait(sem, count)

    def digits(self, order, number):
        at, rest = {}, number
        for dim in order:
            n, me = self.size[dim], self.me[dim]
            digit = lax.rem(rest, n)
            rest = lax.div(rest, n)
            if n == 2:
                at[dim] = lax.rem(me + digit, 2)
                continue
            both = jnp.minimum(me, n - 1 - me)
            away = lax.div(digit + 1, 2)
            side = jnp.where(lax.rem(digit, 2) == 1, me - away, me + away)
            far = jnp.where(me > both, me - (digit - both), me + (digit - both))
            at[dim] = jnp.where(digit <= 2 * both, side, far)
        return at

    def spaced_digits(self, order, number):
        at, ok = {}, None
        rest = number
        for dim in order:
            n = self.size[dim]
            base = 2 if n == 2 else 2 * n - 1
            digit = lax.rem(rest, base)
            rest = lax.div(rest, base)
            if n == 2:
                at[dim] = lax.rem(self.me[dim] + digit, 2)
            elif n == 1:
                at[dim] = self.me[dim]
            else:
                away = lax.div(digit + 1, 2)
                at[dim] = jnp.where(lax.rem(digit, 2) == 1, self.me[dim] - away, self.me[dim] + away)
                inside = (at[dim] >= 0) & (at[dim] < n)
                ok = inside if ok is None else ok & inside
        return at, ok

    def spaced_places(self):
        return math.prod(2 if n == 2 else 2 * n - 1 for n in self.size.values())

    def rank(self, order, at, upto):
        value, width = 0, 1
        for dim in order[:upto]:
            value = value + at[dim] * width
            width *= self.size[dim]
        return value

    def slots(self, order):
        first, count, width = [], 0, 1
        for dim in order:
            n = self.size[dim]
            first.append(count)
            count += width * {1: 0, 2: 1}.get(n, n + 1)
            width *= n
        return first, count

    def slot(self, order, j, w, at):
        first, _ = self.slots(order)
        dim = order[j]
        place = self.rank(order, at, j)
        if self.size[dim] == 2:
            return first[j] + place
        width = math.prod(self.size[d] for d in order[:j])
        return first[j] + place + width * (at[dim] + w)

    def branch(self, order, j, way, at):
        dim = order[j]
        n = self.size[dim]
        ok = None
        for later in order[j + 1 :]:
            same = at[later] == self.me[later]
            ok = same if ok is None else ok & same
        if n == 2:
            here = at[dim] == self.me[dim]
        elif way == 1:
            here = (at[dim] <= self.me[dim]) & (self.me[dim] < n - 1)
        else:
            here = (at[dim] >= self.me[dim]) & (self.me[dim] > 0)
        return here if ok is None else ok & here


ORDERS = {"A": ("z", "x", "y"), "B": ("x", "y", "z"), "C": ("y", "z", "x")}


class Gather:
    def __init__(self, grid, pieces, sources, outs, sems):
        self.grid, self.pieces, self.sources, self.outs = grid, pieces, sources, outs
        self.recv, self.send, self.core_send, self.own_sem = sems
        self.base, slots = [], 0
        for piece in pieces:
            self.base.append(slots)
            slots += grid.slots(ORDERS[piece[3]])[1]
        self.places = grid.plane

    @staticmethod
    def semaphores(grid, pieces, arrays):
        slots = sum(grid.slots(ORDERS[piece[3]])[1] for piece in pieces)
        dma = pltpu.SemaphoreType.DMA
        return [
            dma((len(pieces), grid.total)),
            dma((slots,)),
            dma((len(pieces), grid.plane)),
            dma((arrays,)),
        ]

    def own(self, i):
        mine = self.grid.linear(self.grid.me, self.grid.core)
        return pltpu.make_async_copy(self.sources[i], self.outs[i].at[mine], self.own_sem.at[i])

    def view(self, ref, p):
        return ref.at[:, pl.ds(self.pieces[p][1], self.pieces[p][2])]

    def sends(self, p, at, source, act):
        grid = self.grid
        order = ORDERS[self.pieces[p][3]]
        number = grid.linear(at, grid.core)
        target = self.view(self.outs[self.pieces[p][0]].at[number], p)

        def copy(sem, device):
            return pltpu.make_async_remote_copy(
                src_ref=source,
                dst_ref=target,
                send_sem=sem,
                recv_sem=self.recv.at[p, number],
                device_id=device,
                device_id_type=MESH,
            )

        for j, dim in enumerate(order):
            if grid.size[dim] == 1:
                continue
            ways = grid.dirs(dim)
            for w, way in enumerate(ways):
                slot = grid.slot(order, j, w, at)
                device = grid.partner(dim) if way == 0 else grid.step(dim, way)

                @pl.when(grid.branch(order, j, way, at))
                def _(device=device, slot=slot):
                    act(copy(self.send.at[self.base[p] + slot], device))

        act(copy(self.core_send.at[p, grid.rank(order, at, 3)], grid.step("core", 1)))

    def arrive(self, p, number):
        there = self.view(self.outs[self.pieces[p][0]].at[number], p)
        pltpu.make_async_remote_copy(
            src_ref=there,
            dst_ref=there,
            send_sem=self.core_send.at[p, 0],
            recv_sem=self.recv.at[p, number],
            device_id=self.grid.step("core", 1),
            device_id_type=MESH,
        ).wait_recv()

    def each(self, number, act):
        used = sorted({piece[3] for piece in self.pieces})
        at = {order: self.grid.digits(ORDERS[order], number) for order in used}
        for p, piece in enumerate(self.pieces):
            act(p, at[piece[3]])

    def start(self):
        for i in range(len(self.sources)):
            self.own(i).start()
        for p in range(len(self.pieces)):
            self.sends(
                p, self.grid.me, self.view(self.sources[self.pieces[p][0]], p), lambda c: c.start()
            )

    def relay(self, number):
        def act(p, at):
            where = self.grid.linear(at, self.grid.core)
            self.arrive(p, where)
            self.sends(p, at, self.view(self.outs[self.pieces[p][0]].at[where], p), lambda c: c.start())

        self.each(number, act)

    def finish(self):
        def act(p, at):
            self.arrive(p, self.grid.linear(at, 1 - self.grid.core))
            where = self.grid.linear(at, self.grid.core)
            self.sends(
                p, at, self.view(self.outs[self.pieces[p][0]].at[where], p), lambda c: c.wait_send()
            )

        def one(number, carry):
            self.each(number, act)
            return carry

        lax.fori_loop(0, self.places, one, 0)
        for i in range(len(self.sources)):
            self.own(i).wait()


def gather_kernel(pieces, n_arrays, *refs):
    grid = Grid()
    grid.locate()
    tree = Gather(grid, pieces, refs[:n_arrays], refs[n_arrays : 2 * n_arrays], refs[2 * n_arrays :])
    grid.barrier()
    tree.start()

    def forward(number, carry):
        tree.relay(number)
        return carry

    lax.fori_loop(1, tree.places, forward, 0)
    tree.finish()


def gathered_shapes(grid, arrays):
    return [jax.ShapeDtypeStruct((grid.total, *a.shape), a.dtype) for a in arrays]


def gather_all(arrays, pieces, ident):
    grid = Grid()
    n = len(arrays)
    moved = sum(a.size * a.dtype.itemsize for a in arrays) * grid.total
    return pl.pallas_call(
        functools.partial(gather_kernel, pieces, n),
        out_shape=gathered_shapes(grid, arrays),
        in_specs=[pl.BlockSpec(memory_space=pl.ANY)] * n,
        out_specs=[pl.BlockSpec(memory_space=pl.ANY)] * n,
        scratch_shapes=Gather.semaphores(grid, pieces, n),
        compiler_params=pltpu.CompilerParams(collective_id=ident, has_side_effects=True),
        cost_estimate=pl.CostEstimate(flops=0, bytes_accessed=moved, transcendentals=0),
    )(*arrays)


class Reduce:
    def __init__(self, grid, pieces, parts, outs, scratch):
        n = len(pieces)
        self.grid, self.pieces, self.parts, self.outs = grid, pieces, parts, outs
        self.pair, self.slot, self.held = (scratch[i * n : (i + 1) * n] for i in range(3))
        sems = scratch[3 * n :]
        self.core_send, self.core_recv, self.tree_send, self.tree_recv, self.own_sem = sems
        self.places = grid.spaced_places()

    @staticmethod
    def scratch(grid, pieces, arrays):
        most = max(grid.slots(order)[1] for order in ORDERS.values())
        shape = [(arrays[p[0]].shape[1], p[2]) for p in pieces]
        kind = [arrays[p[0]].dtype for p in pieces]
        count = [grid.slots(ORDERS[p[3]])[1] for p in pieces]
        dma = pltpu.SemaphoreType.DMA
        n = len(pieces)
        return (
            [pltpu.VMEM((grid.plane, *s), k) for s, k in zip(shape, kind)]
            + [pltpu.VMEM((c, *s), k) for c, s, k in zip(count, shape, kind)]
            + [pltpu.VMEM((2, *s), k) for s, k in zip(shape, kind)]
            + [dma((n, grid.plane)), dma((n, grid.plane)), dma((n, grid.plane)), dma((n, most)), dma((n, 2))]
        )

    def each(self, number, act):
        used = {piece[3] for piece in self.pieces}
        places = {order: self.grid.spaced_digits(ORDERS[order], number) for order in sorted(used)}
        for p, piece in enumerate(self.pieces):
            at, ok = places[piece[3]]

            def run(p=p, at=at):
                act(p, at)

            if ok is None:
                run()
            else:
                pl.when(ok)(run)

    def block(self, p, at, core):
        array, lower, count, _ = self.pieces[p]
        return self.parts[array].at[self.grid.linear(at, core), :, pl.ds(lower, count)]

    def rank(self, p, at):
        return self.grid.rank(ORDERS[self.pieces[p][3]], at, 3)

    def to_sibling(self, p, at):
        rank = self.rank(p, at)
        return pltpu.make_async_remote_copy(
            src_ref=self.block(p, at, 1 - self.grid.core),
            dst_ref=self.pair[p].at[rank],
            send_sem=self.core_send.at[p, rank],
            recv_sem=self.core_recv.at[p, rank],
            device_id=self.grid.step("core", 1),
            device_id_type=MESH,
        )

    def fetch(self, p, at, number):
        slot = lax.rem(number, 2)
        return pltpu.make_async_copy(
            self.block(p, at, self.grid.core), self.held[p].at[slot], self.own_sem.at[p, slot]
        )

    def to_parent(self, p, at, act):
        grid = self.grid
        order = ORDERS[self.pieces[p][3]]
        rank = self.rank(p, at)
        for j, dim in enumerate(order):
            if grid.size[dim] == 1:
                continue
            ways = grid.dirs(dim)
            ok = None
            for later in order[j + 1 :]:
                same = at[later] == grid.me[later]
                ok = same if ok is None else ok & same
            for w, way in enumerate(ways):
                slot = grid.slot(order, j, w, at)
                if way == 0:
                    here, device = at[dim] != grid.me[dim], grid.partner(dim)
                elif way == 1:
                    here, device = at[dim] < grid.me[dim], grid.step(dim, -1)
                else:
                    here, device = at[dim] > grid.me[dim], grid.step(dim, 1)
                here = here if ok is None else ok & here

                @pl.when(here)
                def _(slot=slot, device=device):
                    act(
                        pltpu.make_async_remote_copy(
                            src_ref=self.pair[p].at[rank],
                            dst_ref=self.slot[p].at[slot],
                            send_sem=self.tree_send.at[p, rank],
                            recv_sem=self.tree_recv.at[p, slot],
                            device_id=device,
                            device_id_type=MESH,
                        )
                    )

    def add(self, p, at, number, children, out):
        held, pair, slots = self.held[p], self.pair[p], self.slot[p]
        slot, rank = lax.rem(number, 2), self.rank(p, at)
        rows, columns = held.shape[1:]
        width = max(
            w for w in range(128, columns + 1, 128) if columns % w == 0 and (w == 128 or rows * w <= 49152)
        )
        array, lower, _, _ = self.pieces[p]

        def one(step, carry):
            first = pl.multiple_of(step * width, 128)
            here = pl.ds(first, width)
            total = held[slot, :, here].astype(jnp.float32) + pair[rank, :, here].astype(jnp.float32)
            for child in children:
                total = total + slots[child, :, here].astype(jnp.float32)
            if out:
                self.outs[array][:, pl.ds(lower + first, width)] = total
            else:
                pair[rank, :, here] = total.astype(pair.dtype)
            return carry

        lax.fori_loop(0, columns // width, one, 0)

    def combine(self, p, at, number):
        grid = self.grid
        order = ORDERS[self.pieces[p][3]]
        rank = self.rank(p, at)
        self.to_sibling(p, at).wait_recv()
        self.fetch(p, at, number).wait()

        def arrived(slot):
            there = self.slot[p].at[slot]
            pltpu.make_async_remote_copy(
                src_ref=there,
                dst_ref=there,
                send_sem=self.tree_send.at[p, rank],
                recv_sem=self.tree_recv.at[p, slot],
                device_id=grid.step("core", 1),
                device_id_type=MESH,
            ).wait_recv()
            return slot

        def level(j, children):
            if j < 0:
                self.add(p, at, number, children, True)
                return
            dim = order[j]
            n, me = grid.size[dim], grid.me[dim]
            if n == 1:
                level(j - 1, children)
                return
            same = at[dim] == me
            if n == 2:
                pl.when(jnp.logical_not(same))(lambda: self.add(p, at, number, children, False))
                pl.when(same)(lambda: level(j - 1, children + [arrived(grid.slot(order, j, 0, at))]))
                return
            up, down = me < n - 1, me > 0
            more = at[dim] > me
            behind = ((at[dim] < me) & up) | (more & down)

            @pl.when(jnp.logical_not(same) & behind)
            def _():
                w = jnp.where(more, 1, 0)
                self.add(p, at, number, children + [arrived(grid.slot(order, j, w, at))], False)

            pl.when(jnp.logical_not(same | behind))(lambda: self.add(p, at, number, children, False))

            def sides(*ways):
                level(j - 1, children + [arrived(grid.slot(order, j, w, at)) for w in ways])

            pl.when(same & up & down)(lambda: sides(0, 1))
            pl.when(same & up & jnp.logical_not(down))(lambda: sides(0))
            pl.when(same & jnp.logical_not(up) & down)(lambda: sides(1))

        level(2, [])

    def start(self):
        places = self.places

        def one(step, carry):
            self.each(places - 1 - step, lambda p, at: self.to_sibling(p, at).start())
            return carry

        self.each(places - 1, lambda p, at: self.fetch(p, at, places - 1).start())
        lax.fori_loop(0, places, one, 0)

    def climb(self, step):
        number = self.places - 1 - step
        self.each(number - 1, lambda p, at: self.fetch(p, at, number - 1).start())

        def work(p, at):
            self.combine(p, at, number)
            self.to_parent(p, at, lambda copy: copy.start())

        self.each(number, work)

    def finish(self):
        def root(p, at):
            self.combine(p, at, 0)

        self.each(0, root)

        def one(number, carry):
            def drain(p, at):
                self.to_sibling(p, at).wait_send()

                @pl.when(number > 0)
                def _():
                    self.to_parent(p, at, lambda copy: copy.wait_send())

            self.each(number, drain)
            return carry

        lax.fori_loop(0, self.places, one, 0)


def reduce_kernel(pieces, n_arrays, *refs):
    grid = Grid()
    grid.locate()
    tree = Reduce(grid, pieces, refs[:n_arrays], refs[n_arrays : 2 * n_arrays], refs[2 * n_arrays :])
    grid.barrier()
    tree.start()

    def climb(step, carry):
        tree.climb(step)
        return carry

    lax.fori_loop(0, tree.places - 1, climb, 0)
    tree.finish()


VMEM_LIMIT = 62 << 20


def summed_shapes(arrays):
    return [jax.ShapeDtypeStruct(a.shape[1:], jnp.float32) for a in arrays]


def reduce_all(arrays, pieces, ident):
    grid = Grid()
    n = len(arrays)
    moved = sum(a.size * a.dtype.itemsize for a in arrays)
    return pl.pallas_call(
        functools.partial(reduce_kernel, pieces, n),
        out_shape=summed_shapes(arrays),
        in_specs=[pl.BlockSpec(memory_space=pl.ANY)] * n,
        out_specs=[pl.BlockSpec(memory_space=pltpu.VMEM)] * n,
        scratch_shapes=Reduce.scratch(grid, pieces, arrays),
        compiler_params=pltpu.CompilerParams(
            collective_id=ident, has_side_effects=True, vmem_limit_bytes=VMEM_LIMIT
        ),
        cost_estimate=pl.CostEstimate(flops=0, bytes_accessed=2 * moved, transcendentals=0),
    )(*arrays)


HEADS = 16
HEAD_DIM = 64
UNIT = 128
NEGATIVE = -1e30


class Owners:
    def __init__(self, tokens):
        self.seq, self.fsdp = lax.axis_size("seq"), lax.axis_size("fsdp")
        self.total = self.seq * self.fsdp
        self.members = self.total // HEADS
        self.heads_here = HEADS // self.seq
        self.tokens = tokens
        self.halves = tokens // UNIT
        self.units = self.halves * self.total // self.members

    def locate(self):
        s, f = lax.axis_index("seq"), lax.axis_index("fsdp")
        self.s, self.f = s, f
        self.linear = s * self.fsdp + f
        self.block = f * self.seq + s
        self.head = s * self.heads_here + lax.div(f, self.members)
        self.member = lax.rem(f, self.members)

    def of_head(self, head, member):
        return {
            "seq": lax.div(head, self.heads_here),
            "fsdp": lax.rem(head, self.heads_here) * self.members + member,
        }

    def of_block(self, block):
        return {"seq": lax.rem(block, self.seq), "fsdp": lax.div(block, self.seq)}

    def barrier(self):
        sem = pltpu.get_barrier_semaphore()

        def greet(delta, carry):
            other = lax.rem(self.linear + delta, self.total)
            device = {"seq": lax.div(other, self.fsdp), "fsdp": lax.rem(other, self.fsdp)}
            pl.semaphore_signal(sem, inc=1, device_id=device, device_id_type=MESH)
            return carry

        lax.fori_loop(1, self.total, greet, 0)
        pl.semaphore_wait(sem, self.total - 1)


def remote(source, target, send_sem, recv_sem, device):
    return pltpu.make_async_remote_copy(
        src_ref=source,
        dst_ref=target,
        send_sem=send_sem,
        recv_sem=recv_sem,
        device_id=device,
        device_id_type=MESH,
    )


def head_rows(head):
    return pl.ds(pl.multiple_of(head * HEAD_DIM, HEAD_DIM), HEAD_DIM)


def lanes(number, width):
    return pl.ds(pl.multiple_of(number * width, width), width)


def spread_units(own, source, target, send, recv, local, act):
    def to_head(delta, carry):
        head = lax.rem(own.head + delta, HEADS)
        for half in range(own.halves):
            unit = own.halves * own.block + half
            member = lax.rem(unit, own.members)
            place = lax.div(unit, own.members)
            piece = source.at[head_rows(head), pl.ds(half * UNIT, UNIT)]
            there = target.at[:, lanes(place, UNIT)]
            here = (head == own.head) & (member == own.member)

            @pl.when(here)
            def _(piece=piece, there=there, half=half):
                copy = pltpu.make_async_copy(piece, there, local.at[half])
                copy.start() if act == "start" else copy.wait()

            @pl.when(jnp.logical_not(here))
            def _(piece=piece, there=there, half=half, member=member, place=place, head=head):
                copy = remote(
                    piece, there, send.at[head, half], recv.at[place], own.of_head(head, member)
                )
                copy.start() if act == "start" else copy.wait_send()

        return carry

    lax.fori_loop(0, HEADS, to_head, 0)


def await_units(own, target, send, recv):
    def one(place, carry):
        unit = place * own.members + own.member
        there = target.at[:, lanes(place, UNIT)]

        @pl.when(lax.div(unit, own.halves) != own.block)
        def _():
            remote(
                there, there, send.at[0, 0], recv.at[place], own.of_block(0)
            ).wait_recv()

        return carry

    lax.fori_loop(0, own.units, one, 0)


def collect_units(own, source, target, send, recv, local, act, first, count):
    def one(step, carry):
        place = first + step
        unit = place * own.members + own.member
        block, half = lax.div(unit, own.halves), lax.rem(unit, own.halves)
        piece = source.at[:, lanes(place, UNIT)]
        there = target.at[head_rows(own.head), lanes(half, UNIT)]

        @pl.when(block == own.block)
        def _():
            copy = pltpu.make_async_copy(piece, there, local.at[half])
            copy.start() if act == "start" else copy.wait()

        @pl.when(block != own.block)
        def _():
            copy = remote(
                piece, there, send.at[place], recv.at[own.head, half], own.of_block(block)
            )
            copy.start() if act == "start" else copy.wait_send()

        return carry

    lax.fori_loop(0, count, one, 0)


def await_heads(own, target, send, recv):
    def one(head, carry):
        for half in range(own.halves):
            unit = own.halves * own.block + half
            there = target.at[head_rows(head), pl.ds(half * UNIT, UNIT)]

            @pl.when((head != own.head) | (lax.rem(unit, own.members) != own.member))
            def _(there=there, half=half):
                remote(
                    there, there, send.at[0], recv.at[head, half], own.of_block(0)
                ).wait_recv()

        return carry

    lax.fori_loop(0, HEADS, one, 0)


QUERIES = 512
KEYS = 1024
BESIDE_PROJECT = 4
BESIDE_EXCHANGE = 4
BESIDE_TILES = 5
LATER_AT = 8
COLUMNS = 256
ANY = pl.BlockSpec(memory_space=pl.ANY)
WHOLE = pl.BlockSpec(memory_space=pltpu.VMEM)


def plain(left, right):
    return lax.dot_general(left, right, (((1,), (0,)), ((), ())), preferred_element_type=jnp.float32)


def first_dims(left, right):
    return lax.dot_general(left, right, (((0,), (0,)), ((), ())), preferred_element_type=jnp.float32)


def last_dims(left, right):
    return lax.dot_general(left, right, (((1,), (1,)), ((), ())), preferred_element_type=jnp.float32)


class Tiles:
    def __init__(self, own):
        self.span = QUERIES * own.members
        self.groups = own.units * UNIT // QUERIES
        self.longest = own.total * own.tokens // 2

    def fold(self, group, body, state):
        start = group * self.span
        low = lax.div(jnp.maximum(start - self.longest + 1, 0), KEYS)
        edge, high = lax.div(start, KEYS), lax.div(start + self.span + KEYS - 1, KEYS)
        state = lax.fori_loop(low, edge, lambda tile, s: body(tile, False, s), state)
        return lax.fori_loop(edge, high, lambda tile, s: body(tile, True, s), state)


def key_lanes(tile):
    return pl.ds(pl.multiple_of(tile * KEYS, KEYS), KEYS)


def group_lanes(group):
    return pl.ds(pl.multiple_of(group * QUERIES, QUERIES), QUERIES)


def shown(scores, tile, causal, pos, begin):
    number = tile * KEYS + lax.broadcasted_iota(jnp.int32, (KEYS, 1), 0)
    allowed = number >= begin
    if causal:
        allowed = allowed & (number <= pos)
    return jnp.where(allowed, scores, NEGATIVE)


def attend_group(tiles, group, q_ref, k_ref, v_ref, pos_ref, begin_ref, step, number):
    here = group_lanes(group)
    queries, pos, begin = q_ref[:, here], pos_ref[:, here], begin_ref[:, here]

    def body(tile, causal, current):
        number, top, total, summed = current
        number = now_and_then(tile, BESIDE_TILES, step, number)
        scores = shown(first_dims(k_ref[:, key_lanes(tile)], queries), tile, causal, pos, begin)
        new_top = jnp.maximum(top, jnp.max(scores, axis=0, keepdims=True))
        weights = jnp.exp(scores - new_top)
        shrink = jnp.exp(top - new_top)
        total = total * shrink + jnp.sum(weights, axis=0, keepdims=True)
        summed = summed * shrink + plain(v_ref[:, key_lanes(tile)], weights.astype(jnp.bfloat16))
        return number, new_top, total, summed

    number, top, total, summed = tiles.fold(
        group,
        body,
        (
            number,
            jnp.full((1, QUERIES), NEGATIVE, jnp.float32),
            jnp.zeros((1, QUERIES), jnp.float32),
            jnp.zeros((HEAD_DIM, QUERIES), jnp.float32),
        ),
    )
    return summed / total, top + jnp.log(total), number


class ToHeads:
    def __init__(self, own, sources, targets, sems):
        self.own = own
        self.q_ref, *pairs = sources
        self.q_out, *outs = targets
        self.pairs = tuple(zip(pairs, outs))
        self.q_send, self.q_recv, self.q_local, self.send, self.recv, self.local, self.hand_send = sems
        self.shares = own.total // own.members
        self.mine = lax.div(own.f, own.members) * own.seq + own.s

    @staticmethod
    def semaphores(own):
        dma = pltpu.SemaphoreType.DMA
        return [
            dma((HEADS, own.halves)),
            dma((own.units,)),
            dma((own.halves,)),
            dma((2, HEADS)),
            dma((2, own.total)),
            dma((2,)),
            dma((2, own.total // own.members * (own.members - 1))),
        ]

    def keys(self, i, act):
        own = self.own
        source, target = self.pairs[i]

        def to_head(delta, carry):
            head = lax.rem(own.head + delta, HEADS)
            piece = source.at[head_rows(head), :]
            there = target.at[:, lanes(own.block, own.tokens)]

            @pl.when(head == own.head)
            def _(piece=piece, there=there, i=i):
                copy = pltpu.make_async_copy(piece, there, self.local.at[i])
                copy.start() if act == "start" else copy.wait()

            @pl.when(head != own.head)
            def _(piece=piece, there=there, i=i):
                copy = remote(
                    piece,
                    there,
                    self.send.at[i, head],
                    self.recv.at[i, own.block],
                    own.of_head(head, own.member),
                )
                copy.start() if act == "start" else copy.wait_send()

            return carry

        lax.fori_loop(0, HEADS, to_head, 0)

    def hand(self, i, order, block, source, act):
        own = self.own
        for away in range(1, own.members):
            member = lax.rem(own.member + away, own.members)
            copy = remote(
                source,
                self.pairs[i][1].at[:, lanes(block, own.tokens)],
                self.hand_send.at[i, order * (own.members - 1) + away - 1],
                self.recv.at[i, block],
                own.of_head(own.head, member),
            )
            copy.start() if act == "start" else copy.wait_send()

    def hand_own(self, i, act):
        source = self.pairs[i][0].at[head_rows(self.own.head), :]
        self.hand(i, self.shares - 1, self.own.block, source, act)

    def block_of(self, step):
        order = lax.rem(self.mine + step, self.shares)
        f = self.own.member + self.own.members * lax.div(order, self.own.seq)
        return f * self.own.seq + lax.rem(order, self.own.seq)

    def arrive(self, i, block):
        there = self.pairs[i][1].at[:, lanes(block, self.own.tokens)]
        remote(
            there, there, self.send.at[i, 0], self.recv.at[i, block], self.own.of_block(0)
        ).wait_recv()
        return there

    def start_keys(self, i):
        self.keys(i, "start")
        self.hand_own(i, "start")

    def start_queries(self):
        spread_units(self.own, self.q_ref, self.q_out, self.q_send, self.q_recv, self.q_local, "start")

    def relay(self, step):
        block = self.block_of(step)
        for i in range(2):
            self.hand(i, step - 1, block, self.arrive(i, block), "start")

    def finish(self):
        own = self.own

        def rest(block, carry):
            @pl.when(lax.rem(lax.div(block, own.seq), own.members) != own.member)
            def _():
                for i in range(2):
                    self.arrive(i, block)

            return carry

        lax.fori_loop(0, own.total, rest, 0)
        await_units(own, self.q_out, self.q_send, self.q_recv)
        spread_units(own, self.q_ref, self.q_out, self.q_send, self.q_recv, self.q_local, "wait")
        for i in range(2):
            self.keys(i, "wait")
            self.hand_own(i, "wait")

        def settle(step, carry):
            block = self.block_of(step)
            for i, (_, target) in enumerate(self.pairs):
                self.hand(i, step - 1, block, target.at[:, lanes(block, own.tokens)], "wait")
            return carry

        lax.fori_loop(1, self.shares, settle, 0)


def now_and_then(index, every, act, number):
    return lax.cond(lax.rem(index, every) == 0, act, lambda x: x, number)


def rms_scale(tensor):
    return lax.rsqrt(jnp.mean(tensor * tensor, axis=-1, keepdims=True) + EPSILON)


class Front:
    def __init__(self, grid, own, plan, sources, inputs, landed, tokens_of, outs, sems):
        self.grid, self.own = grid, own
        self.x_ref, self.vf_ref, self.cos_ref, self.sin_ref, self.pos_ref = inputs
        self.landed, self.tokens_of = landed, tokens_of
        self.keep, (self.gain_ref, self.normed_ref, self.begin_ref, self.xn_ref) = outs[:3], outs[3:]
        self.keep_sem = sems[-1]
        self.tree = Gather(grid, plan, sources, landed, sems[:-1])

    def keeping(self, i):
        return pltpu.make_async_copy(self.landed[i], self.keep[i], self.keep_sem.at[i])

    def gather(self, between):
        def one(number, carry):
            self.tree.relay(number)
            between(number)
            return carry

        lax.fori_loop(1, self.tree.places, one, 0)
        self.tree.finish()
        for i in range(3):
            self.keeping(i).start()

    def norm(self):
        x = self.x_ref[...].astype(jnp.float32)
        self.xn_ref[...] = x * rms_scale(x)

    def prepare(self):
        gains, places = self.landed[3:]
        near = self.grid.total // 8
        rows = []
        for lane_block in range(8):
            rows.append(
                sum(
                    gains[lane_block * near + i, :8, :].astype(jnp.float32) for i in range(near)
                )
            )
        gain = jnp.concatenate(rows, axis=1)
        self.gain_ref[...] = gain
        self.normed_ref[...] = (self.xn_ref[...] * gain[:1]).astype(self.normed_ref.dtype)
        own = self.own

        def unit(place, carry):
            number = place * own.members + own.member
            block, half = lax.div(number, own.halves), lax.rem(number, own.halves)
            device = lax.rem(block, own.seq) * own.fsdp + lax.div(block, own.seq)
            here = lanes(place, UNIT)
            self.begin_ref[:, here] = self.pos_ref[:, here] - places[device, pl.ds(half, 1), :]
            return carry

        lax.fori_loop(0, own.units, unit, 0)

    def project(self, i, part):
        columns = pl.ds(pl.multiple_of(part * COLUMNS, COLUMNS), COLUMNS)
        weights = self.landed[i][:, :, columns].reshape(-1, COLUMNS)
        found = plain(self.normed_ref[...], weights)
        target = self.tokens_of[i]
        if i == 2:
            mixed = 0.5 * found + 0.5 * self.vf_ref[:, columns].astype(jnp.float32)
            target[columns, :] = mixed.T.astype(target.dtype)
            return
        found = found.T
        cosine, sine_tab = self.cos_ref[...], self.sin_ref[...]
        half, turned = HEAD_DIM // 2, []
        for first in range(0, COLUMNS, HEAD_DIM):
            front, back = found[first : first + half], found[first + half : first + HEAD_DIM]
            turned += [front * cosine - back * sine_tab, back * cosine + front * sine_tab]
        turned = jnp.concatenate(turned, axis=0).astype(target.dtype)
        target[columns, :] = turned * jnp.asarray(HEAD_DIM**-0.5, target.dtype) if i == 0 else turned


def forward_kernel(tokens, plans, counts, *refs):
    refs = list(refs)

    def take(count):
        taken = refs[:count]
        del refs[:count]
        return taken

    n_first, n = counts
    inputs, sources_first, sources = take(5), take(n_first), take(n)
    wholes, first_outs, keep = take(n), take(7), take(3)
    out_ref, lse_ref, back_ref = take(3)
    heads, (low_ref,) = take(3), take(1)
    landed, tokens_of = take(n_first), take(3)
    tree_sems, exchange_sems, (out_send, out_recv, out_local, keep_sem) = take(4), take(7), take(4)
    first_sems = take(5)
    grid, own = Grid(), Owners(tokens)
    grid.locate()
    own.locate()
    front = Front(
        grid, own, plans[0], sources_first, inputs, landed, tokens_of, first_outs, first_sems
    )
    tree = Gather(grid, plans[1], sources, wholes, tree_sems)
    exchange = ToHeads(own, tokens_of, heads, exchange_sems)
    tiles = Tiles(own)
    pos_ref, begin_ref = inputs[4], first_outs[5]

    own.barrier()
    front.tree.start()
    front.norm()
    front.gather(lambda number: pl.when(number == LATER_AT)(tree.start))
    front.prepare()

    def advance(number):
        @pl.when(number < tree.places)
        def _():
            tree.relay(number)

        return number + 1

    number = jnp.int32(1)
    for i in (1, 2, 0):

        def part(index, number, i=i):
            front.project(i, index)
            return now_and_then(index, BESIDE_PROJECT, advance, number)

        number = lax.fori_loop(0, HEADS * HEAD_DIM // COLUMNS, part, number)
        if i:
            exchange.start_keys(i - 1)
        else:
            exchange.start_queries()

    def relay(step, number):
        exchange.relay(step)
        return now_and_then(step, BESIDE_EXCHANGE, advance, number)

    number = lax.fori_loop(1, exchange.shares, relay, number)
    exchange.finish()
    keeping = [pltpu.make_async_copy(heads[i], keep[i], keep_sem.at[i]) for i in range(3)]
    for copy in keeping:
        copy.start()
    units = QUERIES // UNIT

    def one_group(group, number):
        here = group_lanes(group)
        attended, lse, number = attend_group(
            tiles, group, *heads, pos_ref, begin_ref, advance, number
        )
        out_ref[:, here] = attended
        lse_ref[:, here] = lse
        low_ref[:, here] = attended.astype(low_ref.dtype)
        collect_units(
            own, low_ref, back_ref, out_send, out_recv, out_local, "start", group * units, units
        )
        return number

    number = lax.fori_loop(0, tiles.groups, one_group, number)

    def last(number, carry):
        tree.relay(number)
        return carry

    lax.fori_loop(number, tree.places, last, 0)
    await_heads(own, back_ref, out_send, out_recv)
    collect_units(own, low_ref, back_ref, out_send, out_recv, out_local, "wait", 0, own.units)
    tree.finish()
    for copy in keeping:
        copy.wait()
    for i in range(3):
        front.keeping(i).wait()


def forward(inputs, first, first_plan, later, later_plan, ident):
    (tokens, features), kind = inputs[1].shape, inputs[1].dtype
    grid, own = Grid(), Owners(tokens)
    n, n_first = len(later), len(first)
    count = own.units * UNIT
    dma = pltpu.SemaphoreType.DMA
    heads = [(HEAD_DIM, count)] + [(HEAD_DIM, own.total * tokens)] * 2
    pairs = count * own.total * tokens // 3
    moved = sum(a.size * a.dtype.itemsize for a in (*first, *later)) * grid.total
    landed = gathered_shapes(grid, first)
    outs = pl.pallas_call(
        functools.partial(forward_kernel, tokens, (first_plan, later_plan), (n_first, n)),
        out_shape=gathered_shapes(grid, later)
        + landed[:3]
        + [
            jax.ShapeDtypeStruct((8, features), jnp.float32),
            jax.ShapeDtypeStruct((tokens, features), kind),
            jax.ShapeDtypeStruct((1, count), jnp.int32),
            jax.ShapeDtypeStruct((tokens, features), jnp.float32),
        ]
        + [jax.ShapeDtypeStruct(s, kind) for s in heads]
        + [
            jax.ShapeDtypeStruct((HEAD_DIM, count), jnp.float32),
            jax.ShapeDtypeStruct((1, count), jnp.float32),
            jax.ShapeDtypeStruct((features, tokens), kind),
        ],
        in_specs=[WHOLE] * 5 + [ANY] * (n_first + n),
        out_specs=[ANY] * (n + 3) + [WHOLE] * 4 + [ANY] * 3 + [WHOLE] * 2 + [ANY],
        scratch_shapes=[pltpu.VMEM(s, kind) for s in heads]
        + [pltpu.VMEM((HEAD_DIM, count), kind)]
        + [pltpu.VMEM(a.shape, a.dtype) for a in landed]
        + [pltpu.VMEM((features, tokens), kind)] * 3
        + Gather.semaphores(grid, later_plan, n)
        + ToHeads.semaphores(own)
        + [dma((own.units,)), dma((HEADS, own.halves)), dma((own.halves,)), dma((3,))]
        + Gather.semaphores(grid, first_plan, n_first)
        + [dma((3,))],
        compiler_params=pltpu.CompilerParams(
            collective_id=ident, has_side_effects=True, vmem_limit_bytes=VMEM_LIMIT
        ),
        cost_estimate=pl.CostEstimate(
            flops=pairs * 4 * HEAD_DIM, bytes_accessed=moved, transcendentals=pairs
        ),
    )(*inputs, *first, *later)
    return outs[:n], outs[n : n + 3], outs[n + 3 : n + 7], outs[n + 7 : n + 10], outs[n + 10 :]


class GradsBack:
    def __init__(self, own, sums, outs, give_from, given, held, sems):
        self.own, self.sums, self.outs = own, sums, outs
        self.give_from, self.given, self.held = give_from, given, held
        self.give_send, self.give_recv, self.send, self.recv, self.local = sems
        self.others = own.members - 1

    @staticmethod
    def scratch(own, kind):
        shares, others = own.total // own.members, own.members - 1
        dma = pltpu.SemaphoreType.DMA
        blocks = (2, shares * others, HEAD_DIM, own.tokens)
        return [
            pltpu.VMEM(blocks, kind),
            pltpu.VMEM(blocks, kind),
            pltpu.VMEM((2, shares, HEAD_DIM, own.tokens), kind),
            dma((2, shares * others)),
            dma((2, shares * others)),
            dma((2, shares)),
            dma((2, HEADS)),
            dma((2,)),
        ]

    def split(self, block):
        f = lax.div(block, self.own.seq)
        order = lax.div(f, self.own.members) * self.own.seq + lax.rem(block, self.own.seq)
        return lax.rem(f, self.own.members), order

    def give(self, block, act):
        own = self.own
        member, order = self.split(block)
        away = lax.rem(member - own.member + own.members, own.members)

        @pl.when(away > 0)
        def _():
            columns = lanes(block, own.tokens)
            out = order * self.others + away - 1
            back = order * self.others + self.others - away
            for i in range(2):
                if act == "start":
                    self.give_from[i, out] = self.sums[i][:, columns].astype(self.held.dtype)
                copy = remote(
                    self.give_from.at[i, out],
                    self.given.at[i, back],
                    self.give_send.at[i, out],
                    self.give_recv.at[i, back],
                    own.of_head(own.head, member),
                )
                copy.start() if act == "start" else copy.wait_send()

    def back(self, block, order, i, act):
        own = self.own
        there = self.outs[i].at[head_rows(own.head), :]

        @pl.when(block == own.block)
        def _():
            copy = pltpu.make_async_copy(self.held.at[i, order], there, self.local.at[i])
            copy.start() if act == "start" else copy.wait()

        @pl.when(block != own.block)
        def _():
            copy = remote(
                self.held.at[i, order],
                there,
                self.send.at[i, order],
                self.recv.at[i, own.head],
                own.of_block(block),
            )
            copy.start() if act == "start" else copy.wait_send()

    def add(self, block):
        member, order = self.split(block)

        @pl.when(member == self.own.member)
        def _():
            columns = lanes(block, self.own.tokens)
            for i in range(2):
                total = self.sums[i][:, columns]
                for j in range(self.others):
                    slot = order * self.others + j
                    there = self.given.at[i, slot]
                    remote(
                        there,
                        there,
                        self.give_send.at[i, 0],
                        self.give_recv.at[i, slot],
                        self.own.of_block(0),
                    ).wait_recv()
                    total = total + self.given[i, slot].astype(jnp.float32)
                self.held[i, order] = total.astype(self.held.dtype)
                self.back(block, order, i, "start")

    def over(self, first, count, act):
        def one(step, carry):
            act(first + step)
            return carry

        lax.fori_loop(0, count, one, 0)

    def finish(self):
        def arrive(head, carry):
            @pl.when(head != self.own.head)
            def _():
                for i in range(2):
                    there = self.outs[i].at[head_rows(head), :]
                    remote(
                        there, there, self.send.at[i, 0], self.recv.at[i, head], self.own.of_block(0)
                    ).wait_recv()

            return carry

        lax.fori_loop(0, HEADS, arrive, 0)

        def settle(block):
            self.give(block, "wait")
            member, order = self.split(block)

            @pl.when(member == self.own.member)
            def _():
                for i in range(2):
                    self.back(block, order, i, "wait")

        self.over(0, self.own.total, settle)


class Tail:
    def __init__(self, grid, inputs, landed, outs, scratch):
        self.grid = grid
        self.normed_ref, self.xn_ref, self.cos_ref, self.sin_ref, self.ffn_ref = inputs[:5]
        self.weights = inputs[5:]
        self.landed = landed
        self.dh_ref, self.dv_ref = outs
        *self.terms, self.gain_terms, self.weight, self.turned, self.sem = scratch

    @staticmethod
    def scratch(grid, features, tokens, kind):
        rows = features // grid.total
        return (
            [pltpu.VMEM((grid.total, rows, features), kind)] * 3
            + [
                pltpu.VMEM((grid.total, 8, 128), jnp.float32),
                pltpu.VMEM((2, grid.total, rows, features), kind),
                pltpu.VMEM((tokens, features), kind),
                pltpu.SemaphoreType.DMA((2,)),
            ]
        )

    def load(self, step, i):
        return pltpu.make_async_copy(self.weights[i], self.weight.at[step % 2], self.sem.at[step % 2])

    def unrotate(self, i, part):
        columns = pl.ds(pl.multiple_of(part * COLUMNS, COLUMNS), COLUMNS)
        found = self.landed[i][columns, :].astype(jnp.float32)
        if i == 2:
            found = 0.5 * found
        else:
            cosine, sine_tab = self.cos_ref[...], self.sin_ref[...]
            half, turned = HEAD_DIM // 2, []
            for first in range(0, COLUMNS, HEAD_DIM):
                front, back = found[first : first + half], found[first + half : first + HEAD_DIM]
                turned += [front * cosine + back * sine_tab, back * cosine - front * sine_tab]
            found = jnp.concatenate(turned, axis=0)
        turned = found.T.astype(self.turned.dtype)
        self.turned[:, columns] = turned
        if i == 2:
            self.dv_ref[:, columns] = turned

    def project(self, i, step, part, first):
        columns = pl.ds(pl.multiple_of(part * COLUMNS, COLUMNS), COLUMNS)
        per = self.grid.total * COLUMNS // self.normed_ref.shape[1]
        blocks = pl.ds(part * per, per)
        terms = first_dims(self.normed_ref[:, columns], self.turned[...])
        self.terms[i][blocks] = terms.reshape(per, -1, terms.shape[1]).astype(self.terms[i].dtype)
        weights = self.weight[step % 2, blocks].reshape(COLUMNS, -1)
        term = last_dims(self.turned[...], weights)
        self.dh_ref[:, columns] = term if first else self.dh_ref[:, columns] + term

    def gains(self):
        attn = jnp.sum(self.dh_ref[...] * self.xn_ref[...], axis=0, keepdims=True)
        row = lax.broadcasted_iota(jnp.int32, (8, 1), 0)
        both = jnp.where(row == 0, attn, jnp.where(row == 1, self.ffn_ref[...], 0.0))
        near = self.grid.total // 8
        for block in range(8):
            for i in range(near):
                self.gain_terms[block * near + i] = both[:, block * 128 : (block + 1) * 128]


REDUCE_FIRST = 11
REDUCE_TILES = 3
REDUCE_TAIL = 1


def backward_kernel(tokens, plans, counts, *refs):
    refs = list(refs)

    def take(count):
        taken = refs[:count]
        del refs[:count]
        return taken

    n, n_tree, first_counts = counts
    g_ref, q_ref, k_ref, v_ref, out_ref, lse_ref, pos_ref, begin_ref = take(8)
    tail_inputs = take(8) if n else None
    parts = take(n)
    outs = take(2 if n else 3)
    sums = take(n)
    first_sums = take(4 if n else 0)
    grads_ref, dq_ref, dk_sum, dv_sum = take(4)
    back_scratch = take(8)
    g_send, g_recv, g_local, dq_send, dq_recv, dq_local = take(6)
    own = Owners(tokens)
    own.locate()
    tree = None
    dq_out, dk_out, dv_out = landed = take(3) if n else outs
    if n:
        grid = Grid()
        grid.locate()
        tree = Reduce(grid, plans[0], parts, sums, take(n_tree))
        first_scratch = [take(count) for count in first_counts]
        tail = Tail(grid, tail_inputs, landed, outs, refs)
        parts_first = (*tail.terms, tail.gain_terms)
        trees = [
            Reduce(grid, plan, parts_first, first_sums, scratch)
            for plan, scratch in zip(plans[1], first_scratch)
        ]
    grads_back = GradsBack(own, (dk_sum, dv_sum), (dk_out, dv_out), *back_scratch[:3], back_scratch[3:])
    tiles = Tiles(own)

    own.barrier()
    spread_units(own, g_ref, grads_ref, g_send, g_recv, g_local, "start")
    if tree:
        tree.start()
    dk_sum[...] = jnp.zeros_like(dk_sum)
    dv_sum[...] = jnp.zeros_like(dv_sum)

    def advance(number):
        if tree:

            @pl.when(number < tree.places - 1)
            def _():
                tree.climb(number)

        return number + 1

    number = lax.fori_loop(0, REDUCE_FIRST, lambda step, number: advance(number), jnp.int32(0))
    await_units(own, grads_ref, g_send, g_recv)
    spread_units(own, g_ref, grads_ref, g_send, g_recv, g_local, "wait")
    units = QUERIES // UNIT
    blocks = tiles.span // tokens

    def one_group(step, number):
        group = tiles.groups - 1 - step
        here = group_lanes(group)
        queries, grads = q_ref[:, here], grads_ref[:, here]
        pos, begin, lse = pos_ref[:, here], begin_ref[:, here], lse_ref[:, here]
        delta = jnp.sum(grads.astype(jnp.float32) * out_ref[:, here], axis=0, keepdims=True)

        def body(tile, causal, current):
            number, dq = current
            number = now_and_then(tile, REDUCE_TILES, advance, number)
            there = key_lanes(tile)
            keys = k_ref[:, there]
            scores = shown(first_dims(keys, queries), tile, causal, pos, begin)
            probs = jnp.exp(scores - lse)
            dv_sum[:, there] += last_dims(grads, probs.astype(jnp.bfloat16))
            dscores = (probs * (first_dims(v_ref[:, there], grads) - delta)).astype(jnp.bfloat16)
            dk_sum[:, there] += last_dims(queries, dscores)
            return number, dq + plain(keys, dscores)

        number, dq = tiles.fold(
            group, body, (number, jnp.zeros((HEAD_DIM, QUERIES), jnp.float32))
        )
        dq_ref[:, here] = (dq * HEAD_DIM**-0.5).astype(dq_ref.dtype)
        collect_units(
            own, dq_ref, dq_out, dq_send, dq_recv, dq_local, "start", group * units, units
        )
        grads_back.over(group * blocks, blocks, lambda block: grads_back.give(block, "start"))

        @pl.when(step > 0)
        def _():
            grads_back.over((group + 1) * blocks, blocks, grads_back.add)

        return number

    number = lax.fori_loop(0, tiles.groups, one_group, number)
    grads_back.over(0, blocks, grads_back.add)
    await_heads(own, dq_out, dq_send, dq_recv)
    collect_units(own, dq_ref, dq_out, dq_send, dq_recv, dq_local, "wait", 0, own.units)
    grads_back.finish()
    if not tree:
        return

    parts_of = HEADS * HEAD_DIM // COLUMNS
    order = (0, 1, 2)
    tail.load(0, order[0]).start()
    for step, i in enumerate(order):
        tail.load(step, i).wait()
        if step < 2:
            tail.load(step + 1, order[step + 1]).start()

        def turn(part, number, i=i):
            tail.unrotate(i, part)
            return now_and_then(part, REDUCE_TAIL, advance, number)

        def project(part, number, i=i, step=step):
            tail.project(i, step, part, step == 0)
            return now_and_then(part, REDUCE_TAIL, advance, number)

        number = lax.fori_loop(0, parts_of, turn, number)
        number = lax.fori_loop(0, parts_of, project, number)
    tail.gains()
    trees[0].start()

    def climb(step, number):
        trees[0].climb(step)
        return advance(number)

    number = lax.fori_loop(0, trees[0].places - 1, climb, number)

    def last(number, carry):
        tree.climb(number)
        return carry

    lax.fori_loop(number, tree.places - 1, last, 0)
    trees[0].finish()
    tree.finish()


def backward(grads, q, k, v, out, lse, pos, begin, ident, tail=(), arrays=(), plans=((), ())):
    tokens, features, kind = grads.shape[1], grads.shape[0], grads.dtype
    grid, own = Grid(), Owners(tokens)
    n = len(arrays)
    count = own.units * UNIT
    dma = pltpu.SemaphoreType.DMA
    pairs = count * own.total * tokens // 3
    moved = sum(a.size * a.dtype.itemsize for a in arrays) + 6 * k.size
    back = jax.ShapeDtypeStruct(grads.shape, kind)
    scratch = (
        [pltpu.VMEM((HEAD_DIM, count), kind)] * 2
        + [pltpu.VMEM(k.shape, jnp.float32)] * 2
        + GradsBack.scratch(own, kind)
        + [dma((HEADS, own.halves)), dma((own.units,)), dma((own.halves,))]
        + [dma((own.units,)), dma((HEADS, own.halves)), dma((own.halves,))]
    )
    tree_scratch = first_scratch = []
    if n:
        tail_scratch = Tail.scratch(grid, features, tokens, kind)
        first = [jax.ShapeDtypeStruct((grid.total, features // grid.total, features), kind)] * 3
        first.append(jax.ShapeDtypeStruct((grid.total, 8, 128), jnp.float32))
        tree_scratch = Reduce.scratch(grid, plans[0], arrays)
        first_scratch = [Reduce.scratch(grid, plan, first) for plan in plans[1]]
        scratch += [pltpu.VMEM(grads.shape, kind)] * 3 + tree_scratch + sum(first_scratch, [])
        scratch += tail_scratch
        out_shape = [
            jax.ShapeDtypeStruct((tokens, features), jnp.float32),
            jax.ShapeDtypeStruct((tokens, features), kind),
        ]
        out_shape += summed_shapes(arrays) + summed_shapes(first)
        out_specs = [WHOLE] * len(out_shape)
        in_specs = [ANY] + [WHOLE] * 12 + [ANY] * (3 + n)
    else:
        out_shape, out_specs = [back] * 3, [ANY] * 3
        in_specs = [ANY] + [WHOLE] * 7
    outs = pl.pallas_call(
        functools.partial(
            backward_kernel, tokens, plans, (n, len(tree_scratch), [len(one) for one in first_scratch])
        ),
        out_shape=out_shape,
        in_specs=in_specs,
        out_specs=out_specs,
        scratch_shapes=scratch,
        compiler_params=pltpu.CompilerParams(
            collective_id=ident, has_side_effects=True, vmem_limit_bytes=VMEM_LIMIT
        ),
        cost_estimate=pl.CostEstimate(
            flops=pairs * 10 * HEAD_DIM, bytes_accessed=moved, transcendentals=pairs
        ),
    )(grads, q, k, v, out, lse, pos, begin, *tail, *arrays)
    return (outs[:2], outs[2 : 2 + n], outs[2 + n :]) if n else outs


def publish_kernel(x_ref, gain_ref, dh_ref, dy_ref, dv_ref, *refs):
    grad_ref, first_ref = refs[len(refs) // 2 - 1 : len(refs) // 2 + 1]
    sources, targets = refs[: len(refs) // 2 - 1], refs[len(refs) // 2 + 1 :]
    for source, target in zip(sources, targets):
        target[...] = source[...]
    x = x_ref[...].astype(jnp.float32)
    norm = rms_scale(x)
    scaled = dh_ref[...] * gain_ref[:1]
    normed = x * norm
    grad_ref[...] = dy_ref[...] + norm * (
        scaled - normed * jnp.mean(scaled * normed, axis=-1, keepdims=True)
    )
    first_ref[...] = dv_ref[...].astype(jnp.float32)


def publish(x, gains, grad_normed, grad_after, grad_v, arrays):
    wide = jax.ShapeDtypeStruct(x.shape, jnp.float32)
    return pl.pallas_call(
        publish_kernel,
        out_shape=[wide, wide] + [jax.ShapeDtypeStruct(a.shape, a.dtype) for a in arrays],
        in_specs=[WHOLE] * (5 + len(arrays)),
        out_specs=[WHOLE] * (2 + len(arrays)),
        compiler_params=pltpu.CompilerParams(vmem_limit_bytes=VMEM_LIMIT),
    )(x, gains, grad_normed, grad_after, grad_v, *arrays)


def plan(columns, *pieces):
    found, used = [], [0] * len(columns)
    for array, part, order in pieces:
        left = columns[array] - used[array]
        if not left:
            continue
        count = left if part is None else min(part, left)
        found.append((array, used[array], count, order))
        used[array] += count
    return found


def angle_tables(offsets):
    half_dim = HEAD_DIM // 2
    frequency = jnp.power(10000.0, -jnp.arange(half_dim, dtype=jnp.float32) / half_dim)
    angles = frequency[:, None] * offsets.astype(jnp.float32)[None, :]
    return jnp.cos(angles)[None], jnp.sin(angles)[None]


def rotate(tensor, cosine, sine_tab):
    pairs = tensor.reshape(HEADS, 2, HEAD_DIM // 2, -1)
    front, back = pairs[:, 0], pairs[:, 1]
    turned = jnp.stack([front * cosine - back * sine_tab, back * cosine + front * sine_tab], axis=1)
    return turned.reshape(tensor.shape)


def matmul(left, right):
    return jnp.dot(left, right, preferred_element_type=jnp.float32)


def contract(left, right, left_dim, right_dim):
    return lax.dot_general(
        left, right, (((left_dim,), (right_dim,)), ((), ())), preferred_element_type=jnp.float32
    )


def per_device(
    layer_input,
    v_first,
    offsets,
    g_attn,
    w_query,
    w_key,
    w_value,
    w_out,
    g_ffn,
    w_gate,
    w_up,
    w_down,
    out_cot,
):
    low = jnp.bfloat16
    tokens = layer_input.shape[0]
    seq, fsdp = lax.axis_size("seq"), lax.axis_size("fsdp")
    devices = seq * fsdp
    seq_index = lax.axis_index("seq")
    own_offsets = lax.dynamic_slice_in_dim(offsets, seq_index * tokens, tokens, 0)

    share = g_attn.shape[0]
    neighbours = 128 // share
    turn = lax.rem(seq_index * fsdp + lax.axis_index("fsdp"), neighbours) * share
    gains = jnp.zeros((16, 128), low)
    gains = lax.dynamic_update_slice(gains, jnp.stack([g_attn, g_ffn]), (0, turn))
    places = jnp.zeros((8, 128), jnp.int32)
    places = lax.dynamic_update_slice(places, own_offsets.reshape(-1, 128), (0, 0))
    first = (w_query, w_key, w_value, gains, places)
    half = w_key.shape[1] // 2 if devices <= 32 else None
    first_plan = plan(
        [shard.shape[1] for shard in first],
        (0, None, "A"), (1, half, "A"), (1, half, "B"), (2, None, "C"), (3, None, "C"), (4, None, "C"),
    )
    later = (w_gate, w_up, w_down, w_out)
    later_plan = plan(
        [shard.shape[1] for shard in later],
        (0, None, "A"), (1, None, "A"), (2, None, "C"), (3, half, "A"), (3, half, "B"),
    )

    own = Owners(tokens)
    member = lax.rem(lax.axis_index("fsdp"), own.members)
    pos = (
        (jnp.arange(own.units, dtype=jnp.int32)[:, None] * own.members + member) * UNIT
        + jnp.arange(UNIT, dtype=jnp.int32)[None]
    ).reshape(1, -1)
    cosine, sine_tab = angle_tables(own_offsets)
    input_f32 = layer_input.astype(jnp.float32)
    wholes, first_wholes, front, heads, (attended, lse, attn_tokens) = forward(
        (layer_input, v_first, cosine[0], sine_tab[0], pos),
        first, first_plan, later,
        plan(
            [shard.shape[1] for shard in later],
            (0, None, "A"), (1, None, "A"), (2, None, "C"), (3, None, "A"),
        ),
        0,
    )
    gain_rows, normed_a, begin, normed_input = front
    gain_ffn = gain_rows[1]
    proj_query, proj_key, proj_value = (whole.reshape(-1, whole.shape[2]) for whole in first_wholes)
    proj_gate, proj_up, proj_down, proj_out = (whole.reshape(-1, whole.shape[2]) for whole in wholes)

    after_attn = input_f32 + contract(attn_tokens, proj_out, 0, 0)
    norm_ffn = rms_scale(after_attn)
    normed_f = (after_attn * norm_ffn * gain_ffn).astype(low)
    gate_act = matmul(normed_f, proj_gate)
    up_act = matmul(normed_f, proj_up)
    sigmoid_gate = jax.nn.sigmoid(gate_act)
    silu_gate = gate_act * sigmoid_gate
    hidden = (silu_gate * up_act).astype(low)
    result = (after_attn + matmul(hidden, proj_down)).astype(low)

    grad_hidden = contract(out_cot, proj_down, 1, 1)
    grad_gate_low = (
        grad_hidden * up_act * sigmoid_gate * (1.0 + gate_act * (1.0 - sigmoid_gate))
    ).astype(low)
    grad_up_low = (grad_hidden * silu_gate).astype(low)
    grad_normed_f = contract(grad_gate_low, proj_gate, 1, 1) + contract(grad_up_low, proj_up, 1, 1)
    grad_gain_ffn = jnp.sum(grad_normed_f * after_attn * norm_ffn, axis=0)
    scaled_ffn = grad_normed_f * gain_ffn
    grad_after = (
        out_cot.astype(jnp.float32)
        + norm_ffn * scaled_ffn
        - after_attn * norm_ffn**3 * jnp.mean(scaled_ffn * after_attn, axis=-1, keepdims=True)
    )
    grad_attn_low = grad_after.astype(low)
    grad_attended = contract(proj_out, grad_attn_low, 1, 1).astype(low)

    def terms(*grads):
        return [grad.astype(low).reshape(devices, -1, grad.shape[1]) for grad in grads]

    later_terms = terms(
        contract(normed_f, grad_gate_low, 0, 0), contract(normed_f, grad_up_low, 0, 0),
        contract(hidden, out_cot, 0, 0), contract(attn_tokens, grad_attn_low, 1, 0),
    )
    attention = (grad_attended, *heads, attended, lse, pos, begin)
    if devices <= 32:
        (grad_normed_a, grad_v), later_sums, first_sums = backward(
            *attention, 1,
            (
                normed_a, normed_input, cosine[0], sine_tab[0], grad_gain_ffn[None],
                *first_wholes,
            ),
            later_terms, (later_plan, [first_plan[:-1]]),
        )
    else:
        dq_rot, dk_rot, grad_mixed = backward(*attention, 1)
        grad_q = rotate(dq_rot.astype(jnp.float32), cosine, -sine_tab).astype(low)
        grad_k = rotate(dk_rot.astype(jnp.float32), cosine, -sine_tab).astype(low)
        grad_v = grad_mixed * jnp.asarray(0.5, low)
        grad_query_w = contract(normed_a, grad_q, 0, 1)
        grad_key_w = contract(normed_a, grad_k, 0, 1)
        grad_value_w = contract(normed_a, grad_v, 0, 1)
        grad_normed_a = (
            contract(grad_q, proj_query, 0, 1)
            + contract(grad_k, proj_key, 0, 1)
            + contract(grad_v, proj_value, 0, 1)
        )
        grad_gain_attn = jnp.sum(grad_normed_a * normed_input, axis=0)
        grad_v = grad_v.T
        gain_terms = jnp.pad(jnp.stack([grad_gain_attn, grad_gain_ffn]), ((0, 6), (0, 0)))
        gain_terms = jnp.repeat(gain_terms.reshape(8, -1, 128).transpose(1, 0, 2), neighbours, axis=0)
        first_terms = [*terms(grad_query_w, grad_key_w, grad_value_w), gain_terms]
        every = plan(
            [term.shape[2] for term in first_terms + later_terms],
            (0, None, "A"), (1, None, "B"), (2, None, "C"), (3, None, "C"),
            (4, None, "A"), (5, None, "A"), (6, None, "C"), (7, None, "C"),
        )
        all_sums = reduce_all(first_terms + later_terms, every, 2)
        first_sums, later_sums = all_sums[:4], all_sums[4:]
    grad_layer, grad_first, *sums, sum_gains = publish(
        layer_input, gain_rows, grad_normed_a, grad_after, grad_v,
        [*first_sums[:3], *later_sums, first_sums[3]],
    )
    sum_query, sum_key, sum_value, sum_gate, sum_up, sum_down, sum_out = sums
    sum_gains = lax.dynamic_slice_in_dim(sum_gains, turn, share, 1)
    return (
        result,
        grad_layer,
        grad_first,
        sum_gains[0],
        sum_query,
        sum_key,
        sum_value,
        sum_out,
        sum_gains[1],
        sum_gate,
        sum_up,
        sum_down,
    )


def solution(mesh):
    return jax.shard_map(
        per_device,
        mesh=mesh,
        in_specs=(
            P(("fsdp", "seq"), None),
            P(("fsdp", "seq"), None),
            P("fsdp"),
            P(("seq", "fsdp")),
            P(("seq", "fsdp"), None),
            P(("seq", "fsdp"), None),
            P(("seq", "fsdp"), None),
            P(("seq", "fsdp"), None),
            P(("seq", "fsdp")),
            P(("seq", "fsdp"), None),
            P(("seq", "fsdp"), None),
            P(("seq", "fsdp"), None),
            P(("fsdp", "seq"), None),
        ),
        out_specs=(
            P(("fsdp", "seq"), None),
            P(("fsdp", "seq"), None),
            P(("fsdp", "seq"), None),
            P(("seq", "fsdp")),
            P(("seq", "fsdp"), None),
            P(("seq", "fsdp"), None),
            P(("seq", "fsdp"), None),
            P(("seq", "fsdp"), None),
            P(("seq", "fsdp")),
            P(("seq", "fsdp"), None),
            P(("seq", "fsdp"), None),
            P(("seq", "fsdp"), None),
        ),
        check_vma=False,
    )
```
